32 devices in a mesh: fsdp: 2 (over x), seq: 16 (over z, y, core).
Axes of the slice: x: 2, y: 2, z: 4, core: 2. Of those that a mesh axis runs over, the one named last changes fastest.
Arguments:
- hidden_in: bfloat16 [8192, 640], P(('fsdp', 'seq')), may hold values from -6 to 6
- cotangent: bfloat16 [8192, 640], P(('fsdp', 'seq')), may hold values from -6 to 6
- dataset_ids: int32 [8192], P(('fsdp', 'seq')), may hold values from 0 to 15
- mixing: float32 [16], replicated, may hold values from 0.25 to 4
- pad_lengths: int32 [2], P('fsdp'), may hold values from 0 to 2047
- attention_gain: bfloat16 [640], P(('fsdp', 'seq')), may hold values from 0.5 to 1.5
- merged_projection: bfloat16 [640, 1536], P(('fsdp', 'seq')), may hold values from -0.25 to 0.25
- merged_adapter_in: bfloat16 [640, 768], P(('fsdp', 'seq')), may hold values from -0.25 to 0.25
- query_adapter_out: bfloat16 [256, 1024], P(('fsdp', 'seq')), may hold values from -0.375 to 0.375
- keyval_adapter_out: bfloat16 [512, 256], P(('fsdp', 'seq')), may hold values from -0.375 to 0.375
- output_projection: bfloat16 [1024, 640], P(('fsdp', 'seq')), may hold values from -4 to 4
- output_adapter_in: bfloat16 [1024, 256], P(('fsdp', 'seq')), may hold values from -4 to 4
- output_adapter_out: bfloat16 [256, 640], P(('fsdp', 'seq')), may hold values from -0.375 to 0.375
- feedforward_gain: bfloat16 [640], P(('fsdp', 'seq')), may hold values from 0.5 to 1.5
- gate_up_weight: bfloat16 [640, 4096], P(('fsdp', 'seq')), may hold values from -0.25 to 0.25
- gate_up_adapter_in: bfloat16 [640, 512], P(('fsdp', 'seq')), may hold values from -0.25 to 0.25
- gate_up_adapter_out: bfloat16 [512, 2048], P(('fsdp', 'seq')), may hold values from -0.375 to 0.375
- down_weight: bfloat16 [2048, 640], P(('fsdp', 'seq')), may hold values from -0.125 to 0.125
- down_adapter_in: bfloat16 [2048, 256], P(('fsdp', 'seq')), may hold values from -0.125 to 0.125
- down_adapter_out: bfloat16 [256, 640], P(('fsdp', 'seq')), may hold values from -0.375 to 0.375
Outputs:
- output: bfloat16 [8192, 640], P(('fsdp', 'seq'))
- hidden_grad: bfloat16 [8192, 640], P(('fsdp', 'seq'))
- attention_gain_grad: float32 [640], P(('fsdp', 'seq'))
- merged_projection_grad: float32 [640, 1536], P(('fsdp', 'seq'))
- merged_adapter_in_grad: float32 [640, 768], P(('fsdp', 'seq'))
- query_adapter_out_grad: float32 [256, 1024], P(('fsdp', 'seq'))
- keyval_adapter_out_grad: float32 [512, 256], P(('fsdp', 'seq'))
- output_projection_grad: float32 [1024, 640], P(('fsdp', 'seq'))
- output_adapter_in_grad: float32 [1024, 256], P(('fsdp', 'seq'))
- output_adapter_out_grad: float32 [256, 640], P(('fsdp', 'seq'))
- feedforward_gain_grad: float32 [640], P(('fsdp', 'seq'))
- gate_up_weight_grad: float32 [640, 4096], P(('fsdp', 'seq'))
- gate_up_adapter_in_grad: float32 [640, 512], P(('fsdp', 'seq'))
- gate_up_adapter_out_grad: float32 [512, 2048], P(('fsdp', 'seq'))
- down_weight_grad: float32 [2048, 640], P(('fsdp', 'seq'))
- down_adapter_in_grad: float32 [2048, 256], P(('fsdp', 'seq'))
- down_adapter_out_grad: float32 [256, 640], P(('fsdp', 'seq'))
The draws below stay inside these ranges and needn't reach their ends.
All inputs are finite; a program needn't handle non-finite values.
Results may differ from the reference program's by a relative error of at most 0.019.
The reference program's roundings to bfloat16 on the way count: a program that leaves them out, or rounds other values in their place, can miss the bound.
Values may be sent and summed in bfloat16 or wider, within the bound.
A program may use at most 192 MiB of HBM per device.

```python
import math
import jax
import jax.numpy as jnp
import numpy as np
from jax import lax

D = 640
HEADS = 4
HEAD_DIM = 256
FF = 2048
RANK = 256
DATASETS = 16
TOK_DEV = 256
SEQ_LEN = 4096
SEQUENCES = 2
TOKENS = 8192
N_SEQ = 16


def place_ends(drawn, own_key, smallest, top_value):
    longest = drawn.shape.index(max(drawn.shape))
    spots = []
    for shift in (0, 1):
        where = [jax.random.randint(jax.random.fold_in(own_key, axis), (), 0, length) for axis, length in enumerate(drawn.shape)]
        where[longest] = (where[longest] + shift) % drawn.shape[longest]
        spots.append(tuple(where))
    return drawn.at[spots[0]].set(smallest).at[spots[1]].set(top_value)


def block_scale(own_key, dims, pieces, low, high):
    level = 1.0
    for dim, parts in pieces:
        draws = jax.random.uniform(jax.random.fold_in(jax.random.fold_in(own_key, 6), dim), (parts,), jnp.float32, low / len(pieces), high / len(pieces))
        level = level * jnp.repeat(jnp.exp(draws), dims[dim] // parts).reshape((-1,) + (1,) * (len(dims) - 1 - dim))
    return level


def rank_bounds(number_of, skew):
    weights = [(1 << 20) // math.isqrt(grade ** skew) + 1 for grade in range(1, number_of + 1)]
    width = 1 + sum(weights) // (1 << 30)
    return np.cumsum(np.array([max(1, weight // width) for weight in weights]))


def ranked_ids(key, dims, amount, slope):
    table = rank_bounds(amount, slope)
    pick = jax.random.randint(jax.random.fold_in(key, 1), dims, 0, int(table[amount - 1]))
    rank = jnp.searchsorted(jnp.asarray(table, jnp.int32), pick, side="right")
    return jax.random.permutation(jax.random.fold_in(key, 2), amount)[rank].astype(jnp.int32)


def scatter_about(key, extent, deviation, limit, pieces=(), held_as=jnp.bfloat16):
    drawn = jax.random.normal(key, extent, jnp.float32) * deviation
    if len(pieces) > 0:
        drawn = block_scale(key, extent, pieces, -0.22, 0.18) * drawn
    return jnp.clip(drawn, min=-limit, max=limit).astype(held_as)


def setup_inputs(seed: int = 0) -> dict:
    seeds = jax.random.split(jax.random.key(seed), 21)
    hidden_in = scatter_about(seeds[0], (TOKENS, D), 1.0, 6.0, ((0, 32),))
    cotangent = scatter_about(seeds[1], (TOKENS, D), 1.0, 6.0, ((0, 32),))
    dataset_ids = place_ends(ranked_ids(seeds[2], (TOKENS,), DATASETS, 2), jax.random.fold_in(seeds[2], 3), 0, DATASETS - 1).astype(jnp.int32)
    mixing = jnp.clip(jnp.exp(jax.random.uniform(seeds[3], (DATASETS,), jnp.float32, math.log(0.25), math.log(4.0))), 0.25, 4.0)
    pad_lengths = jax.random.randint(seeds[4], (SEQUENCES,), 0, TOK_DEV * N_SEQ // 2).astype(jnp.int32)
    attention_gain = jnp.clip(1.0 + 0.1 * jax.random.normal(seeds[5], (D,), jnp.float32), 0.5, 1.5).astype(jnp.bfloat16)
    merged_projection = scatter_about(seeds[6], (D, HEADS * HEAD_DIM + 2 * HEAD_DIM), D ** -0.5, 0.25, ((0, 32),))
    merged_adapter_in = scatter_about(seeds[7], (D, 3 * RANK), D ** -0.5, 0.25, ((0, 32),))
    query_adapter_out = scatter_about(seeds[8], (RANK, HEADS * HEAD_DIM), RANK ** -0.5, 0.375, ((0, 32),))
    keyval_adapter_out = scatter_about(seeds[9], (2 * RANK, HEAD_DIM), RANK ** -0.5, 0.375, ((0, 32),))
    output_projection = scatter_about(seeds[10], (HEADS * HEAD_DIM, D), (max(1, 8 * HEADS * HEAD_DIM // (TOK_DEV * N_SEQ))) ** -0.5, 4.0, ((0, 32),))
    output_adapter_in = scatter_about(seeds[11], (HEADS * HEAD_DIM, RANK), (max(1, 8 * HEADS * HEAD_DIM // (TOK_DEV * N_SEQ))) ** -0.5, 4.0, ((0, 32),))
    output_adapter_out = scatter_about(seeds[12], (RANK, D), RANK ** -0.5, 0.375, ((0, 32),))
    feedforward_gain = jnp.clip(1.0 + 0.1 * jax.random.normal(seeds[13], (D,), jnp.float32), 0.5, 1.5).astype(jnp.bfloat16)
    gate_up_weight = scatter_about(seeds[14], (D, 2 * FF), D ** -0.5, 0.25, ((0, 32),))
    gate_up_adapter_in = scatter_about(seeds[15], (D, 2 * RANK), D ** -0.5, 0.25, ((0, 32),))
    gate_up_adapter_out = scatter_about(seeds[16], (2 * RANK, FF), RANK ** -0.5, 0.375, ((0, 32),))
    down_weight = scatter_about(seeds[17], (FF, D), FF ** -0.5, 0.125, ((0, 32),))
    down_adapter_in = scatter_about(seeds[18], (FF, RANK), FF ** -0.5, 0.125, ((0, 32),))
    down_adapter_out = scatter_about(seeds[19], (RANK, D), RANK ** -0.5, 0.375, ((0, 32),))
    return dict(hidden_in=hidden_in, cotangent=cotangent, dataset_ids=dataset_ids, mixing=mixing, pad_lengths=pad_lengths, attention_gain=attention_gain, merged_projection=merged_projection, merged_adapter_in=merged_adapter_in, query_adapter_out=query_adapter_out, keyval_adapter_out=keyval_adapter_out, output_projection=output_projection, output_adapter_in=output_adapter_in, output_adapter_out=output_adapter_out, feedforward_gain=feedforward_gain, gate_up_weight=gate_up_weight, gate_up_adapter_in=gate_up_adapter_in, gate_up_adapter_out=gate_up_adapter_out, down_weight=down_weight, down_adapter_in=down_adapter_in, down_adapter_out=down_adapter_out)


EPSILON = 1e-06
HIGHEST = lax.Precision.HIGHEST

@jax.custom_vjp
def low(v):
    return lax.optimization_barrier(v.astype(jnp.bfloat16)).astype(jnp.float32)

@jax.custom_vjp
def low_back(v):
    return v

def low_keep(v):
    return (low(v), None)

def low_pass(kept, grad):
    return (grad,)

def back_keep(v):
    return (v, None)

def back_low(kept, grad):
    return (low(grad),)
low.defvjp(low_keep, low_pass)
low_back.defvjp(back_keep, back_low)

def matmul(left_side, right_side):
    return jnp.dot(left_side, right_side, precision=HIGHEST, preferred_element_type=jnp.float32)

def rms_scale(values, gain_vector):
    inverse = lax.rsqrt(lax.optimization_barrier(jnp.mean(values * values, axis=-1, keepdims=True)) + EPSILON)
    return values * inverse * gain_vector

def rotary_tables(positions):
    half_width = HEAD_DIM // 2
    inverse = 10000.0 ** (-2.0 * jnp.arange(half_width, dtype=jnp.float32) / HEAD_DIM)
    angles = positions.astype(jnp.float32)[:, None] * inverse[None, :]
    return (jnp.cos(angles), jnp.sin(angles))

def rotate(values, cosine_table, sine_table):
    half_width = values.shape[-1] // 2
    first = values[..., :half_width]
    second = values[..., half_width:]
    return jnp.concatenate([first * cosine_table - second * sine_table, second * cosine_table + first * sine_table], axis=-1)

def attend(query_block, block_start, key_rows, value_rows, valid_count):
    row_count = query_block.shape[0]
    scores = jnp.einsum('thd,kd->thk', query_block, key_rows, precision=HIGHEST) * HEAD_DIM ** (-0.5)
    scores = low_back(scores)
    query_pos = block_start + jnp.arange(row_count)
    key_pos = jnp.arange(key_rows.shape[0])
    allowed = (key_pos[None, :] <= query_pos[:, None]) & (key_pos[None, :] < valid_count)
    scores = jnp.where(allowed[:, None, :], scores, -jnp.inf)
    soft_weights = low(jax.nn.softmax(scores, axis=-1))
    return jnp.einsum('thk,kd->thd', soft_weights, value_rows, precision=HIGHEST)

def feed_block(row_block, weights):
    feedforward_gain, gate_up_weight, gate_up_adapter_in, gate_up_adapter_out, down_weight, down_adapter_in, down_adapter_out = weights
    normed_two = low(rms_scale(row_block, feedforward_gain))
    pre_gate = matmul(normed_two, gate_up_weight)
    lifted_two = low(low_back(matmul(normed_two, gate_up_adapter_in)))
    gate_part = pre_gate[:, :FF] + matmul(lifted_two[:, :RANK], gate_up_adapter_out[:RANK])
    upper_part = pre_gate[:, FF:] + matmul(lifted_two[:, RANK:], gate_up_adapter_out[RANK:])
    gate_part = low_back(gate_part)
    upper_part = low_back(upper_part)
    inner = low(jax.nn.gelu(gate_part, approximate=True) * upper_part)
    lifted_down = low(low_back(matmul(inner, down_adapter_in)))
    branch = low_back(matmul(inner, down_weight) + matmul(lifted_down, down_adapter_out))
    return row_block + branch

def sequence_forward(params, hidden, valid_count):
    attention_gain, merged_projection, merged_adapter_in, query_adapter_out, keyval_adapter_out, output_projection, output_adapter_in, output_adapter_out = params[:8]
    length = hidden.shape[0]
    query_width = HEADS * HEAD_DIM
    normed = low(rms_scale(hidden, attention_gain))
    projected = matmul(normed, merged_projection)
    lifted = low(low_back(matmul(normed, merged_adapter_in)))
    query_rows = projected[:, :query_width] + matmul(lifted[:, :RANK], query_adapter_out)
    key_rows = projected[:, query_width:query_width + HEAD_DIM] + matmul(lifted[:, RANK:2 * RANK], keyval_adapter_out[:RANK])
    value_rows = projected[:, query_width + HEAD_DIM:] + matmul(lifted[:, 2 * RANK:], keyval_adapter_out[RANK:])
    cosine_table, sine_table = rotary_tables(jnp.arange(length))
    query_rows = low(rotate(low_back(query_rows).reshape(length, HEADS, HEAD_DIM), cosine_table[:, None, :], sine_table[:, None, :]))
    key_rows = low(rotate(low_back(key_rows), cosine_table, sine_table))
    value_rows = low(low_back(value_rows))
    block_size = min(512, length)
    starts = jnp.arange(length // block_size) * block_size
    checked = jax.checkpoint(attend)
    attended = lax.map(lambda pair_item: checked(pair_item[0], pair_item[1], key_rows, value_rows, valid_count), (query_rows.reshape(length // block_size, block_size, HEADS, HEAD_DIM), starts))
    attended = low(low_back(attended.reshape(length, query_width)))
    lifted_out = low(low_back(matmul(attended, output_adapter_in)))
    middle = hidden + low_back(matmul(attended, output_projection) + matmul(lifted_out, output_adapter_out))
    feed_rows = min(1024, length)
    feed_checked = jax.checkpoint(feed_block)
    ffn_weights = params[8:]
    result = lax.map(lambda row_block: feed_checked(row_block, ffn_weights), middle.reshape(length // feed_rows, feed_rows, D))
    return result.reshape(length, D)

def reference(hidden_in, cotangent, dataset_ids, mixing, pad_lengths, attention_gain, merged_projection, merged_adapter_in, query_adapter_out, keyval_adapter_out, output_projection, output_adapter_in, output_adapter_out, feedforward_gain, gate_up_weight, gate_up_adapter_in, gate_up_adapter_out, down_weight, down_adapter_in, down_adapter_out):
    params = tuple((member.astype(jnp.float32) for member in (attention_gain, merged_projection, merged_adapter_in, query_adapter_out, keyval_adapter_out, output_projection, output_adapter_in, output_adapter_out, feedforward_gain, gate_up_weight, gate_up_adapter_in, gate_up_adapter_out, down_weight, down_adapter_in, down_adapter_out)))
    valid_counts = SEQ_LEN - pad_lengths

    def forward(hidden, weights):
        chains = hidden.reshape(SEQUENCES, SEQ_LEN, D)
        outputs = lax.map(lambda pair_item: sequence_forward(weights, pair_item[0], pair_item[1]), (chains, valid_counts))
        return outputs.reshape(TOKENS, D)
    output, pullback = jax.vjp(forward, hidden_in.astype(jnp.float32), params)
    positions = jnp.arange(TOKENS) % SEQ_LEN
    owners = jnp.arange(TOKENS) // SEQ_LEN
    row_weight = jnp.where(positions < valid_counts[owners], mixing[dataset_ids], 0.0)
    hidden_grad, grads = pullback(cotangent.astype(jnp.float32) * row_weight[:, None])
    return (output.astype(jnp.bfloat16), hidden_grad.astype(jnp.bfloat16), grads[0], grads[1], grads[2], grads[3], grads[4], grads[5], grads[6], grads[7], grads[8], grads[9], grads[10], grads[11], grads[12], grads[13], grads[14])
```

```python
from functools import partial

import jax
import jax.numpy as jnp
from jax import lax
from jax.experimental import pallas as pl
from jax.experimental.pallas import tpu as pltpu
from jax.sharding import PartitionSpec as P

HEADS = 4
HEAD_DIM = 256
FF = 2048
RANK = 256
DATASETS = 16
EPSILON = 1e-06
MESH = pl.DeviceIdType.MESH
VMEM_LIMIT = 60 * 1024 * 1024
AXES = ("fsdp", "seq")
BF16 = jnp.bfloat16
F32 = jnp.float32


def rms_scale(values, gain_vector):
    inverse = lax.rsqrt(jnp.mean(values * values, axis=-1, keepdims=True) + EPSILON)
    return values * inverse * gain_vector


def rotary_tables(positions):
    half_width = HEAD_DIM // 2
    inverse = 10000.0 ** (-2.0 * jnp.arange(half_width, dtype=F32) / HEAD_DIM)
    angles = positions.astype(F32)[:, None] * inverse[None, :]
    return (jnp.cos(angles), jnp.sin(angles))


def rotate(values, cosine_table, sine_table):
    half_width = values.shape[-1] // 2
    first = values[..., :half_width]
    second = values[..., half_width:]
    return jnp.concatenate(
        [first * cosine_table - second * sine_table, second * cosine_table + first * sine_table],
        axis=-1,
    )


def rotate_heads(values, cosine_table, sine_table):
    parts = [
        rotate(values[:, h * HEAD_DIM : (h + 1) * HEAD_DIM], cosine_table, sine_table)
        for h in range(HEADS)
    ]
    return jnp.concatenate(parts, axis=1)


def matmul(left_side, right_side):
    return jnp.dot(left_side, right_side, preferred_element_type=F32)


def times_transposed(left_side, right_side):
    return lax.dot_general(
        left_side, right_side, (((1,), (1,)), ((), ())), preferred_element_type=F32
    )


def transposed_times(left_side, right_side, out=F32):
    return lax.dot_general(
        left_side, right_side, (((0,), (0,)), ((), ())), preferred_element_type=F32
    ).astype(out)


def padded_rows(rows):
    return -(-rows // 8) * 8


def pad_shard(shard):
    rows = shard.shape[0]
    return jnp.pad(shard, ((0, padded_rows(rows) - rows), (0, 0)))


def selection(rows, count):
    wide = padded_rows(rows)
    source = lax.broadcasted_iota(jnp.int32, (count * rows, count * wide), 0)
    target = lax.broadcasted_iota(jnp.int32, (count * rows, count * wide), 1)
    inside = target % wide
    return ((source == target // wide * rows + inside) & (inside < rows)).astype(BF16)


def spread(values, rows):
    if padded_rows(rows) == rows:
        return values
    return matmul(values, selection(rows, values.shape[1] // rows)).astype(BF16)


def collect(values, rows):
    wide = padded_rows(rows)
    if wide == rows:
        return values
    chosen = selection(rows, values.shape[1] // wide)
    first = values.astype(BF16)
    rest = values - first.astype(F32)
    second = rest.astype(BF16)
    third = (rest - second.astype(F32)).astype(BF16)
    return (
        times_transposed(first, chosen)
        + times_transposed(second, chosen)
        + times_transposed(third, chosen)
    )


def place(groups):
    f = lax.axis_index("fsdp")
    s = lax.axis_index("seq")
    c = lax.rem(s, 2)
    y = lax.rem(s // 2, 2)
    z = s // 4
    return f, z, y, c


def device(f, z, y, c):
    return (f, (z * 2 + y) * 2 + c)


def greet(groups, both):
    f, z, y, c = place(groups)
    barrier = pltpu.get_barrier_semaphore()
    peers = [device(f, z, y, 1 - c), device(f, z, 1 - y, c)]
    if both:
        peers.append(device(1 - f, z, y, c))
    for d in range(1, groups):
        peers.append(device(f, lax.rem(z + d, groups), y, c))
    for peer in peers:
        pl.semaphore_signal(barrier, inc=1, device_id=peer, device_id_type=MESH)
    pl.semaphore_wait(barrier, len(peers))


def gather_kernel(groups, orders, *refs):
    count = len(orders)
    ins, outs = refs[:count], refs[count : 2 * count]
    send, recv, local = refs[2 * count :]
    f, z, y, c = place(groups)
    greet(groups, True)

    def remote(src, dst, a, slot, peer):
        return pltpu.make_async_remote_copy(
            src_ref=src,
            dst_ref=dst,
            send_sem=send.at[a, slot],
            recv_sem=recv.at[a, slot],
            device_id=peer,
            device_id_type=MESH,
        )

    core = device(f, z, y, 1 - c)
    across = {"y": device(f, z, 1 - y, c), "x": device(1 - f, z, y, c)}
    started = []

    def start(copy):
        copy.start()
        started.append(copy)

    for a in range(count):
        pltpu.make_async_copy(ins[a], outs[a].at[f, z, y, c], local.at[a]).start()
        for d in range(1, groups):
            start(
                remote(
                    ins[a],
                    outs[a].at[f, z, y, c],
                    a,
                    d,
                    device(f, lax.rem(z + d, groups), y, c),
                )
            )
    for a in range(count):
        pltpu.make_async_copy(ins[a], outs[a].at[f, z, y, c], local.at[a]).wait()
        for d in range(1, groups):
            block = outs[a].at[f, lax.rem(z + groups - d, groups), y, c]
            remote(block, block, a, d, core).wait_recv()
        mine = outs[a].at[f, :, y, c]
        start(remote(mine, mine, a, 0, across[orders[a][0]]))
        start(remote(mine, mine, a, groups, core))
    for a in range(count):
        if orders[a] == "yx":
            got = outs[a].at[f, :, 1 - y, c]
            mine = outs[a].at[f, :, :, c]
        else:
            got = outs[a].at[1 - f, :, y, c]
            mine = outs[a].at[:, :, y, c]
        remote(got, got, a, 0, core).wait_recv()
        start(remote(mine, mine, a, groups + 1, across[orders[a][1]]))
        start(remote(got, got, a, groups + 2, core))
    for a in range(count):
        if orders[a] == "yx":
            got = outs[a].at[1 - f, :, :, c]
        else:
            got = outs[a].at[:, :, 1 - y, c]
        remote(got, got, a, groups + 1, core).wait_recv()
        start(remote(got, got, a, groups + 3, core))
    for a in range(count):
        other = 1 - c
        block = outs[a].at[f, :, y, other]
        remote(block, block, a, groups, core).wait_recv()
        if orders[a] == "yx":
            second, third = outs[a].at[f, :, 1 - y, other], outs[a].at[1 - f, :, :, other]
        else:
            second, third = outs[a].at[1 - f, :, y, other], outs[a].at[:, :, 1 - y, other]
        remote(second, second, a, groups + 2, core).wait_recv()
        remote(third, third, a, groups + 3, core).wait_recv()
    for copy in started:
        copy.wait_send()


def gather(shards, orders, identity):
    n_f, n_s = lax.axis_size("fsdp"), lax.axis_size("seq")
    groups = n_s // 4
    count = len(shards)
    results = pl.pallas_call(
        partial(gather_kernel, groups, tuple(orders)),
        out_shape=[
            jax.ShapeDtypeStruct((n_f, groups, 2, 2) + shard.shape, shard.dtype)
            for shard in shards
        ],
        in_specs=[pl.BlockSpec(memory_space=pltpu.VMEM)] * count,
        out_specs=[pl.BlockSpec(memory_space=pltpu.HBM)] * count,
        scratch_shapes=[
            pltpu.SemaphoreType.DMA((count, groups + 4)),
            pltpu.SemaphoreType.DMA((count, groups + 4)),
            pltpu.SemaphoreType.DMA((count,)),
        ],
        compiler_params=pltpu.CompilerParams(
            collective_id=identity, has_side_effects=True, vmem_limit_bytes=VMEM_LIMIT
        ),
        name=f"gather_{identity}",
    )(*shards)
    return [
        whole.reshape(n_f * n_s * shard.shape[0], shard.shape[1])
        for whole, shard in zip(results, shards)
    ]


def gather_seq_kernel(groups, count, *refs):
    ins, outs = refs[:count], refs[count : 2 * count]
    send, recv, local = refs[2 * count :]
    f, z, y, c = place(groups)
    greet(groups, False)

    def remote(src, dst, a, slot, peer):
        return pltpu.make_async_remote_copy(
            src_ref=src,
            dst_ref=dst,
            send_sem=send.at[a, slot],
            recv_sem=recv.at[a, slot],
            device_id=peer,
            device_id_type=MESH,
        )

    core = device(f, z, y, 1 - c)
    side = device(f, z, 1 - y, c)
    started = []

    def start(copy):
        copy.start()
        started.append(copy)

    for a in range(count):
        pltpu.make_async_copy(ins[a], outs[a].at[z, y, c], local.at[a]).start()
        for d in range(1, groups):
            start(
                remote(
                    ins[a], outs[a].at[z, y, c], a, d, device(f, lax.rem(z + d, groups), y, c)
                )
            )
    for a in range(count):
        pltpu.make_async_copy(ins[a], outs[a].at[z, y, c], local.at[a]).wait()
        for d in range(1, groups):
            block = outs[a].at[lax.rem(z + groups - d, groups), y, c]
            remote(block, block, a, d, core).wait_recv()
        mine = outs[a].at[:, y, c]
        start(remote(mine, mine, a, 0, side))
        start(remote(mine, mine, a, groups, core))
    for a in range(count):
        got = outs[a].at[:, 1 - y, c]
        remote(got, got, a, 0, core).wait_recv()
        start(remote(got, got, a, groups + 1, core))
    for a in range(count):
        block = outs[a].at[:, y, 1 - c]
        remote(block, block, a, groups, core).wait_recv()
        block = outs[a].at[:, 1 - y, 1 - c]
        remote(block, block, a, groups + 1, core).wait_recv()
    for copy in started:
        copy.wait_send()


def gather_seq(shards, identity):
    n_s = lax.axis_size("seq")
    groups = n_s // 4
    count = len(shards)
    results = pl.pallas_call(
        partial(gather_seq_kernel, groups, count),
        out_shape=[
            jax.ShapeDtypeStruct((groups, 2, 2) + shard.shape, shard.dtype) for shard in shards
        ],
        in_specs=[pl.BlockSpec(memory_space=pltpu.VMEM)] * count,
        out_specs=[pl.BlockSpec(memory_space=pltpu.HBM)] * count,
        scratch_shapes=[
            pltpu.SemaphoreType.DMA((count, groups + 2)),
            pltpu.SemaphoreType.DMA((count, groups + 2)),
            pltpu.SemaphoreType.DMA((count,)),
        ],
        compiler_params=pltpu.CompilerParams(
            collective_id=identity, has_side_effects=True, vmem_limit_bytes=VMEM_LIMIT
        ),
        name=f"gather_seq_{identity}",
    )(*shards)
    return [
        whole.reshape(n_s * shard.shape[0], shard.shape[1])
        for whole, shard in zip(results, shards)
    ]


def scatter_kernel(groups, orders, *refs):
    count = len(orders)
    ins, outs = refs[:count], refs[count : 2 * count]
    held = refs[2 * count : 3 * count]
    from_core = refs[3 * count : 4 * count]
    from_first = refs[4 * count : 5 * count]
    from_second = refs[5 * count : 6 * count]
    from_z = refs[6 * count : 7 * count]
    send, recv, local = refs[7 * count :]
    f, z, y, c = place(groups)
    greet(groups, True)

    def remote(src, dst, a, slot, peer):
        return pltpu.make_async_remote_copy(
            src_ref=src,
            dst_ref=dst,
            send_sem=send.at[a, slot],
            recv_sem=recv.at[a, slot],
            device_id=peer,
            device_id_type=MESH,
        )

    core = device(f, z, y, 1 - c)
    across = {"y": device(f, z, 1 - y, c), "x": device(1 - f, z, y, c)}
    started = []

    def start(copy):
        copy.start()
        started.append(copy)

    def add(into, other):
        into[...] = (into[...].astype(F32) + other[...].astype(F32)).astype(BF16)

    for a in range(count):
        start(remote(ins[a].at[:, :, :, 1 - c], from_core[a], a, 0, core))
        pltpu.make_async_copy(ins[a].at[:, :, :, c], held[a], local.at[a]).start()
    for a in range(count):
        pltpu.make_async_copy(ins[a].at[:, :, :, c], held[a], local.at[a]).wait()
        remote(from_core[a], from_core[a], a, 0, core).wait_recv()
        if orders[a] == "xy":

            def part(g, carry, a=a):
                for k in range(2):
                    add(held[a].at[1 - f, g, k], from_core[a].at[1 - f, g, k])
                return carry

            lax.fori_loop(0, groups, part, 0)
            start(remote(held[a].at[1 - f], from_first[a], a, 1, across["x"]))

            def part(g, carry, a=a):
                for k in range(2):
                    add(held[a].at[f, g, k], from_core[a].at[f, g, k])
                return carry

            lax.fori_loop(0, groups, part, 0)
        else:

            def part(g, carry, a=a):
                for k in range(2):
                    add(held[a].at[k, g, 1 - y], from_core[a].at[k, g, 1 - y])
                return carry

            lax.fori_loop(0, groups, part, 0)
            start(remote(held[a].at[:, :, 1 - y], from_first[a], a, 1, across["y"]))

            def part(g, carry, a=a):
                for k in range(2):
                    add(held[a].at[k, g, y], from_core[a].at[k, g, y])
                return carry

            lax.fori_loop(0, groups, part, 0)
    for a in range(count):
        remote(from_first[a], from_first[a], a, 1, core).wait_recv()
        if orders[a] == "xy":

            def part(g, carry, a=a):
                for k in range(2):
                    add(held[a].at[f, g, k], from_first[a].at[g, k])
                return carry

            lax.fori_loop(0, groups, part, 0)
            start(remote(held[a].at[f, :, 1 - y], from_second[a], a, 2, across["y"]))
        else:

            def part(g, carry, a=a):
                for k in range(2):
                    add(held[a].at[k, g, y], from_first[a].at[k, g])
                return carry

            lax.fori_loop(0, groups, part, 0)
            start(remote(held[a].at[1 - f, :, y], from_second[a], a, 2, across["x"]))
    for a in range(count):
        remote(from_second[a], from_second[a], a, 2, core).wait_recv()

        def part(g, carry, a=a):
            add(held[a].at[f, g, y], from_second[a].at[g])
            return carry

        lax.fori_loop(0, groups, part, 0)
        for d in range(1, groups):
            there = lax.rem(z + d, groups)
            start(
                remote(held[a].at[f, there, y], from_z[a].at[d - 1], a, 2 + d, device(f, there, y, c))
            )
    for a in range(count):
        total = held[a][f, z, y].astype(F32)
        for d in range(1, groups):
            remote(from_z[a].at[d - 1], from_z[a].at[d - 1], a, 2 + d, core).wait_recv()
            total = total + from_z[a][d - 1].astype(F32)
        outs[a][...] = total
    for copy in started:
        copy.wait_send()


def scatter(partials, orders, identity):
    n_f, n_s = lax.axis_size("fsdp"), lax.axis_size("seq")
    groups = n_s // 4
    count = len(partials)
    blocks = [(p.shape[0] // (n_f * n_s), p.shape[1]) for p in partials]
    results = pl.pallas_call(
        partial(scatter_kernel, groups, tuple(orders)),
        out_shape=[jax.ShapeDtypeStruct(b, F32) for b in blocks],
        in_specs=[pl.BlockSpec(memory_space=pltpu.HBM)] * count,
        out_specs=[pl.BlockSpec(memory_space=pltpu.VMEM)] * count,
        scratch_shapes=[pltpu.VMEM((n_f, groups, 2) + b, BF16) for b in blocks]
        + [pltpu.VMEM((n_f, groups, 2) + b, BF16) for b in blocks]
        + [
            pltpu.VMEM(((groups, 2) if order == "xy" else (n_f, groups)) + b, BF16)
            for b, order in zip(blocks, orders)
        ]
        + [pltpu.VMEM((groups,) + b, BF16) for b in blocks]
        + [pltpu.VMEM((groups - 1,) + b, BF16) for b in blocks]
        + [
            pltpu.SemaphoreType.DMA((count, groups + 2)),
            pltpu.SemaphoreType.DMA((count, groups + 2)),
            pltpu.SemaphoreType.DMA((count,)),
        ],
        compiler_params=pltpu.CompilerParams(
            collective_id=identity, has_side_effects=True, vmem_limit_bytes=VMEM_LIMIT
        ),
        name=f"scatter_{identity}",
    )(*[p.reshape((n_f, groups, 2, 2) + b) for p, b in zip(partials, blocks)])
    return results


def scatter_seq_kernel(groups, in_ref, out_ref, held, from_core, from_y, from_z, send, recv, local):
    f, z, y, c = place(groups)
    greet(groups, False)

    def remote(src, dst, slot, peer):
        return pltpu.make_async_remote_copy(
            src_ref=src,
            dst_ref=dst,
            send_sem=send.at[slot],
            recv_sem=recv.at[slot],
            device_id=peer,
            device_id_type=MESH,
        )

    core = device(f, z, y, 1 - c)
    side = device(f, z, 1 - y, c)
    started = []

    def start(copy):
        copy.start()
        started.append(copy)

    def add(into, other):
        into[...] = (into[...].astype(F32) + other[...].astype(F32)).astype(BF16)

    start(remote(in_ref.at[:, :, 1 - c], from_core, 0, core))
    pltpu.make_async_copy(in_ref.at[:, :, c], held, local.at[0]).start()
    pltpu.make_async_copy(in_ref.at[:, :, c], held, local.at[0]).wait()
    remote(from_core, from_core, 0, core).wait_recv()

    def part(g, carry):
        add(held.at[g, 1 - y], from_core.at[g, 1 - y])
        return carry

    lax.fori_loop(0, groups, part, 0)
    start(remote(held.at[:, 1 - y], from_y, 1, side))

    def part(g, carry):
        add(held.at[g, y], from_core.at[g, y])
        return carry

    lax.fori_loop(0, groups, part, 0)
    remote(from_y, from_y, 1, side).wait_recv()

    def part(g, carry):
        add(held.at[g, y], from_y.at[g])
        return carry

    lax.fori_loop(0, groups, part, 0)
    for d in range(1, groups):
        there = lax.rem(z + d, groups)
        start(remote(held.at[there, y], from_z.at[d - 1], 1 + d, device(f, there, y, c)))
    total = held[z, y].astype(F32)
    for d in range(1, groups):
        remote(from_z.at[d - 1], from_z.at[d - 1], 1 + d, core).wait_recv()
        total = total + from_z[d - 1].astype(F32)
    out_ref[...] = total
    for copy in started:
        copy.wait_send()


def scatter_seq(partial_sums, identity):
    n_s = lax.axis_size("seq")
    groups = n_s // 4
    block = (partial_sums.shape[0] // n_s, partial_sums.shape[1])
    return pl.pallas_call(
        partial(scatter_seq_kernel, groups),
        out_shape=jax.ShapeDtypeStruct(block, F32),
        in_specs=[pl.BlockSpec(memory_space=pltpu.HBM)],
        out_specs=pl.BlockSpec(memory_space=pltpu.VMEM),
        scratch_shapes=[
            pltpu.VMEM((groups, 2) + block, BF16),
            pltpu.VMEM((groups, 2) + block, BF16),
            pltpu.VMEM((groups,) + block, BF16),
            pltpu.VMEM((groups - 1,) + block, BF16),
            pltpu.SemaphoreType.DMA((groups + 1,)),
            pltpu.SemaphoreType.DMA((groups + 1,)),
            pltpu.SemaphoreType.DMA((1,)),
        ],
        compiler_params=pltpu.CompilerParams(
            collective_id=identity, has_side_effects=True, vmem_limit_bytes=VMEM_LIMIT
        ),
        name=f"scatter_seq_{identity}",
    )(partial_sums.reshape((groups, 2, 2) + block))


def forward_kernel(span, bounds, query_ref, key_ref, value_ref, out_ref, norm_ref, stacked, peak, total):
    tokens = query_ref.shape[0]
    rows = tokens * HEADS
    scale = HEAD_DIM ** (-0.5)
    start, valid = bounds[0], bounds[1]
    for h in range(HEADS):
        stacked[h * tokens : (h + 1) * tokens, :] = query_ref[:, h * HEAD_DIM : (h + 1) * HEAD_DIM]
    peak[...] = jnp.full(peak.shape, -jnp.inf, F32)
    total[...] = jnp.zeros(total.shape, F32)
    out_ref[...] = jnp.zeros(out_ref.shape, F32)

    def block(j, masked):
        at = pl.multiple_of(j * span, span)
        keys = key_ref[pl.ds(at, span), :]
        values = value_ref[pl.ds(at, span), :]
        raw = times_transposed(stacked[...], keys) * scale
        if masked:
            key_pos = at + lax.broadcasted_iota(jnp.int32, (tokens, span), 1)
            row_pos = start + lax.broadcasted_iota(jnp.int32, (tokens, span), 0)
            allowed = (key_pos <= row_pos) & (key_pos < valid)
            raw = jnp.where(allowed[None], raw.reshape(HEADS, tokens, span), -jnp.inf)
            raw = raw.reshape(rows, span)
        old = peak[...]
        new = jnp.maximum(old, jnp.max(raw, axis=1, keepdims=True))
        shrink = jnp.exp(old - new)
        weights = jnp.exp(raw - new)
        total[...] = total[...] * shrink + jnp.sum(weights, axis=1, keepdims=True)
        out_ref[...] = out_ref[...] * shrink + matmul(weights.astype(BF16), values)
        peak[...] = new

    plain = jnp.minimum(start, valid) // span
    last = jnp.minimum(start + tokens, valid)
    every = (last + span - 1) // span

    def free(j, carry):
        block(j, False)
        return carry

    def edge(j, carry):
        block(j, True)
        return carry

    lax.fori_loop(0, plain, free, 0)
    lax.fori_loop(plain, every, edge, 0)
    out_ref[...] = out_ref[...] / total[...]
    norm_ref[...] = peak[...] + jnp.log(total[...])


def attention_forward(bounds, query, keys, values, span):
    tokens = query.shape[0]
    rows = tokens * HEADS
    return pl.pallas_call(
        partial(forward_kernel, span),
        out_shape=[
            jax.ShapeDtypeStruct((rows, HEAD_DIM), F32),
            jax.ShapeDtypeStruct((rows, 1), F32),
        ],
        in_specs=[pl.BlockSpec(memory_space=pltpu.SMEM)]
        + [pl.BlockSpec(memory_space=pltpu.VMEM)] * 3,
        out_specs=[pl.BlockSpec(memory_space=pltpu.VMEM)] * 2,
        scratch_shapes=[
            pltpu.VMEM((rows, HEAD_DIM), BF16),
            pltpu.VMEM((rows, 1), F32),
            pltpu.VMEM((rows, 1), F32),
        ],
        compiler_params=pltpu.CompilerParams(vmem_limit_bytes=VMEM_LIMIT),
        name="attention_forward",
    )(bounds, query, keys, values)


def backward_kernel(
    span, bounds, query_ref, grad_ref, key_ref, value_ref, norm_ref, delta_ref, gq_ref, gkv_ref, stacked, grads
):
    tokens = query_ref.shape[0]
    rows = tokens * HEADS
    scale = HEAD_DIM ** (-0.5)
    start, valid = bounds[0], bounds[1]
    for h in range(HEADS):
        columns = slice(h * HEAD_DIM, (h + 1) * HEAD_DIM)
        stacked[h * tokens : (h + 1) * tokens, :] = query_ref[:, columns]
        grads[h * tokens : (h + 1) * tokens, :] = grad_ref[:, columns]
    gq_ref[...] = jnp.zeros(gq_ref.shape, F32)

    def block(j, masked):
        at = pl.multiple_of(j * span, span)
        keys = key_ref[pl.ds(at, span), :]
        values = value_ref[pl.ds(at, span), :]
        raw = times_transposed(keys, stacked[...]) * scale
        soft = jnp.exp(raw - norm_ref[...])
        if masked:
            key_pos = at + lax.broadcasted_iota(jnp.int32, (span, tokens), 0)
            row_pos = start + lax.broadcasted_iota(jnp.int32, (span, tokens), 1)
            allowed = (key_pos <= row_pos) & (key_pos < valid)
            soft = jnp.where(jnp.concatenate([allowed] * HEADS, axis=1), soft, 0.0)
        toward = times_transposed(values, grads[...])
        pulled = (soft * (toward - delta_ref[...])).astype(BF16)
        gkv_ref[pl.ds(at, span), HEAD_DIM:] = matmul(soft.astype(BF16), grads[...]).astype(BF16)
        gkv_ref[pl.ds(at, span), :HEAD_DIM] = (matmul(pulled, stacked[...]) * scale).astype(BF16)
        gq_ref[...] += transposed_times(pulled, keys)

    plain = jnp.minimum(start, valid) // span
    last = jnp.minimum(start + tokens, valid)
    every = jnp.where(start < valid, (last + span - 1) // span, 0)
    plain = jnp.minimum(plain, every)

    def free(j, carry):
        block(j, False)
        return carry

    def edge(j, carry):
        block(j, True)
        return carry

    def empty(j, carry):
        at = pl.multiple_of(j * span, span)
        gkv_ref[pl.ds(at, span), :] = jnp.zeros((span, 2 * HEAD_DIM), BF16)
        return carry

    lax.fori_loop(0, plain, free, 0)
    lax.fori_loop(plain, every, edge, 0)
    lax.fori_loop(every, key_ref.shape[0] // span, empty, 0)
    gq_ref[...] = gq_ref[...] * scale


def attention_backward(bounds, query, grad, keys, values, norm, delta, span):
    tokens = query.shape[0]
    rows = tokens * HEADS
    return pl.pallas_call(
        partial(backward_kernel, span),
        out_shape=[
            jax.ShapeDtypeStruct((rows, HEAD_DIM), F32),
            jax.ShapeDtypeStruct((keys.shape[0], 2 * HEAD_DIM), BF16),
        ],
        in_specs=[pl.BlockSpec(memory_space=pltpu.SMEM)]
        + [pl.BlockSpec(memory_space=pltpu.VMEM)] * 6,
        out_specs=[pl.BlockSpec(memory_space=pltpu.VMEM)] * 2,
        scratch_shapes=[
            pltpu.VMEM((rows, HEAD_DIM), BF16),
            pltpu.VMEM((rows, HEAD_DIM), BF16),
        ],
        compiler_params=pltpu.CompilerParams(vmem_limit_bytes=VMEM_LIMIT),
        name="attention_backward",
    )(bounds, query, grad, keys, values, norm, delta)


def heads_to_columns(stacked):
    tokens = stacked.shape[0] // HEADS
    return jnp.concatenate([stacked[h * tokens : (h + 1) * tokens] for h in range(HEADS)], axis=1)


def gain_shard(gain):
    return jnp.zeros((8, 128), BF16).at[0, : gain.shape[0]].set(gain)


def gain_whole(gathered, rows):
    return gathered.reshape(-1, 8, 128)[:, 0, :rows].reshape(-1).astype(F32)


def gain_partial(grad, rows):
    count = grad.shape[0] // rows
    return jnp.pad(
        grad.astype(BF16).reshape(count, 1, rows), ((0, 0), (0, 7), (0, 128 - rows))
    ).reshape(count * 8, 128)


def per_device(
    hidden_in,
    cotangent,
    dataset_ids,
    mixing,
    pad_lengths,
    attention_gain,
    merged_projection,
    merged_adapter_in,
    query_adapter_out,
    keyval_adapter_out,
    output_projection,
    output_adapter_in,
    output_adapter_out,
    feedforward_gain,
    gate_up_weight,
    gate_up_adapter_in,
    gate_up_adapter_out,
    down_weight,
    down_adapter_in,
    down_adapter_out,
):
    tokens = hidden_in.shape[0]
    query_width = HEADS * HEAD_DIM
    model_rows = merged_projection.shape[0]
    rank_rows = query_adapter_out.shape[0]
    pair_rows = keyval_adapter_out.shape[0]
    out_rows = output_projection.shape[0]
    ff_rows = down_weight.shape[0]

    gain_one, merged, adapt_merged, lift_query, lift_keyval = gather(
        [
            gain_shard(attention_gain),
            pad_shard(merged_projection),
            pad_shard(merged_adapter_in),
            pad_shard(query_adapter_out),
            pad_shard(keyval_adapter_out),
        ],
        ["xy", "yx", "xy", "xy", "xy"],
        0,
    )
    out_full, adapt_out, lift_out, gain_two, gate_up, adapt_gate_up, lift_gate_up, down, adapt_down, lift_down = gather(
        [
            pad_shard(output_projection),
            pad_shard(output_adapter_in),
            pad_shard(output_adapter_out),
            gain_shard(feedforward_gain),
            pad_shard(gate_up_weight),
            pad_shard(gate_up_adapter_in),
            pad_shard(gate_up_adapter_out),
            pad_shard(down_weight),
            pad_shard(down_adapter_in),
            pad_shard(down_adapter_out),
        ],
        ["yx", "xy", "xy", "xy", "yx", "xy", "xy", "xy", "xy", "xy"],
        1,
    )
    gain_one = gain_whole(gain_one, model_rows)
    gain_two = gain_whole(gain_two, model_rows)

    hidden = hidden_in.astype(F32)
    normed_one, norm_one_back = jax.vjp(rms_scale, hidden, gain_one)
    first_in = spread(normed_one.astype(BF16), model_rows)
    projected = matmul(first_in, merged)
    lifted = matmul(first_in, adapt_merged).astype(BF16)
    lifted_query = spread(lifted[:, :RANK], rank_rows)
    lifted_pair = spread(lifted[:, RANK:], pair_rows)
    half_pair = lifted_pair.shape[1] // 2
    query_rows = projected[:, :query_width] + matmul(lifted_query, lift_query)
    key_rows = projected[:, query_width : query_width + HEAD_DIM] + matmul(
        lifted_pair[:, :half_pair], lift_keyval[:half_pair]
    )
    value_rows = projected[:, query_width + HEAD_DIM :] + matmul(
        lifted_pair[:, half_pair:], lift_keyval[half_pair:]
    )
    start_pos = lax.axis_index("seq") * tokens
    positions = start_pos + jnp.arange(tokens, dtype=jnp.int32)
    cosine_table, sine_table = rotary_tables(positions)
    query_rot = rotate_heads(query_rows, cosine_table, sine_table).astype(BF16)
    keys_rot = rotate(key_rows, cosine_table, sine_table).astype(BF16)
    keys_all, values_all = gather_seq([keys_rot, value_rows.astype(BF16)], 2)
    length = keys_all.shape[0]
    valid_count = length - pad_lengths[0]
    span = min(512, length)
    bounds = jnp.stack([start_pos, valid_count])

    attended, log_norm = attention_forward(bounds, query_rot, keys_all, values_all, span)
    attended_low = heads_to_columns(attended.astype(BF16))
    out_base = matmul(attended_low, out_full)
    lifted_out = matmul(attended_low, adapt_out).astype(BF16)
    lifted_out_wide = spread(lifted_out, rank_rows)
    middle = hidden + (out_base + matmul(lifted_out_wide, lift_out))

    normed_two, norm_two_back = jax.vjp(rms_scale, middle, gain_two)
    second_in = spread(normed_two.astype(BF16), model_rows)
    pre_gate = matmul(second_in, gate_up)
    lifted_gate_up = spread(matmul(second_in, adapt_gate_up).astype(BF16), pair_rows)
    half_gate = lifted_gate_up.shape[1] // 2
    gate_part = pre_gate[:, :FF] + matmul(lifted_gate_up[:, :half_gate], lift_gate_up[:half_gate])
    upper_part = pre_gate[:, FF:] + matmul(lifted_gate_up[:, half_gate:], lift_gate_up[half_gate:])
    activated, gelu_back = jax.vjp(partial(jax.nn.gelu, approximate=True), gate_part)
    inner = spread((activated * upper_part).astype(BF16), ff_rows)
    down_base = matmul(inner, down)
    lifted_down = spread(matmul(inner, adapt_down).astype(BF16), rank_rows)
    output = middle + (down_base + matmul(lifted_down, lift_down))

    matches = dataset_ids[:, None] == jnp.arange(DATASETS, dtype=jnp.int32)[None, :]
    picked = jnp.sum(jnp.where(matches, mixing[None, :], 0.0), axis=1)
    row_weight = jnp.where(positions < valid_count, picked, 0.0)
    scaled = cotangent.astype(F32) * row_weight[:, None]

    grad_branch = scaled.astype(BF16)
    grad_lifted_down = collect(times_transposed(grad_branch, lift_down), rank_rows).astype(BF16)
    grad_inner = collect(
        times_transposed(grad_branch, down) + times_transposed(grad_lifted_down, adapt_down), ff_rows
    )
    grad_gate = gelu_back(grad_inner * upper_part)[0].astype(BF16)
    grad_upper = (grad_inner * activated).astype(BF16)
    grad_gate_up = jnp.concatenate([grad_gate, grad_upper], axis=1)
    grad_lifted_gate_up = jnp.concatenate(
        [
            collect(times_transposed(grad_gate, lift_gate_up[:half_gate]), pair_rows),
            collect(times_transposed(grad_upper, lift_gate_up[half_gate:]), pair_rows),
        ],
        axis=1,
    ).astype(BF16)
    grad_normed_two = collect(
        times_transposed(grad_gate_up, gate_up)
        + times_transposed(grad_lifted_gate_up, adapt_gate_up),
        model_rows,
    )
    grad_middle_norm, gain_two_grad = norm_two_back(grad_normed_two)
    grad_middle = scaled + grad_middle_norm

    grad_attn = grad_middle.astype(BF16)
    grad_lifted_out = collect(times_transposed(grad_attn, lift_out), rank_rows).astype(BF16)
    grad_attention = (
        times_transposed(grad_attn, out_full) + times_transposed(grad_lifted_out, adapt_out)
    ).astype(BF16)
    correction = jnp.concatenate(
        [
            jnp.sum(
                grad_attention[:, h * HEAD_DIM : (h + 1) * HEAD_DIM].astype(F32)
                * attended[h * tokens : (h + 1) * tokens],
                axis=1,
            )
            for h in range(HEADS)
        ]
    )
    grad_query_rot, kv_terms = attention_backward(
        bounds,
        query_rot,
        grad_attention,
        keys_all,
        values_all,
        log_norm.reshape(1, -1),
        correction.reshape(1, -1),
        span,
    )
    kv_summed = scatter_seq(kv_terms, 3)
    grad_query_pre = rotate_heads(heads_to_columns(grad_query_rot), cosine_table, -sine_table)
    grad_keys = rotate(kv_summed[:, :HEAD_DIM], cosine_table, -sine_table)
    grad_merged = jnp.concatenate(
        [grad_query_pre.astype(BF16), grad_keys.astype(BF16), kv_summed[:, HEAD_DIM:].astype(BF16)],
        axis=1,
    )
    grad_lifted = jnp.concatenate(
        [
            collect(times_transposed(grad_merged[:, :query_width], lift_query), rank_rows),
            collect(
                times_transposed(
                    grad_merged[:, query_width : query_width + HEAD_DIM], lift_keyval[:half_pair]
                ),
                pair_rows,
            ),
            collect(
                times_transposed(grad_merged[:, query_width + HEAD_DIM :], lift_keyval[half_pair:]),
                pair_rows,
            ),
        ],
        axis=1,
    ).astype(BF16)
    grad_normed_one = collect(
        times_transposed(grad_merged, merged) + times_transposed(grad_lifted, adapt_merged),
        model_rows,
    )
    grad_hidden_norm, gain_one_grad = norm_one_back(grad_normed_one)
    hidden_grad = grad_middle + grad_hidden_norm

    keyval_term = jnp.concatenate(
        [
            transposed_times(
                lifted_pair[:, :half_pair], grad_merged[:, query_width : query_width + HEAD_DIM], BF16
            ),
            transposed_times(
                lifted_pair[:, half_pair:], grad_merged[:, query_width + HEAD_DIM :], BF16
            ),
        ],
        axis=0,
    )
    gate_up_term = jnp.concatenate(
        [
            transposed_times(lifted_gate_up[:, :half_gate], grad_gate, BF16),
            transposed_times(lifted_gate_up[:, half_gate:], grad_upper, BF16),
        ],
        axis=0,
    )
    summed = scatter(
        [
            transposed_times(second_in, grad_gate_up, BF16),
            transposed_times(inner, grad_branch, BF16),
            gate_up_term,
            transposed_times(first_in, grad_merged, BF16),
            transposed_times(attended_low, grad_attn, BF16),
            transposed_times(first_in, grad_lifted, BF16),
            transposed_times(inner, grad_lifted_down, BF16),
            transposed_times(second_in, grad_lifted_gate_up, BF16),
            transposed_times(lifted_query, grad_merged[:, :query_width], BF16),
            transposed_times(attended_low, grad_lifted_out, BF16),
            transposed_times(lifted_out_wide, grad_attn, BF16),
            transposed_times(lifted_down, grad_branch, BF16),
            keyval_term,
            gain_partial(gain_one_grad, model_rows),
            gain_partial(gain_two_grad, model_rows),
        ],
        ["xy", "yx", "yx", "xy", "xy", "yx", "yx", "yx", "yx", "yx", "yx", "yx", "yx", "yx", "yx"],
        4,
    )
    (
        gate_up_sum,
        down_sum,
        gate_up_out_sum,
        merged_sum,
        out_proj_sum,
        merged_in_sum,
        down_in_sum,
        gate_up_in_sum,
        query_out_sum,
        out_in_sum,
        out_out_sum,
        down_out_sum,
        keyval_sum,
        gain_one_sum,
        gain_two_sum,
    ) = summed
    return (
        output.astype(BF16),
        hidden_grad.astype(BF16),
        gain_one_sum[0, :model_rows],
        merged_sum[:model_rows],
        merged_in_sum[:model_rows],
        query_out_sum[:rank_rows],
        keyval_sum[:pair_rows],
        out_proj_sum[:out_rows],
        out_in_sum[:out_rows],
        out_out_sum[:rank_rows],
        gain_two_sum[0, :model_rows],
        gate_up_sum[:model_rows],
        gate_up_in_sum[:model_rows],
        gate_up_out_sum[:pair_rows],
        down_sum[:ff_rows],
        down_in_sum[:ff_rows],
        down_out_sum[:rank_rows],
    )


def solution(mesh):
    rows, vector = P(AXES, None), P(AXES)
    return jax.shard_map(
        per_device,
        mesh=mesh,
        in_specs=(rows, rows, vector, P(), P("fsdp"), vector)
        + (rows,) * 7
        + (vector,)
        + (rows,) * 6,
        out_specs=(rows, rows, vector) + (rows,) * 7 + (vector,) + (rows,) * 6,
        check_vma=False,
    )
```

```python
from functools import partial

import jax
import jax.numpy as jnp
from jax import lax
from jax.experimental import pallas as pl
from jax.experimental.pallas import tpu as pltpu
from jax.sharding import PartitionSpec as P

HEADS = 4
HEAD_DIM = 256
FF = 2048
RANK = 256
DATASETS = 16
EPSILON = 1e-06
MESH = pl.DeviceIdType.MESH
VMEM_LIMIT = 60 * 1024 * 1024
AXES = ("fsdp", "seq")
BF16 = jnp.bfloat16
F32 = jnp.float32


def rms_scale(values, gain_vector):
    inverse = lax.rsqrt(jnp.mean(values * values, axis=-1, keepdims=True) + EPSILON)
    return values * inverse * gain_vector


def rotary_tables(positions):
    half_width = HEAD_DIM // 2
    inverse = 10000.0 ** (-2.0 * jnp.arange(half_width, dtype=F32) / HEAD_DIM)
    angles = positions.astype(F32)[:, None] * inverse[None, :]
    return (jnp.cos(angles), jnp.sin(angles))


def rotate(values, cosine_table, sine_table):
    half_width = values.shape[-1] // 2
    first = values[..., :half_width]
    second = values[..., half_width:]
    return jnp.concatenate(
        [first * cosine_table - second * sine_table, second * cosine_table + first * sine_table],
        axis=-1,
    )


def rotate_heads(values, cosine_table, sine_table):
    parts = [
        rotate(values[:, h * HEAD_DIM : (h + 1) * HEAD_DIM], cosine_table, sine_table)
        for h in range(HEADS)
    ]
    return jnp.concatenate(parts, axis=1)


def matmul(left_side, right_side):
    return jnp.dot(left_side, right_side, preferred_element_type=F32)


def times_transposed(left_side, right_side):
    return lax.dot_general(
        left_side, right_side, (((1,), (1,)), ((), ())), preferred_element_type=F32
    )


def transposed_times(left_side, right_side, out=F32):
    return lax.dot_general(
        left_side, right_side, (((0,), (0,)), ((), ())), preferred_element_type=F32
    ).astype(out)


def padded_rows(rows):
    return -(-rows // 8) * 8


def padded_model_rows(rows):
    return -(-(rows + 1) // 8) * 8


def selection(rows, wide, count):
    source = lax.broadcasted_iota(jnp.int32, (count * rows, count * wide), 0)
    target = lax.broadcasted_iota(jnp.int32, (count * rows, count * wide), 1)
    inside = target % wide
    return ((source == target // wide * rows + inside) & (inside < rows)).astype(BF16)


def spread(values, rows, wide):
    if wide == rows:
        return values
    return matmul(values, selection(rows, wide, values.shape[1] // rows)).astype(BF16)


def collect(values, rows, wide):
    if wide == rows:
        return values
    chosen = selection(rows, wide, values.shape[1] // wide)
    first = values.astype(BF16)
    rest = values - first.astype(F32)
    second = rest.astype(BF16)
    third = (rest - second.astype(F32)).astype(BF16)
    return (
        times_transposed(first, chosen)
        + times_transposed(second, chosen)
        + times_transposed(third, chosen)
    )


def place(groups):
    f = lax.axis_index("fsdp")
    s = lax.axis_index("seq")
    c = lax.rem(s, 2)
    y = lax.rem(s // 2, 2)
    z = s // 4
    return f, z, y, c


def device(f, z, y, c):
    return (f, (z * 2 + y) * 2 + c)


def greet(groups, both):
    f, z, y, c = place(groups)
    barrier = pltpu.get_barrier_semaphore()
    peers = [device(f, z, y, 1 - c), device(f, z, 1 - y, c)]
    if both:
        peers.append(device(1 - f, z, y, c))
    for d in range(1, groups):
        peers.append(device(f, lax.rem(z + d, groups), y, c))
    for peer in peers:
        pl.semaphore_signal(barrier, inc=1, device_id=peer, device_id_type=MESH)
    pl.semaphore_wait(barrier, len(peers))


def pieces(rows, columns, target):
    count = max(1, min(columns // 128, round(rows * columns * 2 / target)))
    edges = [round(columns // 128 * i / count) * 128 for i in range(count)] + [columns]
    return [(lo, hi - lo) for lo, hi in zip(edges[:-1], edges[1:])]


def balanced(chunks, weight_first, loads):
    orders = []
    for bytes_each in chunks:
        light, heavy = (4, 8) if weight_first == "light" else (8, 4)
        xy = max(loads[0] + light * bytes_each, loads[1] + heavy * bytes_each)
        yx = max(loads[0] + heavy * bytes_each, loads[1] + light * bytes_each)
        if xy <= yx:
            orders.append("xy")
            loads = (loads[0] + light * bytes_each, loads[1] + heavy * bytes_each)
        else:
            orders.append("yx")
            loads = (loads[0] + heavy * bytes_each, loads[1] + light * bytes_each)
    return orders


def mixed(rows_jobs, jobs):
    step = MIX * len(jobs) / max(1, len(rows_jobs))
    keyed = [(i * step, 0, job) for i, job in enumerate(rows_jobs)]
    keyed += [(float(i), 1, job) for i, job in enumerate(jobs)]
    return [job for _, _, job in sorted(keyed, key=lambda entry: entry[:2])]


def run_jobs(jobs, spacing):
    depth = max(len(stages) for stages in jobs)
    for tick in range(len(jobs) + spacing * (depth - 1)):
        for stage in reversed(range(depth)):
            j = tick - spacing * stage
            if 0 <= j < len(jobs) and stage < len(jobs[j]):
                jobs[j][stage]()


class Mover:
    def __init__(self, groups, send, recv, local):
        self.groups = groups
        self.send, self.recv, self.local = send, recv, local
        self.f, self.z, self.y, self.c = place(groups)
        f, z, y, c = self.f, self.z, self.y, self.c
        self.core = device(f, z, y, 1 - c)
        self.across = {"y": device(f, z, 1 - y, c), "x": device(1 - f, z, y, c)}
        self.started = []

    def along_z(self, d):
        return device(self.f, lax.rem(self.z + d, self.groups), self.y, self.c)

    def remote(self, src, dst, job, slot, peer):
        return pltpu.make_async_remote_copy(
            src_ref=src,
            dst_ref=dst,
            send_sem=self.send.at[job, slot],
            recv_sem=self.recv.at[job, slot],
            device_id=peer,
            device_id_type=MESH,
        )

    def start(self, src, dst, job, slot, peer):
        copy = self.remote(src, dst, job, slot, peer)
        copy.start()
        self.started.append(copy)

    def arrived(self, ref, job, slot):
        self.remote(ref, ref, job, slot, self.core).wait_recv()

    def drain(self):
        for copy in self.started:
            copy.wait_send()


def gather_job(m, job, order, source, whole, lo, width):
    groups, f, z, y, c = m.groups, m.f, m.z, m.y, m.c
    columns = slice(lo, lo + width)
    own = source.at[:, columns]

    def at(*index):
        return whole.at[index + (slice(None), columns)]

    every = slice(None)

    def begin():
        pltpu.make_async_copy(own, at(f, z, y, c), m.local.at[job]).start()
        for d in range(1, groups):
            m.start(own, at(f, z, y, c), job, d, m.along_z(d))

    def first():
        pltpu.make_async_copy(own, at(f, z, y, c), m.local.at[job]).wait()
        for d in range(1, groups):
            m.arrived(at(f, lax.rem(z + groups - d, groups), y, c), job, d)
        mine = at(f, every, y, c)
        m.start(mine, mine, job, 0, m.across[order[0]])
        m.start(mine, mine, job, groups, m.core)

    def second():
        if order == "yx":
            got, mine = at(f, every, 1 - y, c), at(f, every, every, c)
        else:
            got, mine = at(1 - f, every, y, c), at(every, every, y, c)
        m.arrived(got, job, 0)
        m.start(mine, mine, job, groups + 1, m.across[order[1]])
        m.start(got, got, job, groups + 2, m.core)

    def third():
        got = at(1 - f, every, every, c) if order == "yx" else at(every, every, 1 - y, c)
        m.arrived(got, job, groups + 1)
        m.start(got, got, job, groups + 3, m.core)

    def last():
        other = 1 - c
        m.arrived(at(f, every, y, other), job, groups)
        if order == "yx":
            m.arrived(at(f, every, 1 - y, other), job, groups + 2)
            m.arrived(at(1 - f, every, every, other), job, groups + 3)
        else:
            m.arrived(at(1 - f, every, y, other), job, groups + 2)
            m.arrived(at(every, every, 1 - y, other), job, groups + 3)

    return [begin, first, second, third, last]


def gather_rows_job(m, job, source, whole, lo, width):
    groups, z, y, c = m.groups, m.z, m.y, m.c
    columns = slice(lo, lo + width)
    own = source.at[:, columns]
    every = slice(None)

    def at(*index):
        return whole.at[index + (slice(None), columns)]

    def begin():
        pltpu.make_async_copy(own, at(z, y, c), m.local.at[job]).start()
        for d in range(1, groups):
            m.start(own, at(z, y, c), job, d, m.along_z(d))

    def first():
        pltpu.make_async_copy(own, at(z, y, c), m.local.at[job]).wait()
        for d in range(1, groups):
            m.arrived(at(lax.rem(z + groups - d, groups), y, c), job, d)
        mine = at(every, y, c)
        m.start(mine, mine, job, 0, m.across["y"])
        m.start(mine, mine, job, groups, m.core)

    def second():
        got = at(every, 1 - y, c)
        m.arrived(got, job, 0)
        m.start(got, got, job, groups + 1, m.core)

    def last():
        m.arrived(at(every, y, 1 - c), job, groups)
        m.arrived(at(every, 1 - y, 1 - c), job, groups + 1)

    return [begin, first, second, last]


MIX = 0.6
GATHER_BYTES = 20 * 1024
ROWS_BYTES = 32 * 1024
GATHER_SPACING = 3
SCATTER_BYTES = 20 * 1024
SCATTER_SPACING = 4


def gather_kernel(groups, plan, rows_plan, *refs):
    rows_count = len({entry[0] for entry in rows_plan})
    count = rows_count + len({entry[0] for entry in plan})
    ins, outs = refs[:count], refs[count : 2 * count]
    send, recv, local = refs[2 * count :]
    greet(groups, True)
    m = Mover(groups, send, recv, local)
    jobs = []
    for a, lo, width in rows_plan:
        jobs.append(gather_rows_job(m, len(jobs), ins[a], outs[a], lo, width))
    for a, lo, width, order in plan:
        jobs.append(gather_job(m, len(jobs), order, ins[rows_count + a], outs[rows_count + a], lo, width))
    run_jobs(mixed(jobs[: len(rows_plan)], jobs[len(rows_plan) :]), GATHER_SPACING)
    m.drain()


def gather(token_rows, shards, identity):
    n_f, n_s = lax.axis_size("fsdp"), lax.axis_size("seq")
    groups = n_s // 4
    rows_plan = [
        (a, lo, width)
        for a, block in enumerate(token_rows)
        for lo, width in pieces(block.shape[0], block.shape[1], ROWS_BYTES)
    ]
    cuts = [
        (a, lo, width)
        for a, shard in enumerate(shards)
        for lo, width in pieces(shard.shape[0], shard.shape[1], GATHER_BYTES)
    ]
    sizes = [shards[a].shape[0] * width for a, _, width in cuts]
    held = sum(4 * block.shape[0] * block.shape[1] for block in token_rows)
    orders = balanced(sizes, "light", (0, held))
    plan = [cut + (order,) for cut, order in zip(cuts, orders)]
    operands = list(token_rows) + list(shards)
    jobs = len(rows_plan) + len(plan)
    results = pl.pallas_call(
        partial(gather_kernel, groups, tuple(plan), tuple(rows_plan)),
        out_shape=[
            jax.ShapeDtypeStruct((groups, 2, 2) + block.shape, block.dtype) for block in token_rows
        ]
        + [
            jax.ShapeDtypeStruct((n_f, groups, 2, 2) + shard.shape, shard.dtype)
            for shard in shards
        ],
        in_specs=[pl.BlockSpec(memory_space=pltpu.VMEM)] * len(operands),
        out_specs=[pl.BlockSpec(memory_space=pltpu.HBM)] * len(operands),
        scratch_shapes=[
            pltpu.SemaphoreType.DMA((jobs, groups + 4)),
            pltpu.SemaphoreType.DMA((jobs, groups + 4)),
            pltpu.SemaphoreType.DMA((jobs,)),
        ],
        compiler_params=pltpu.CompilerParams(
            collective_id=identity, has_side_effects=True, vmem_limit_bytes=VMEM_LIMIT
        ),
        name=f"gather_{identity}",
    )(*operands)
    return [whole.reshape(-1, block.shape[1]) for whole, block in zip(results, operands)]


def scatter_job(m, job, order, source, out, lo, width, buffers):
    groups, f, z, y, c = m.groups, m.f, m.z, m.y, m.c
    columns = slice(lo, lo + width)
    every = slice(None)
    held, from_core, from_first, from_second, from_z = buffers

    def half(core):
        return source.at[:, :, :, core, :, columns]

    def add(into, other):
        into[...] = into[...] + other[...]

    def each(step):
        def part(g, carry):
            step(g)
            return carry

        lax.fori_loop(0, groups, part, 0)

    def begin():
        m.start(half(1 - c), from_core, job, 0, m.core)
        pltpu.make_async_copy(half(c), held, m.local.at[job]).start()

    def first():
        pltpu.make_async_copy(half(c), held, m.local.at[job]).wait()
        m.arrived(from_core, job, 0)
        if order == "xy":
            def pair(side):
                def step(g):
                    for k in range(2):
                        add(held.at[side, g, k], from_core.at[side, g, k])
                return step

            each(pair(1 - f))
            m.start(held.at[1 - f], from_first, job, 1, m.across["x"])
            each(pair(f))
        else:
            def pair(side):
                def step(g):
                    for k in range(2):
                        add(held.at[k, g, side], from_core.at[k, g, side])
                return step

            each(pair(1 - y))
            m.start(held.at[:, :, 1 - y], from_first, job, 1, m.across["y"])
            each(pair(y))

    def second():
        m.arrived(from_first, job, 1)
        if order == "xy":
            def side(k):
                return lambda g: add(held.at[f, g, k], from_first.at[g, k])

            each(side(1 - y))
            m.start(held.at[f, :, 1 - y], from_second, job, 2, m.across["y"])
            each(side(y))
        else:
            def side(k):
                return lambda g: add(held.at[k, g, y], from_first.at[k, g])

            each(side(1 - f))
            m.start(held.at[1 - f, :, y], from_second, job, 2, m.across["x"])
            each(side(f))

    def third():
        m.arrived(from_second, job, 2)
        each(lambda g: add(held.at[f, g, y], from_second.at[g]))
        for d in range(1, groups):
            there = lax.rem(z + d, groups)
            m.start(held.at[f, there, y], from_z.at[d - 1], job, 2 + d, m.along_z(d))

    def last():
        total = held[f, z, y].astype(F32)
        for d in range(1, groups):
            m.arrived(from_z.at[d - 1], job, 2 + d)
            total = total + from_z[d - 1].astype(F32)
        out[:, columns] = total

    return [begin, first, second, third, last]


def scatter_rows_job(m, job, source, out, lo, width, buffers):
    groups, z, y, c = m.groups, m.z, m.y, m.c
    columns = slice(lo, lo + width)
    held, from_core, from_y, from_z = buffers

    def half(core):
        return source.at[:, :, core, :, columns]

    def add(into, other):
        into[...] = into[...] + other[...]

    def each(step):
        def part(g, carry):
            step(g)
            return carry

        lax.fori_loop(0, groups, part, 0)

    def begin():
        m.start(half(1 - c), from_core, job, 0, m.core)
        pltpu.make_async_copy(half(c), held, m.local.at[job]).start()

    def first():
        pltpu.make_async_copy(half(c), held, m.local.at[job]).wait()
        m.arrived(from_core, job, 0)
        each(lambda g: add(held.at[g, 1 - y], from_core.at[g, 1 - y]))
        m.start(held.at[:, 1 - y], from_y, job, 1, m.across["y"])
        each(lambda g: add(held.at[g, y], from_core.at[g, y]))

    def second():
        m.arrived(from_y, job, 1)
        each(lambda g: add(held.at[g, y], from_y.at[g]))
        for d in range(1, groups):
            there = lax.rem(z + d, groups)
            m.start(held.at[there, y], from_z.at[d - 1], job, 2 + d, m.along_z(d))

    def last():
        total = held[z, y].astype(F32)
        for d in range(1, groups):
            m.arrived(from_z.at[d - 1], job, 2 + d)
            total = total + from_z[d - 1].astype(F32)
        out[:, columns] = total

    return [begin, first, second, last]


def scatter_kernel(groups, plan, rows_plan, rows_count, count, *refs):
    ins, outs = refs[:count], refs[count : 2 * count]
    send, recv, local = refs[2 * count : 2 * count + 3]
    scratch = list(refs[2 * count + 3 :])
    greet(groups, True)
    m = Mover(groups, send, recv, local)
    jobs = []
    for a, lo, width in rows_plan:
        buffers, scratch = scratch[:4], scratch[4:]
        jobs.append(scatter_rows_job(m, len(jobs), ins[a], outs[a], lo, width, buffers))
    for a, lo, width, order in plan:
        buffers, scratch = scratch[:5], scratch[5:]
        jobs.append(
            scatter_job(m, len(jobs), order, ins[rows_count + a], outs[rows_count + a], lo, width, buffers)
        )
    run_jobs(mixed(jobs[: len(rows_plan)], jobs[len(rows_plan) :]), SCATTER_SPACING)
    m.drain()


def scatter(token_rows, partials, identity):
    n_f, n_s = lax.axis_size("fsdp"), lax.axis_size("seq")
    groups = n_s // 4
    row_blocks = [(p.shape[0] // n_s, p.shape[1]) for p in token_rows]
    blocks = [(p.shape[0] // (n_f * n_s), p.shape[1]) for p in partials]
    rows_plan = [
        (a, lo, width)
        for a, block in enumerate(row_blocks)
        for lo, width in pieces(block[0], block[1], ROWS_BYTES)
    ]
    cuts = [
        (a, lo, width)
        for a, block in enumerate(blocks)
        for lo, width in pieces(block[0], block[1], SCATTER_BYTES)
    ]
    sizes = [blocks[a][0] * width for a, _, width in cuts]
    held = sum(4 * rows * columns for rows, columns in row_blocks)
    orders = balanced(sizes, "heavy", (0, held))
    plan = [cut + (order,) for cut, order in zip(cuts, orders)]
    jobs = len(rows_plan) + len(plan)
    scratch = []
    for a, _, width in rows_plan:
        block = (row_blocks[a][0], width)
        scratch += [
            pltpu.VMEM((groups, 2) + block, BF16),
            pltpu.VMEM((groups, 2) + block, BF16),
            pltpu.VMEM((groups,) + block, BF16),
            pltpu.VMEM((groups - 1,) + block, BF16),
        ]
    for a, _, width, order in plan:
        block = (blocks[a][0], width)
        scratch += [
            pltpu.VMEM((n_f, groups, 2) + block, BF16),
            pltpu.VMEM((n_f, groups, 2) + block, BF16),
            pltpu.VMEM(((groups, 2) if order == "xy" else (n_f, groups)) + block, BF16),
            pltpu.VMEM((groups,) + block, BF16),
            pltpu.VMEM((groups - 1,) + block, BF16),
        ]
    count = len(row_blocks) + len(blocks)
    return pl.pallas_call(
        partial(scatter_kernel, groups, tuple(plan), tuple(rows_plan), len(row_blocks), count),
        out_shape=[jax.ShapeDtypeStruct(b, F32) for b in row_blocks + blocks],
        in_specs=[pl.BlockSpec(memory_space=pltpu.HBM)] * count,
        out_specs=[pl.BlockSpec(memory_space=pltpu.VMEM)] * count,
        scratch_shapes=[
            pltpu.SemaphoreType.DMA((jobs, groups + 2)),
            pltpu.SemaphoreType.DMA((jobs, groups + 2)),
            pltpu.SemaphoreType.DMA((jobs,)),
        ]
        + scratch,
        compiler_params=pltpu.CompilerParams(
            collective_id=identity, has_side_effects=True, vmem_limit_bytes=VMEM_LIMIT
        ),
        name=f"scatter_{identity}",
    )(
        *[p.reshape((groups, 2, 2) + b) for p, b in zip(token_rows, row_blocks)],
        *[p.reshape((n_f, groups, 2, 2) + b) for p, b in zip(partials, blocks)],
    )


def finish_kernel(cuts, count, *refs):
    total = len(cuts)
    ins, outs = refs[:count], refs[count : count + total]
    staged, sems = refs[count + total : count + 2 * total], refs[count + 2 * total]
    for i, (a, rows, lo, width) in enumerate(cuts):
        staged[i][...] = ins[a][0:rows, lo : lo + width]
    for i in range(total):
        pltpu.make_async_copy(staged[i], outs[i], sems.at[i]).start()
    for i in range(total):
        pltpu.make_async_copy(staged[i], outs[i], sems.at[i]).wait()


def finish(sums, cuts):
    shapes = [(rows, width) for _, rows, _, width in cuts]
    return pl.pallas_call(
        partial(finish_kernel, tuple(cuts), len(sums)),
        out_shape=[jax.ShapeDtypeStruct(shape, F32) for shape in shapes],
        in_specs=[pl.BlockSpec(memory_space=pltpu.VMEM)] * len(sums),
        out_specs=[pl.BlockSpec(memory_space=pltpu.HBM)] * len(cuts),
        scratch_shapes=[pltpu.VMEM(shape, F32) for shape in shapes]
        + [pltpu.SemaphoreType.DMA((len(cuts),))],
        compiler_params=pltpu.CompilerParams(vmem_limit_bytes=VMEM_LIMIT),
        name="finish",
    )(*sums)


def forward_kernel(span, bounds, query_ref, key_ref, value_ref, out_ref, norm_ref, stacked, peak, total):
    tokens = query_ref.shape[0]
    rows = tokens * HEADS
    scale = HEAD_DIM ** (-0.5)
    start, valid = bounds[0], bounds[1]
    for h in range(HEADS):
        stacked[h * tokens : (h + 1) * tokens, :] = query_ref[:, h * HEAD_DIM : (h + 1) * HEAD_DIM]
    peak[...] = jnp.full(peak.shape, -jnp.inf, F32)
    total[...] = jnp.zeros(total.shape, F32)
    out_ref[...] = jnp.zeros(out_ref.shape, F32)

    def block(j, masked):
        at = pl.multiple_of(j * span, span)
        keys = key_ref[pl.ds(at, span), :]
        values = value_ref[pl.ds(at, span), :]
        raw = times_transposed(stacked[...], keys) * scale
        if masked:
            key_pos = at + lax.broadcasted_iota(jnp.int32, (tokens, span), 1)
            row_pos = start + lax.broadcasted_iota(jnp.int32, (tokens, span), 0)
            allowed = (key_pos <= row_pos) & (key_pos < valid)
            raw = jnp.where(allowed[None], raw.reshape(HEADS, tokens, span), -jnp.inf)
            raw = raw.reshape(rows, span)
        old = peak[...]
        new = jnp.maximum(old, jnp.max(raw, axis=1, keepdims=True))
        shrink = jnp.exp(old - new)
        weights = jnp.exp(raw - new)
        total[...] = total[...] * shrink + jnp.sum(weights, axis=1, keepdims=True)
        out_ref[...] = out_ref[...] * shrink + matmul(weights.astype(BF16), values)
        peak[...] = new

    plain = jnp.minimum(start, valid) // span
    last = jnp.minimum(start + tokens, valid)
    every = (last + span - 1) // span

    def free(j, carry):
        block(j, False)
        return carry

    def edge(j, carry):
        block(j, True)
        return carry

    lax.fori_loop(0, plain, free, 0)
    lax.fori_loop(plain, every, edge, 0)
    out_ref[...] = out_ref[...] / total[...]
    norm_ref[...] = peak[...] + jnp.log(total[...])


def attention_forward(bounds, query, keys, values, span):
    tokens = query.shape[0]
    rows = tokens * HEADS
    return pl.pallas_call(
        partial(forward_kernel, span),
        out_shape=[
            jax.ShapeDtypeStruct((rows, HEAD_DIM), F32),
            jax.ShapeDtypeStruct((rows, 1), F32),
        ],
        in_specs=[pl.BlockSpec(memory_space=pltpu.SMEM)]
        + [pl.BlockSpec(memory_space=pltpu.VMEM)] * 3,
        out_specs=[pl.BlockSpec(memory_space=pltpu.VMEM)] * 2,
        scratch_shapes=[
            pltpu.VMEM((rows, HEAD_DIM), BF16),
            pltpu.VMEM((rows, 1), F32),
            pltpu.VMEM((rows, 1), F32),
        ],
        compiler_params=pltpu.CompilerParams(vmem_limit_bytes=VMEM_LIMIT),
        name="attention_forward",
    )(bounds, query, keys, values)


def backward_kernel(
    span, bounds, query_ref, grad_ref, key_ref, value_ref, norm_ref, delta_ref, gq_ref, gkv_ref, stacked, grads
):
    tokens = query_ref.shape[0]
    rows = tokens * HEADS
    scale = HEAD_DIM ** (-0.5)
    start, valid = bounds[0], bounds[1]
    for h in range(HEADS):
        columns = slice(h * HEAD_DIM, (h + 1) * HEAD_DIM)
        stacked[h * tokens : (h + 1) * tokens, :] = query_ref[:, columns]
        grads[h * tokens : (h + 1) * tokens, :] = grad_ref[:, columns]
    gq_ref[...] = jnp.zeros(gq_ref.shape, F32)

    def block(j, masked):
        at = pl.multiple_of(j * span, span)
        keys = key_ref[pl.ds(at, span), :]
        values = value_ref[pl.ds(at, span), :]
        raw = times_transposed(keys, stacked[...]) * scale
        soft = jnp.exp(raw - norm_ref[...])
        if masked:
            key_pos = at + lax.broadcasted_iota(jnp.int32, (span, tokens), 0)
            row_pos = start + lax.broadcasted_iota(jnp.int32, (span, tokens), 1)
            allowed = (key_pos <= row_pos) & (key_pos < valid)
            soft = jnp.where(jnp.concatenate([allowed] * HEADS, axis=1), soft, 0.0)
        toward = times_transposed(values, grads[...])
        pulled = (soft * (toward - delta_ref[...])).astype(BF16)
        gkv_ref[pl.ds(at, span), HEAD_DIM:] = matmul(soft.astype(BF16), grads[...]).astype(BF16)
        gkv_ref[pl.ds(at, span), :HEAD_DIM] = (matmul(pulled, stacked[...]) * scale).astype(BF16)
        gq_ref[...] += transposed_times(pulled, keys)

    plain = jnp.minimum(start, valid) // span
    last = jnp.minimum(start + tokens, valid)
    every = jnp.where(start < valid, (last + span - 1) // span, 0)
    plain = jnp.minimum(plain, every)

    def free(j, carry):
        block(j, False)
        return carry

    def edge(j, carry):
        block(j, True)
        return carry

    def empty(j, carry):
        at = pl.multiple_of(j * span, span)
        gkv_ref[pl.ds(at, span), :] = jnp.zeros((span, 2 * HEAD_DIM), BF16)
        return carry

    lax.fori_loop(0, plain, free, 0)
    lax.fori_loop(plain, every, edge, 0)
    lax.fori_loop(every, key_ref.shape[0] // span, empty, 0)
    gq_ref[...] = gq_ref[...] * scale


def attention_backward(bounds, query, grad, keys, values, norm, delta, span):
    tokens = query.shape[0]
    rows = tokens * HEADS
    return pl.pallas_call(
        partial(backward_kernel, span),
        out_shape=[
            jax.ShapeDtypeStruct((rows, HEAD_DIM), F32),
            jax.ShapeDtypeStruct((keys.shape[0], 2 * HEAD_DIM), BF16),
        ],
        in_specs=[pl.BlockSpec(memory_space=pltpu.SMEM)]
        + [pl.BlockSpec(memory_space=pltpu.VMEM)] * 6,
        out_specs=[pl.BlockSpec(memory_space=pltpu.VMEM)] * 2,
        scratch_shapes=[
            pltpu.VMEM((rows, HEAD_DIM), BF16),
            pltpu.VMEM((rows, HEAD_DIM), BF16),
        ],
        compiler_params=pltpu.CompilerParams(vmem_limit_bytes=VMEM_LIMIT),
        name="attention_backward",
    )(bounds, query, grad, keys, values, norm, delta)


def heads_to_columns(stacked):
    tokens = stacked.shape[0] // HEADS
    return jnp.concatenate([stacked[h * tokens : (h + 1) * tokens] for h in range(HEADS)], axis=1)


def model_shard(first, second, gain):
    rows = first.shape[0]
    wide = padded_model_rows(rows)
    block = jnp.concatenate([first, second], axis=1)
    spare = jnp.pad(gain[None], ((0, wide - rows - 1), (0, block.shape[1] - rows)))
    return jnp.concatenate([block, spare], axis=0)


def plain_shard(*weights):
    block = weights[0] if len(weights) == 1 else jnp.concatenate(weights, axis=1)
    rows = block.shape[0]
    return jnp.pad(block, ((0, padded_rows(rows) - rows), (0, 0)))


def gain_whole(gathered, rows):
    wide = padded_model_rows(rows)
    return gathered.reshape(-1, wide, gathered.shape[1])[:, rows, :rows].reshape(-1).astype(F32)


def with_gain(partial_sums, gain_grad, rows):
    wide = padded_model_rows(rows)
    blocks = partial_sums.reshape(-1, wide, partial_sums.shape[1])
    return blocks.at[:, rows, :rows].set(gain_grad.reshape(-1, rows).astype(BF16)).reshape(partial_sums.shape)


def per_device(
    hidden_in,
    cotangent,
    dataset_ids,
    mixing,
    pad_lengths,
    attention_gain,
    merged_projection,
    merged_adapter_in,
    query_adapter_out,
    keyval_adapter_out,
    output_projection,
    output_adapter_in,
    output_adapter_out,
    feedforward_gain,
    gate_up_weight,
    gate_up_adapter_in,
    gate_up_adapter_out,
    down_weight,
    down_adapter_in,
    down_adapter_out,
):
    tokens, width = hidden_in.shape
    query_width = HEADS * HEAD_DIM
    merged_width = query_width + 2 * HEAD_DIM
    model_rows = merged_projection.shape[0]
    rank_rows = query_adapter_out.shape[0]
    pair_rows = keyval_adapter_out.shape[0]
    out_rows = output_projection.shape[0]
    ff_rows = down_weight.shape[0]
    model_wide, rank_wide = padded_model_rows(model_rows), padded_rows(rank_rows)
    pair_wide, ff_wide = padded_rows(pair_rows), padded_rows(ff_rows)

    merged, lift_query, lift_keyval = gather(
        [],
        [
            model_shard(merged_projection, merged_adapter_in, attention_gain),
            plain_shard(query_adapter_out),
            plain_shard(keyval_adapter_out),
        ],
        0,
    )
    gain_one = gain_whole(merged, model_rows)

    hidden = hidden_in.astype(F32)
    normed_one, norm_one_back = jax.vjp(rms_scale, hidden, gain_one)
    first_in = spread(normed_one.astype(BF16), model_rows, model_wide)
    projected = matmul(first_in, merged)
    lifted = projected[:, merged_width:].astype(BF16)
    lifted_query = spread(lifted[:, :RANK], rank_rows, rank_wide)
    lifted_pair = spread(lifted[:, RANK:], pair_rows, pair_wide)
    half_pair = lifted_pair.shape[1] // 2
    query_rows = projected[:, :query_width] + matmul(lifted_query, lift_query)
    key_rows = projected[:, query_width : query_width + HEAD_DIM] + matmul(
        lifted_pair[:, :half_pair], lift_keyval[:half_pair]
    )
    value_rows = projected[:, query_width + HEAD_DIM : merged_width] + matmul(
        lifted_pair[:, half_pair:], lift_keyval[half_pair:]
    )
    start_pos = lax.axis_index("seq") * tokens
    positions = start_pos + jnp.arange(tokens, dtype=jnp.int32)
    cosine_table, sine_table = rotary_tables(positions)
    query_rot = rotate_heads(query_rows, cosine_table, sine_table).astype(BF16)
    keys_rot = rotate(key_rows, cosine_table, sine_table).astype(BF16)
    keys_all, values_all, out_full, lift_out, gate_up, lift_gate_up, down, lift_down = gather(
        [keys_rot, value_rows.astype(BF16)],
        [
            plain_shard(output_projection, output_adapter_in),
            plain_shard(output_adapter_out),
            model_shard(gate_up_weight, gate_up_adapter_in, feedforward_gain),
            plain_shard(gate_up_adapter_out),
            plain_shard(down_weight, down_adapter_in),
            plain_shard(down_adapter_out),
        ],
        1,
    )
    gain_two = gain_whole(gate_up, model_rows)
    length = keys_all.shape[0]
    valid_count = length - pad_lengths[0]
    span = min(512, length)
    bounds = jnp.stack([start_pos, valid_count])

    attended, log_norm = attention_forward(bounds, query_rot, keys_all, values_all, span)
    attended_low = heads_to_columns(attended.astype(BF16))
    out_both = matmul(attended_low, out_full)
    lifted_out = spread(out_both[:, width:].astype(BF16), rank_rows, rank_wide)
    middle = hidden + (out_both[:, :width] + matmul(lifted_out, lift_out))

    normed_two, norm_two_back = jax.vjp(rms_scale, middle, gain_two)
    second_in = spread(normed_two.astype(BF16), model_rows, model_wide)
    pre_gate = matmul(second_in, gate_up)
    lifted_gate_up = spread(pre_gate[:, 2 * FF :].astype(BF16), pair_rows, pair_wide)
    half_gate = lifted_gate_up.shape[1] // 2
    gate_part = pre_gate[:, :FF] + matmul(lifted_gate_up[:, :half_gate], lift_gate_up[:half_gate])
    upper_part = pre_gate[:, FF : 2 * FF] + matmul(
        lifted_gate_up[:, half_gate:], lift_gate_up[half_gate:]
    )
    activated, gelu_back = jax.vjp(partial(jax.nn.gelu, approximate=True), gate_part)
    inner = spread((activated * upper_part).astype(BF16), ff_rows, ff_wide)
    down_both = matmul(inner, down)
    lifted_down = spread(down_both[:, width:].astype(BF16), rank_rows, rank_wide)
    output = middle + (down_both[:, :width] + matmul(lifted_down, lift_down))

    matches = dataset_ids[:, None] == jnp.arange(DATASETS, dtype=jnp.int32)[None, :]
    picked = jnp.sum(jnp.where(matches, mixing[None, :], 0.0), axis=1)
    row_weight = jnp.where(positions < valid_count, picked, 0.0)
    scaled = cotangent.astype(F32) * row_weight[:, None]

    grad_branch = scaled.astype(BF16)
    grad_lifted_down = collect(times_transposed(grad_branch, lift_down), rank_rows, rank_wide)
    grad_down = jnp.concatenate([grad_branch, grad_lifted_down.astype(BF16)], axis=1)
    grad_inner = collect(times_transposed(grad_down, down), ff_rows, ff_wide)
    grad_gate = gelu_back(grad_inner * upper_part)[0].astype(BF16)
    grad_upper = (grad_inner * activated).astype(BF16)
    grad_gate_up = jnp.concatenate(
        [
            grad_gate,
            grad_upper,
            collect(
                times_transposed(grad_gate, lift_gate_up[:half_gate]), pair_rows, pair_wide
            ).astype(BF16),
            collect(
                times_transposed(grad_upper, lift_gate_up[half_gate:]), pair_rows, pair_wide
            ).astype(BF16),
        ],
        axis=1,
    )
    grad_normed_two = collect(times_transposed(grad_gate_up, gate_up), model_rows, model_wide)
    grad_middle_norm, gain_two_grad = norm_two_back(grad_normed_two)
    grad_middle = scaled + grad_middle_norm

    grad_attn = grad_middle.astype(BF16)
    grad_lifted_out = collect(times_transposed(grad_attn, lift_out), rank_rows, rank_wide)
    grad_out = jnp.concatenate([grad_attn, grad_lifted_out.astype(BF16)], axis=1)
    grad_attention = times_transposed(grad_out, out_full).astype(BF16)
    correction = jnp.concatenate(
        [
            jnp.sum(
                grad_attention[:, h * HEAD_DIM : (h + 1) * HEAD_DIM].astype(F32)
                * attended[h * tokens : (h + 1) * tokens],
                axis=1,
            )
            for h in range(HEADS)
        ]
    )
    grad_query_rot, kv_terms = attention_backward(
        bounds,
        query_rot,
        grad_attention,
        keys_all,
        values_all,
        log_norm.reshape(1, -1),
        correction.reshape(1, -1),
        span,
    )
    gate_up_out_term = jnp.concatenate(
        [
            transposed_times(lifted_gate_up[:, :half_gate], grad_gate, BF16),
            transposed_times(lifted_gate_up[:, half_gate:], grad_upper, BF16),
        ],
        axis=0,
    )
    kv_summed, gate_up_sum, down_sum, out_sum, gate_up_out_sum, out_out_sum, down_out_sum = scatter(
        [kv_terms],
        [
            with_gain(transposed_times(second_in, grad_gate_up, BF16), gain_two_grad, model_rows),
            transposed_times(inner, grad_down, BF16),
            transposed_times(attended_low, grad_out, BF16),
            gate_up_out_term,
            transposed_times(lifted_out, grad_attn, BF16),
            transposed_times(lifted_down, grad_branch, BF16),
        ],
        2,
    )
    grad_query_pre = rotate_heads(heads_to_columns(grad_query_rot), cosine_table, -sine_table)
    grad_keys = rotate(kv_summed[:, :HEAD_DIM], cosine_table, -sine_table)
    grad_query_low = grad_query_pre.astype(BF16)
    grad_keys_low = grad_keys.astype(BF16)
    grad_values_low = kv_summed[:, HEAD_DIM:].astype(BF16)
    grad_merged = jnp.concatenate(
        [
            grad_query_low,
            grad_keys_low,
            grad_values_low,
            collect(times_transposed(grad_query_low, lift_query), rank_rows, rank_wide).astype(BF16),
            collect(
                times_transposed(grad_keys_low, lift_keyval[:half_pair]), pair_rows, pair_wide
            ).astype(BF16),
            collect(
                times_transposed(grad_values_low, lift_keyval[half_pair:]), pair_rows, pair_wide
            ).astype(BF16),
        ],
        axis=1,
    )
    grad_normed_one = collect(times_transposed(grad_merged, merged), model_rows, model_wide)
    grad_hidden_norm, gain_one_grad = norm_one_back(grad_normed_one)
    hidden_grad = grad_middle + grad_hidden_norm

    keyval_term = jnp.concatenate(
        [
            transposed_times(lifted_pair[:, :half_pair], grad_keys_low, BF16),
            transposed_times(lifted_pair[:, half_pair:], grad_values_low, BF16),
        ],
        axis=0,
    )
    merged_sum, query_out_sum, keyval_sum = scatter(
        [],
        [
            with_gain(transposed_times(first_in, grad_merged, BF16), gain_one_grad, model_rows),
            transposed_times(lifted_query, grad_query_low, BF16),
            keyval_term,
        ],
        3,
    )
    grads = finish(
        [
            merged_sum,
            query_out_sum,
            keyval_sum,
            out_sum,
            out_out_sum,
            gate_up_sum,
            gate_up_out_sum,
            down_sum,
            down_out_sum,
        ],
        [
            (0, model_rows, 0, merged_width),
            (0, model_rows, merged_width, 3 * RANK),
            (1, rank_rows, 0, query_width),
            (2, pair_rows, 0, HEAD_DIM),
            (3, out_rows, 0, width),
            (3, out_rows, width, RANK),
            (4, rank_rows, 0, width),
            (5, model_rows, 0, 2 * FF),
            (5, model_rows, 2 * FF, 2 * RANK),
            (6, pair_rows, 0, FF),
            (7, ff_rows, 0, width),
            (7, ff_rows, width, RANK),
            (8, rank_rows, 0, width),
        ],
    )
    return (
        output.astype(BF16),
        hidden_grad.astype(BF16),
        merged_sum[model_rows, :model_rows],
        *grads[:7],
        gate_up_sum[model_rows, :model_rows],
        *grads[7:],
    )


def solution(mesh):
    rows, vector = P(AXES, None), P(AXES)
    return jax.shard_map(
        per_device,
        mesh=mesh,
        in_specs=(rows, rows, vector, P(), P("fsdp"), vector)
        + (rows,) * 7
        + (vector,)
        + (rows,) * 6,
        out_specs=(rows, rows, vector) + (rows,) * 7 + (vector,) + (rows,) * 6,
        check_vma=False,
    )
```

```python
from functools import partial

import jax
import jax.numpy as jnp
from jax import lax
from jax.experimental import pallas as pl
from jax.experimental.pallas import tpu as pltpu
from jax.sharding import PartitionSpec as P

HEADS = 4
HEAD_DIM = 256
FF = 2048
RANK = 256
DATASETS = 16
EPSILON = 1e-06
MESH = pl.DeviceIdType.MESH
VMEM_LIMIT = 60 * 1024 * 1024
AXES = ("fsdp", "seq")
BF16 = jnp.bfloat16
F32 = jnp.float32


def rms_scale(values, gain_vector):
    inverse = lax.rsqrt(jnp.mean(values * values, axis=-1, keepdims=True) + EPSILON)
    return values * inverse * gain_vector


def rotary_tables(positions):
    half_width = HEAD_DIM // 2
    inverse = 10000.0 ** (-2.0 * jnp.arange(half_width, dtype=F32) / HEAD_DIM)
    angles = positions.astype(F32)[:, None] * inverse[None, :]
    return (jnp.cos(angles), jnp.sin(angles))


def rotate(values, cosine_table, sine_table):
    half_width = values.shape[-1] // 2
    first = values[..., :half_width]
    second = values[..., half_width:]
    return jnp.concatenate(
        [first * cosine_table - second * sine_table, second * cosine_table + first * sine_table],
        axis=-1,
    )


def matmul(left_side, right_side):
    return jnp.dot(left_side, right_side, preferred_element_type=F32)


def times_transposed(left_side, right_side):
    return lax.dot_general(
        left_side, right_side, (((1,), (1,)), ((), ())), preferred_element_type=F32
    )


def transposed_times(left_side, right_side, out=F32):
    return lax.dot_general(
        left_side, right_side, (((0,), (0,)), ((), ())), preferred_element_type=F32
    ).astype(out)


def padded_rows(rows):
    return -(-rows // 8) * 8


def padded_model_rows(rows):
    return -(-(rows + 1) // 8) * 8


def selection(rows, wide, count):
    source = lax.broadcasted_iota(jnp.int32, (count * rows, count * wide), 0)
    target = lax.broadcasted_iota(jnp.int32, (count * rows, count * wide), 1)
    inside = target % wide
    return ((source == target // wide * rows + inside) & (inside < rows)).astype(BF16)


def spread(values, rows, wide):
    if wide == rows:
        return values
    return matmul(values, selection(rows, wide, values.shape[1] // rows)).astype(BF16)


def collect(values, rows, wide):
    if wide == rows:
        return values
    chosen = selection(rows, wide, values.shape[1] // wide)
    first = values.astype(BF16)
    rest = values - first.astype(F32)
    second = rest.astype(BF16)
    third = (rest - second.astype(F32)).astype(BF16)
    return (
        times_transposed(first, chosen)
        + times_transposed(second, chosen)
        + times_transposed(third, chosen)
    )


def place(groups):
    f = lax.axis_index("fsdp")
    s = lax.axis_index("seq")
    c = lax.rem(s, 2)
    y = lax.rem(s // 2, 2)
    z = s // 4
    return f, z, y, c


def device(f, z, y, c):
    return (f, (z * 2 + y) * 2 + c)


def greet(groups, both):
    f, z, y, c = place(groups)
    barrier = pltpu.get_barrier_semaphore()
    peers = [device(f, z, y, 1 - c), device(f, z, 1 - y, c)]
    if both:
        peers.append(device(1 - f, z, y, c))
    for d in range(1, groups):
        peers.append(device(f, lax.rem(z + d, groups), y, c))
    for peer in peers:
        pl.semaphore_signal(barrier, inc=1, device_id=peer, device_id_type=MESH)
    pl.semaphore_wait(barrier, len(peers))


def pieces(rows, columns, target):
    count = max(1, min(columns // 128, round(rows * columns * 2 / target)))
    edges = [round(columns // 128 * i / count) * 128 for i in range(count)] + [columns]
    return [(lo, hi - lo) for lo, hi in zip(edges[:-1], edges[1:])]


def balanced(entries, first, second):
    orders = []
    x = y = 0
    for is_rows, size in entries:
        if is_rows:
            orders.append("y")
            y += 4 * size
        elif max(x + first * size, y + second * size) <= max(x + second * size, y + first * size):
            orders.append("xy")
            x, y = x + first * size, y + second * size
        else:
            orders.append("yx")
            x, y = x + second * size, y + first * size
    return orders


def mixed(row_chunks, chunks):
    step = MIX * len(chunks) / max(1, len(row_chunks))
    keyed = [(i * step, 0, (True,) + chunk) for i, chunk in enumerate(row_chunks)]
    keyed += [(float(i), 1, (False,) + chunk) for i, chunk in enumerate(chunks)]
    return [chunk for _, _, chunk in sorted(keyed, key=lambda entry: entry[:2])]


def run_jobs(jobs, spacing):
    depth = max(len(stages) for stages in jobs)
    for tick in range(len(jobs) + spacing * (depth - 1)):
        for stage in reversed(range(depth)):
            j = tick - spacing * stage
            if 0 <= j < len(jobs) and stage < len(jobs[j]):
                jobs[j][stage]()


class Mover:
    def __init__(self, groups, send, recv, local):
        self.groups = groups
        self.send, self.recv, self.local = send, recv, local
        self.f, self.z, self.y, self.c = place(groups)
        f, z, y, c = self.f, self.z, self.y, self.c
        self.core = device(f, z, y, 1 - c)
        self.across = {"y": device(f, z, 1 - y, c), "x": device(1 - f, z, y, c)}
        self.started = []

    def along_z(self, d):
        return device(self.f, lax.rem(self.z + d, self.groups), self.y, self.c)

    def remote(self, src, dst, job, slot, peer):
        return pltpu.make_async_remote_copy(
            src_ref=src,
            dst_ref=dst,
            send_sem=self.send.at[job, slot],
            recv_sem=self.recv.at[job, slot],
            device_id=peer,
            device_id_type=MESH,
        )

    def start(self, src, dst, job, slot, peer):
        copy = self.remote(src, dst, job, slot, peer)
        copy.start()
        self.started.append(copy)

    def arrived(self, ref, job, slot):
        self.remote(ref, ref, job, slot, self.core).wait_recv()

    def drain(self):
        for copy in self.started:
            copy.wait_send()


def gather_job(m, job, order, source, whole, lo, width):
    groups, f, z, y, c = m.groups, m.f, m.z, m.y, m.c
    columns = slice(lo, lo + width)
    own = source.at[:, columns]

    def at(*index):
        return whole.at[index + (slice(None), columns)]

    every = slice(None)

    def begin():
        pltpu.make_async_copy(own, at(f, z, y, c), m.local.at[job]).start()
        for d in range(1, groups):
            m.start(own, at(f, z, y, c), job, d, m.along_z(d))

    def first():
        pltpu.make_async_copy(own, at(f, z, y, c), m.local.at[job]).wait()
        for d in range(1, groups):
            m.arrived(at(f, lax.rem(z + groups - d, groups), y, c), job, d)
        mine = at(f, every, y, c)
        m.start(mine, mine, job, 0, m.across[order[0]])
        m.start(mine, mine, job, groups, m.core)

    def second():
        if order == "yx":
            got, mine = at(f, every, 1 - y, c), at(f, every, every, c)
        else:
            got, mine = at(1 - f, every, y, c), at(every, every, y, c)
        m.arrived(got, job, 0)
        m.start(mine, mine, job, groups + 1, m.across[order[1]])
        m.start(got, got, job, groups + 2, m.core)

    def third():
        got = at(1 - f, every, every, c) if order == "yx" else at(every, every, 1 - y, c)
        m.arrived(got, job, groups + 1)
        m.start(got, got, job, groups + 3, m.core)

    def last():
        other = 1 - c
        m.arrived(at(f, every, y, other), job, groups)
        if order == "yx":
            m.arrived(at(f, every, 1 - y, other), job, groups + 2)
            m.arrived(at(1 - f, every, every, other), job, groups + 3)
        else:
            m.arrived(at(1 - f, every, y, other), job, groups + 2)
            m.arrived(at(every, every, 1 - y, other), job, groups + 3)

    return [begin, first, second, third, last]


def gather_rows_job(m, job, source, whole, lo, width):
    groups, z, y, c = m.groups, m.z, m.y, m.c
    columns = slice(lo, lo + width)
    own = source.at[:, columns]
    every = slice(None)

    def at(*index):
        return whole.at[index + (slice(None), columns)]

    def begin():
        pltpu.make_async_copy(own, at(z, y, c), m.local.at[job]).start()
        for d in range(1, groups):
            m.start(own, at(z, y, c), job, d, m.along_z(d))

    def first():
        pltpu.make_async_copy(own, at(z, y, c), m.local.at[job]).wait()
        for d in range(1, groups):
            m.arrived(at(lax.rem(z + groups - d, groups), y, c), job, d)
        mine = at(every, y, c)
        m.start(mine, mine, job, 0, m.across["y"])
        m.start(mine, mine, job, groups, m.core)

    def second():
        got = at(every, 1 - y, c)
        m.arrived(got, job, 0)
        m.start(got, got, job, groups + 1, m.core)

    def last():
        m.arrived(at(every, y, 1 - c), job, groups)
        m.arrived(at(every, 1 - y, 1 - c), job, groups + 1)

    return [begin, first, second, last]


MIX = 0.6
GATHER_BYTES = 20 * 1024
ROWS_BYTES = 32 * 1024
GATHER_SPACING = 4
SCATTER_BYTES = 20 * 1024
SCATTER_SPACING = 4


def plan_of(row_blocks, blocks, target, first, second):
    row_cuts = [
        (a, lo, width)
        for a, (rows, columns) in enumerate(row_blocks)
        for lo, width in pieces(rows, columns, ROWS_BYTES)
    ]
    cuts = [
        (a, lo, width)
        for a, (rows, columns) in enumerate(blocks)
        for lo, width in pieces(rows, columns, target)
    ]
    chunks = mixed(row_cuts, cuts)
    entries = [
        (is_rows, (row_blocks if is_rows else blocks)[a][0] * width) for is_rows, a, _, width in chunks
    ]
    orders = balanced(entries, first, second)
    return tuple(chunk + (order,) for chunk, order in zip(chunks, orders))


def gather_kernel(groups, plan, rows_count, count, *refs):
    ins, outs = refs[:count], refs[count : 2 * count]
    send, recv, local = refs[2 * count :]
    greet(groups, True)
    m = Mover(groups, send, recv, local)
    jobs = []
    for is_rows, a, lo, width, order in plan:
        if is_rows:
            jobs.append(gather_rows_job(m, len(jobs), ins[a], outs[a], lo, width))
        else:
            b = rows_count + a
            jobs.append(gather_job(m, len(jobs), order, ins[b], outs[b], lo, width))
    run_jobs(jobs, GATHER_SPACING)
    m.drain()


def gather(token_rows, shards, identity):
    n_f, n_s = lax.axis_size("fsdp"), lax.axis_size("seq")
    groups = n_s // 4
    operands = list(token_rows) + list(shards)
    plan = plan_of(
        [block.shape for block in token_rows], [shard.shape for shard in shards], GATHER_BYTES, 4, 8
    )
    results = pl.pallas_call(
        partial(gather_kernel, groups, plan, len(token_rows), len(operands)),
        out_shape=[
            jax.ShapeDtypeStruct((groups, 2, 2) + block.shape, block.dtype) for block in token_rows
        ]
        + [
            jax.ShapeDtypeStruct((n_f, groups, 2, 2) + shard.shape, shard.dtype)
            for shard in shards
        ],
        in_specs=[pl.BlockSpec(memory_space=pltpu.VMEM)] * len(operands),
        out_specs=[pl.BlockSpec(memory_space=pltpu.HBM)] * len(operands),
        scratch_shapes=[
            pltpu.SemaphoreType.DMA((len(plan), groups + 4)),
            pltpu.SemaphoreType.DMA((len(plan), groups + 4)),
            pltpu.SemaphoreType.DMA((len(plan),)),
        ],
        compiler_params=pltpu.CompilerParams(
            collective_id=identity, has_side_effects=True, vmem_limit_bytes=VMEM_LIMIT
        ),
        name=f"gather_{identity}",
    )(*operands)
    return [whole.reshape(-1, block.shape[1]) for whole, block in zip(results, operands)]


def scatter_job(m, job, order, source, out, lo, width, buffers):
    groups, f, z, y, c = m.groups, m.f, m.z, m.y, m.c
    columns = slice(lo, lo + width)
    every = slice(None)
    held, from_core, from_first, from_second, from_z = buffers

    def half(core):
        return source.at[:, :, :, core, :, columns]

    def add(into, other):
        into[...] = into[...] + other[...]

    def each(step):
        def part(g, carry):
            step(g)
            return carry

        lax.fori_loop(0, groups, part, 0)

    def begin():
        m.start(half(1 - c), from_core, job, 0, m.core)
        pltpu.make_async_copy(half(c), held, m.local.at[job]).start()

    def first():
        pltpu.make_async_copy(half(c), held, m.local.at[job]).wait()
        m.arrived(from_core, job, 0)
        if order == "xy":
            def pair(side):
                def step(g):
                    for k in range(2):
                        add(held.at[side, g, k], from_core.at[side, g, k])
                return step

            each(pair(1 - f))
            m.start(held.at[1 - f], from_first, job, 1, m.across["x"])
            each(pair(f))
        else:
            def pair(side):
                def step(g):
                    for k in range(2):
                        add(held.at[k, g, side], from_core.at[k, g, side])
                return step

            each(pair(1 - y))
            m.start(held.at[:, :, 1 - y], from_first, job, 1, m.across["y"])
            each(pair(y))

    def second():
        m.arrived(from_first, job, 1)
        if order == "xy":
            def side(k):
                return lambda g: add(held.at[f, g, k], from_first.at[g, k])

            each(side(1 - y))
            m.start(held.at[f, :, 1 - y], from_second, job, 2, m.across["y"])
            each(side(y))
        else:
            def side(k):
                return lambda g: add(held.at[k, g, y], from_first.at[k, g])

            each(side(1 - f))
            m.start(held.at[1 - f, :, y], from_second, job, 2, m.across["x"])
            each(side(f))

    def third():
        m.arrived(from_second, job, 2)
        each(lambda g: add(held.at[f, g, y], from_second.at[g]))
        for d in range(1, groups):
            there = lax.rem(z + d, groups)
            m.start(held.at[f, there, y], from_z.at[d - 1], job, 2 + d, m.along_z(d))

    def last():
        total = held[f, z, y].astype(F32)
        for d in range(1, groups):
            m.arrived(from_z.at[d - 1], job, 2 + d)
            total = total + from_z[d - 1].astype(F32)
        out[:, columns] = total

    return [begin, first, second, third, last]


def scatter_rows_job(m, job, source, out, lo, width, buffers):
    groups, z, y, c = m.groups, m.z, m.y, m.c
    columns = slice(lo, lo + width)
    held, from_core, from_y, from_z = buffers

    def half(core):
        return source.at[:, :, core, :, columns]

    def add(into, other):
        into[...] = into[...] + other[...]

    def each(step):
        def part(g, carry):
            step(g)
            return carry

        lax.fori_loop(0, groups, part, 0)

    def begin():
        m.start(half(1 - c), from_core, job, 0, m.core)
        pltpu.make_async_copy(half(c), held, m.local.at[job]).start()

    def first():
        pltpu.make_async_copy(half(c), held, m.local.at[job]).wait()
        m.arrived(from_core, job, 0)
        each(lambda g: add(held.at[g, 1 - y], from_core.at[g, 1 - y]))
        m.start(held.at[:, 1 - y], from_y, job, 1, m.across["y"])
        each(lambda g: add(held.at[g, y], from_core.at[g, y]))

    def second():
        m.arrived(from_y, job, 1)
        each(lambda g: add(held.at[g, y], from_y.at[g]))
        for d in range(1, groups):
            there = lax.rem(z + d, groups)
            m.start(held.at[there, y], from_z.at[d - 1], job, 2 + d, m.along_z(d))

    def last():
        total = held[z, y].astype(F32)
        for d in range(1, groups):
            m.arrived(from_z.at[d - 1], job, 2 + d)
            total = total + from_z[d - 1].astype(F32)
        out[:, columns] = total

    return [begin, first, second, last]


def scatter_kernel(groups, plan, rows_count, count, *refs):
    ins, outs = refs[:count], refs[count : 2 * count]
    send, recv, local = refs[2 * count : 2 * count + 3]
    scratch = list(refs[2 * count + 3 :])
    greet(groups, True)
    m = Mover(groups, send, recv, local)
    jobs = []
    for is_rows, a, lo, width, order in plan:
        if is_rows:
            buffers, scratch = scratch[:4], scratch[4:]
            jobs.append(scatter_rows_job(m, len(jobs), ins[a], outs[a], lo, width, buffers))
        else:
            buffers, scratch = scratch[:5], scratch[5:]
            b = rows_count + a
            jobs.append(scatter_job(m, len(jobs), order, ins[b], outs[b], lo, width, buffers))
    run_jobs(jobs, SCATTER_SPACING)
    m.drain()


def scatter(token_rows, partials, identity):
    n_f, n_s = lax.axis_size("fsdp"), lax.axis_size("seq")
    groups = n_s // 4
    row_blocks = [(p.shape[0] // n_s, p.shape[1]) for p in token_rows]
    blocks = [(p.shape[0] // (n_f * n_s), p.shape[1]) for p in partials]
    plan = plan_of(row_blocks, blocks, SCATTER_BYTES, 8, 4)
    scratch = []
    for is_rows, a, _, width, order in plan:
        if is_rows:
            block = (row_blocks[a][0], width)
            scratch += [
                pltpu.VMEM((groups, 2) + block, BF16),
                pltpu.VMEM((groups, 2) + block, BF16),
                pltpu.VMEM((groups,) + block, BF16),
                pltpu.VMEM((groups - 1,) + block, BF16),
            ]
        else:
            block = (blocks[a][0], width)
            scratch += [
                pltpu.VMEM((n_f, groups, 2) + block, BF16),
                pltpu.VMEM((n_f, groups, 2) + block, BF16),
                pltpu.VMEM(((groups, 2) if order == "xy" else (n_f, groups)) + block, BF16),
                pltpu.VMEM((groups,) + block, BF16),
                pltpu.VMEM((groups - 1,) + block, BF16),
            ]
    count = len(row_blocks) + len(blocks)
    return pl.pallas_call(
        partial(scatter_kernel, groups, plan, len(row_blocks), count),
        out_shape=[jax.ShapeDtypeStruct(b, F32) for b in row_blocks + blocks],
        in_specs=[pl.BlockSpec(memory_space=pltpu.HBM)] * count,
        out_specs=[pl.BlockSpec(memory_space=pltpu.VMEM)] * count,
        scratch_shapes=[
            pltpu.SemaphoreType.DMA((len(plan), groups + 2)),
            pltpu.SemaphoreType.DMA((len(plan), groups + 2)),
            pltpu.SemaphoreType.DMA((len(plan),)),
        ]
        + scratch,
        compiler_params=pltpu.CompilerParams(
            collective_id=identity, has_side_effects=True, vmem_limit_bytes=VMEM_LIMIT
        ),
        name=f"scatter_{identity}",
    )(
        *[p.reshape((groups, 2, 2) + b) for p, b in zip(token_rows, row_blocks)],
        *[p.reshape((n_f, groups, 2, 2) + b) for p, b in zip(partials, blocks)],
    )


def finish_kernel(cuts, count, *refs):
    total = len(cuts)
    ins, outs = refs[:count], refs[count : count + total]
    staged, sems = refs[count + total : count + 2 * total], refs[count + 2 * total]
    for i, (a, rows, lo, width) in enumerate(cuts):
        staged[i][...] = ins[a][0:rows, lo : lo + width]
    for i in range(total):
        pltpu.make_async_copy(staged[i], outs[i], sems.at[i]).start()
    for i in range(total):
        pltpu.make_async_copy(staged[i], outs[i], sems.at[i]).wait()


def finish(sums, cuts):
    shapes = [(rows, width) for _, rows, _, width in cuts]
    return pl.pallas_call(
        partial(finish_kernel, tuple(cuts), len(sums)),
        out_shape=[jax.ShapeDtypeStruct(shape, F32) for shape in shapes],
        in_specs=[pl.BlockSpec(memory_space=pltpu.VMEM)] * len(sums),
        out_specs=[pl.BlockSpec(memory_space=pltpu.HBM)] * len(cuts),
        scratch_shapes=[pltpu.VMEM(shape, F32) for shape in shapes]
        + [pltpu.SemaphoreType.DMA((len(cuts),))],
        compiler_params=pltpu.CompilerParams(vmem_limit_bytes=VMEM_LIMIT),
        name="finish",
    )(*sums)


def as_row(column):
    return jnp.transpose(jnp.broadcast_to(column, (column.shape[0], 128)))[0:1, :]


def forward_kernel(
    span, bounds, query_ref, cosine, sine, key_ref, value_ref, out_ref, low_ref, norm_ref, stacked, peak, total
):
    tokens = query_ref.shape[0]
    rows = tokens * HEADS
    half = HEAD_DIM // 2
    scale = HEAD_DIM ** (-0.5)
    start, valid = bounds[0], bounds[1]
    for h in range(HEADS):
        first = query_ref[:, h * HEAD_DIM : h * HEAD_DIM + half]
        second = query_ref[:, h * HEAD_DIM + half : (h + 1) * HEAD_DIM]
        at = slice(h * tokens, (h + 1) * tokens)
        stacked[at, :half] = (first * cosine[...] - second * sine[...]).astype(BF16)
        stacked[at, half:] = (second * cosine[...] + first * sine[...]).astype(BF16)
    peak[...] = jnp.full(peak.shape, -jnp.inf, F32)
    total[...] = jnp.zeros(total.shape, F32)
    out_ref[...] = jnp.zeros(out_ref.shape, F32)

    def block(j, masked):
        at = pl.multiple_of(j * span, span)

        def head(h, carry):
            own = pl.ds(pl.multiple_of(h * tokens, tokens), tokens)
            raw = times_transposed(stacked[own, :], key_ref[pl.ds(at, span), :]) * scale
            if masked:
                key_pos = at + lax.broadcasted_iota(jnp.int32, (tokens, span), 1)
                row_pos = start + lax.broadcasted_iota(jnp.int32, (tokens, span), 0)
                raw = jnp.where(key_pos <= jnp.minimum(row_pos, valid - 1), raw, -jnp.inf)
            old = peak[own, :]
            new = jnp.maximum(old, jnp.max(raw, axis=1, keepdims=True))
            shrink = jnp.exp(old - new)
            weights = jnp.exp(raw - new)
            total[own, :] = total[own, :] * shrink + jnp.sum(weights, axis=1, keepdims=True)
            out_ref[own, :] = out_ref[own, :] * shrink + matmul(
                weights.astype(BF16), value_ref[pl.ds(at, span), :]
            )
            peak[own, :] = new
            return carry

        lax.fori_loop(0, HEADS, head, 0)

    plain = jnp.minimum(start, valid) // span
    last = jnp.minimum(start + tokens, valid)
    every = (last + span - 1) // span

    def free(j, carry):
        block(j, False)
        return carry

    def edge(j, carry):
        block(j, True)
        return carry

    lax.fori_loop(0, plain, free, 0)
    lax.fori_loop(plain, every, edge, 0)
    for h in range(HEADS):
        at = slice(h * tokens, (h + 1) * tokens)
        result = out_ref[at, :] / total[at, :]
        out_ref[at, :] = result
        low_ref[:, h * HEAD_DIM : (h + 1) * HEAD_DIM] = result.astype(BF16)
        norm_ref[0:1, at] = as_row(peak[at, :] + jnp.log(total[at, :]))


def attention_forward(bounds, query, cosine, sine, keys, values, span):
    tokens = query.shape[0]
    rows = tokens * HEADS
    return pl.pallas_call(
        partial(forward_kernel, span),
        out_shape=[
            jax.ShapeDtypeStruct((rows, HEAD_DIM), F32),
            jax.ShapeDtypeStruct((tokens, HEADS * HEAD_DIM), BF16),
            jax.ShapeDtypeStruct((1, rows), F32),
            jax.ShapeDtypeStruct((rows, HEAD_DIM), BF16),
        ],
        in_specs=[pl.BlockSpec(memory_space=pltpu.SMEM)]
        + [pl.BlockSpec(memory_space=pltpu.VMEM)] * 5,
        out_specs=[pl.BlockSpec(memory_space=pltpu.VMEM)] * 4,
        scratch_shapes=[
            pltpu.VMEM((rows, 1), F32),
            pltpu.VMEM((rows, 1), F32),
        ],
        compiler_params=pltpu.CompilerParams(vmem_limit_bytes=VMEM_LIMIT),
        name="attention_forward",
    )(bounds, query, cosine, sine, keys, values)


def backward_kernel(
    span,
    bounds,
    stacked,
    grad_ref,
    attended,
    cosine,
    sine,
    key_ref,
    value_ref,
    norm_ref,
    gq_ref,
    gkv_ref,
    grads,
    gathered,
    delta,
    sums,
):
    tokens = grad_ref.shape[0]
    half = HEAD_DIM // 2
    scale = HEAD_DIM ** (-0.5)
    start, valid = bounds[0], bounds[1]
    for h in range(HEADS):
        at = slice(h * tokens, (h + 1) * tokens)
        part = grad_ref[:, h * HEAD_DIM : (h + 1) * HEAD_DIM]
        grads[at, :] = part
        delta[0:1, at] = as_row(
            jnp.sum(part.astype(F32) * attended[at, :], axis=1, keepdims=True)
        )
    gathered[...] = jnp.zeros(gathered.shape, F32)

    def block(j, masked):
        at = pl.multiple_of(j * span, span)
        here = pl.ds(at, span)
        sums[...] = jnp.zeros(sums.shape, F32)

        def head(h, carry):
            low = pl.multiple_of(h * tokens, tokens)
            own = pl.ds(low, tokens)
            raw = times_transposed(key_ref[here, :], stacked[own, :]) * scale
            soft = jnp.exp(raw - norm_ref[:, own])
            if masked:
                key_pos = at + lax.broadcasted_iota(jnp.int32, (span, tokens), 0)
                row_pos = start + lax.broadcasted_iota(jnp.int32, (span, tokens), 1)
                soft = jnp.where(key_pos <= jnp.minimum(row_pos, valid - 1), soft, 0.0)
            toward = times_transposed(value_ref[here, :], grads[own, :])
            pulled = (soft * (toward - delta[:, own])).astype(BF16)
            sums[:, HEAD_DIM:] += matmul(soft.astype(BF16), grads[own, :])
            sums[:, :HEAD_DIM] += matmul(pulled, stacked[own, :])
            gathered[own, :] += transposed_times(pulled, key_ref[here, :])
            return carry

        lax.fori_loop(0, HEADS, head, 0)
        gkv_ref[here, HEAD_DIM:] = sums[:, HEAD_DIM:].astype(BF16)
        gkv_ref[here, :HEAD_DIM] = (sums[:, :HEAD_DIM] * scale).astype(BF16)

    plain = jnp.minimum(start, valid) // span
    last = jnp.minimum(start + tokens, valid)
    every = jnp.where(start < valid, (last + span - 1) // span, 0)
    plain = jnp.minimum(plain, every)

    def free(j, carry):
        block(j, False)
        return carry

    def edge(j, carry):
        block(j, True)
        return carry

    def empty(j, carry):
        at = pl.multiple_of(j * span, span)
        gkv_ref[pl.ds(at, span), :] = jnp.zeros((span, 2 * HEAD_DIM), BF16)
        return carry

    lax.fori_loop(0, plain, free, 0)
    lax.fori_loop(plain, every, edge, 0)
    lax.fori_loop(every, key_ref.shape[0] // span, empty, 0)
    for h in range(HEADS):
        at = slice(h * tokens, (h + 1) * tokens)
        first = gathered[at, :half] * scale
        second = gathered[at, half:] * scale
        lo = h * HEAD_DIM
        gq_ref[:, lo : lo + half] = (first * cosine[...] + second * sine[...]).astype(BF16)
        gq_ref[:, lo + half : lo + HEAD_DIM] = (second * cosine[...] - first * sine[...]).astype(BF16)


def attention_backward(bounds, stacked, grad, attended, cosine, sine, keys, values, norm, span):
    tokens = grad.shape[0]
    rows = tokens * HEADS
    return pl.pallas_call(
        partial(backward_kernel, span),
        out_shape=[
            jax.ShapeDtypeStruct((tokens, HEADS * HEAD_DIM), BF16),
            jax.ShapeDtypeStruct((keys.shape[0], 2 * HEAD_DIM), BF16),
        ],
        in_specs=[pl.BlockSpec(memory_space=pltpu.SMEM)]
        + [pl.BlockSpec(memory_space=pltpu.VMEM)] * 8,
        out_specs=[pl.BlockSpec(memory_space=pltpu.VMEM)] * 2,
        scratch_shapes=[
            pltpu.VMEM((rows, HEAD_DIM), BF16),
            pltpu.VMEM((rows, HEAD_DIM), F32),
            pltpu.VMEM((1, rows), F32),
            pltpu.VMEM((span, 2 * HEAD_DIM), F32),
        ],
        compiler_params=pltpu.CompilerParams(vmem_limit_bytes=VMEM_LIMIT),
        name="attention_backward",
    )(bounds, stacked, grad, attended, cosine, sine, keys, values, norm)


def pack_kernel(cuts, gains, count, *refs):
    ins, gain_refs = refs[:count], refs[count : count + len(gains)]
    outs = refs[count + len(gains) :]
    for out in outs:
        out[...] = jnp.zeros(out.shape, BF16)
    for source, (target, lo) in zip(ins, cuts):
        outs[target][0 : source.shape[0], lo : lo + source.shape[1]] = source[...]
    for gain, target in zip(gain_refs, gains):
        rows = gain.shape[1]
        outs[target][rows : rows + 1, 0:rows] = gain[...]


def pack(groups_of_weights, gains, gain_targets):
    weights, cuts, shapes = [], [], []
    for target, (wide, members) in enumerate(groups_of_weights):
        lo = 0
        for member in members:
            weights.append(member)
            cuts.append((target, lo))
            lo += member.shape[1]
        shapes.append((wide, lo))
    return pl.pallas_call(
        partial(pack_kernel, tuple(cuts), tuple(gain_targets), len(weights)),
        out_shape=[jax.ShapeDtypeStruct(shape, BF16) for shape in shapes],
        in_specs=[pl.BlockSpec(memory_space=pltpu.VMEM)] * (len(weights) + len(gains)),
        out_specs=[pl.BlockSpec(memory_space=pltpu.VMEM)] * len(shapes),
        compiler_params=pltpu.CompilerParams(vmem_limit_bytes=VMEM_LIMIT),
        name="pack",
    )(*weights, *[gain[None] for gain in gains])


def gain_whole(gathered, rows):
    wide = padded_model_rows(rows)
    return gathered.reshape(-1, wide, gathered.shape[1])[:, rows, :rows].reshape(-1).astype(F32)


def with_gain(partial_sums, gain_grad, rows):
    wide = padded_model_rows(rows)
    blocks = partial_sums.reshape(-1, wide, partial_sums.shape[1])
    return blocks.at[:, rows, :rows].set(gain_grad.reshape(-1, rows).astype(BF16)).reshape(partial_sums.shape)


def per_device(
    hidden_in,
    cotangent,
    dataset_ids,
    mixing,
    pad_lengths,
    attention_gain,
    merged_projection,
    merged_adapter_in,
    query_adapter_out,
    keyval_adapter_out,
    output_projection,
    output_adapter_in,
    output_adapter_out,
    feedforward_gain,
    gate_up_weight,
    gate_up_adapter_in,
    gate_up_adapter_out,
    down_weight,
    down_adapter_in,
    down_adapter_out,
):
    tokens, width = hidden_in.shape
    query_width = HEADS * HEAD_DIM
    merged_width = query_width + 2 * HEAD_DIM
    model_rows = merged_projection.shape[0]
    rank_rows = query_adapter_out.shape[0]
    pair_rows = keyval_adapter_out.shape[0]
    out_rows = output_projection.shape[0]
    ff_rows = down_weight.shape[0]
    model_wide, rank_wide = padded_model_rows(model_rows), padded_rows(rank_rows)
    pair_wide, ff_wide = padded_rows(pair_rows), padded_rows(ff_rows)

    packed = pack(
        [
            (model_wide, [merged_projection, merged_adapter_in]),
            (model_wide, [gate_up_weight, gate_up_adapter_in]),
            (rank_wide, [query_adapter_out]),
            (pair_wide, [keyval_adapter_out]),
            (padded_rows(out_rows), [output_projection, output_adapter_in]),
            (rank_wide, [output_adapter_out]),
            (pair_wide, [gate_up_adapter_out]),
            (ff_wide, [down_weight, down_adapter_in]),
            (rank_wide, [down_adapter_out]),
        ],
        [attention_gain, feedforward_gain],
        [0, 1],
    )
    merged, lift_query, lift_keyval = gather([], [packed[0], packed[2], packed[3]], 0)
    gain_one = gain_whole(merged, model_rows)

    hidden = hidden_in.astype(F32)
    normed_one, norm_one_back = jax.vjp(rms_scale, hidden, gain_one)
    first_in = spread(normed_one.astype(BF16), model_rows, model_wide)
    projected = matmul(first_in, merged)
    lifted = projected[:, merged_width:].astype(BF16)
    lifted_query = spread(lifted[:, :RANK], rank_rows, rank_wide)
    lifted_pair = spread(lifted[:, RANK:], pair_rows, pair_wide)
    half_pair = lifted_pair.shape[1] // 2
    query_rows = projected[:, :query_width] + matmul(lifted_query, lift_query)
    key_rows = projected[:, query_width : query_width + HEAD_DIM] + matmul(
        lifted_pair[:, :half_pair], lift_keyval[:half_pair]
    )
    value_rows = projected[:, query_width + HEAD_DIM : merged_width] + matmul(
        lifted_pair[:, half_pair:], lift_keyval[half_pair:]
    )
    start_pos = lax.axis_index("seq") * tokens
    positions = start_pos + jnp.arange(tokens, dtype=jnp.int32)
    cosine_table, sine_table = rotary_tables(positions)
    keys_rot = rotate(key_rows, cosine_table, sine_table).astype(BF16)
    keys_all, values_all, out_full, lift_out, gate_up, lift_gate_up, down, lift_down = gather(
        [keys_rot, value_rows.astype(BF16)],
        [packed[4], packed[5], packed[1], packed[6], packed[7], packed[8]],
        1,
    )
    gain_two = gain_whole(gate_up, model_rows)
    length = keys_all.shape[0]
    valid_count = length - pad_lengths[0]
    span = min(1024, length)
    bounds = jnp.stack([start_pos, valid_count])

    attended, attended_low, log_norm, query_rot = attention_forward(
        bounds, query_rows, cosine_table, sine_table, keys_all, values_all, span
    )
    out_both = matmul(attended_low, out_full)
    lifted_out = spread(out_both[:, width:].astype(BF16), rank_rows, rank_wide)
    middle = hidden + (out_both[:, :width] + matmul(lifted_out, lift_out))

    normed_two, norm_two_back = jax.vjp(rms_scale, middle, gain_two)
    second_in = spread(normed_two.astype(BF16), model_rows, model_wide)
    pre_gate = matmul(second_in, gate_up)
    lifted_gate_up = spread(pre_gate[:, 2 * FF :].astype(BF16), pair_rows, pair_wide)
    half_gate = lifted_gate_up.shape[1] // 2
    gate_part = pre_gate[:, :FF] + matmul(lifted_gate_up[:, :half_gate], lift_gate_up[:half_gate])
    upper_part = pre_gate[:, FF : 2 * FF] + matmul(
        lifted_gate_up[:, half_gate:], lift_gate_up[half_gate:]
    )
    activated, gelu_back = jax.vjp(partial(jax.nn.gelu, approximate=True), gate_part)
    inner = spread((activated * upper_part).astype(BF16), ff_rows, ff_wide)
    down_both = matmul(inner, down)
    lifted_down = spread(down_both[:, width:].astype(BF16), rank_rows, rank_wide)
    output = middle + (down_both[:, :width] + matmul(lifted_down, lift_down))

    matches = dataset_ids[:, None] == jnp.arange(DATASETS, dtype=jnp.int32)[None, :]
    picked = jnp.sum(jnp.where(matches, mixing[None, :], 0.0), axis=1)
    row_weight = jnp.where(positions < valid_count, picked, 0.0)
    scaled = cotangent.astype(F32) * row_weight[:, None]

    grad_branch = scaled.astype(BF16)
    grad_lifted_down = collect(times_transposed(grad_branch, lift_down), rank_rows, rank_wide)
    grad_down = jnp.concatenate([grad_branch, grad_lifted_down.astype(BF16)], axis=1)
    grad_inner = collect(times_transposed(grad_down, down), ff_rows, ff_wide)
    grad_gate = gelu_back(grad_inner * upper_part)[0].astype(BF16)
    grad_upper = (grad_inner * activated).astype(BF16)
    grad_gate_up = jnp.concatenate(
        [
            grad_gate,
            grad_upper,
            collect(
                times_transposed(grad_gate, lift_gate_up[:half_gate]), pair_rows, pair_wide
            ).astype(BF16),
            collect(
                times_transposed(grad_upper, lift_gate_up[half_gate:]), pair_rows, pair_wide
            ).astype(BF16),
        ],
        axis=1,
    )
    grad_normed_two = collect(times_transposed(grad_gate_up, gate_up), model_rows, model_wide)
    grad_middle_norm, gain_two_grad = norm_two_back(grad_normed_two)
    grad_middle = scaled + grad_middle_norm

    grad_attn = grad_middle.astype(BF16)
    grad_lifted_out = collect(times_transposed(grad_attn, lift_out), rank_rows, rank_wide)
    grad_out = jnp.concatenate([grad_attn, grad_lifted_out.astype(BF16)], axis=1)
    grad_attention = times_transposed(grad_out, out_full).astype(BF16)
    grad_query_low, kv_terms = attention_backward(
        bounds,
        query_rot,
        grad_attention,
        attended,
        cosine_table,
        sine_table,
        keys_all,
        values_all,
        log_norm,
        span,
    )
    gate_up_out_term = jnp.concatenate(
        [
            transposed_times(lifted_gate_up[:, :half_gate], grad_gate, BF16),
            transposed_times(lifted_gate_up[:, half_gate:], grad_upper, BF16),
        ],
        axis=0,
    )
    kv_summed, gate_up_sum, down_sum, out_sum, gate_up_out_sum, out_out_sum, down_out_sum = scatter(
        [kv_terms],
        [
            with_gain(transposed_times(second_in, grad_gate_up, BF16), gain_two_grad, model_rows),
            transposed_times(inner, grad_down, BF16),
            transposed_times(attended_low, grad_out, BF16),
            gate_up_out_term,
            transposed_times(lifted_out, grad_attn, BF16),
            transposed_times(lifted_down, grad_branch, BF16),
        ],
        2,
    )
    grad_keys = rotate(kv_summed[:, :HEAD_DIM], cosine_table, -sine_table)
    grad_keys_low = grad_keys.astype(BF16)
    grad_values_low = kv_summed[:, HEAD_DIM:].astype(BF16)
    grad_merged = jnp.concatenate(
        [
            grad_query_low,
            grad_keys_low,
            grad_values_low,
            collect(times_transposed(grad_query_low, lift_query), rank_rows, rank_wide).astype(BF16),
            collect(
                times_transposed(grad_keys_low, lift_keyval[:half_pair]), pair_rows, pair_wide
            ).astype(BF16),
            collect(
                times_transposed(grad_values_low, lift_keyval[half_pair:]), pair_rows, pair_wide
            ).astype(BF16),
        ],
        axis=1,
    )
    grad_normed_one = collect(times_transposed(grad_merged, merged), model_rows, model_wide)
    grad_hidden_norm, gain_one_grad = norm_one_back(grad_normed_one)
    hidden_grad = grad_middle + grad_hidden_norm

    keyval_term = jnp.concatenate(
        [
            transposed_times(lifted_pair[:, :half_pair], grad_keys_low, BF16),
            transposed_times(lifted_pair[:, half_pair:], grad_values_low, BF16),
        ],
        axis=0,
    )
    merged_sum, query_out_sum, keyval_sum = scatter(
        [],
        [
            with_gain(transposed_times(first_in, grad_merged, BF16), gain_one_grad, model_rows),
            transposed_times(lifted_query, grad_query_low, BF16),
            keyval_term,
        ],
        3,
    )
    grads = finish(
        [
            merged_sum,
            query_out_sum,
            keyval_sum,
            out_sum,
            out_out_sum,
            gate_up_sum,
            gate_up_out_sum,
            down_sum,
            down_out_sum,
        ],
        [
            (0, model_rows, 0, merged_width),
            (0, model_rows, merged_width, 3 * RANK),
            (1, rank_rows, 0, query_width),
            (2, pair_rows, 0, HEAD_DIM),
            (3, out_rows, 0, width),
            (3, out_rows, width, RANK),
            (4, rank_rows, 0, width),
            (5, model_rows, 0, 2 * FF),
            (5, model_rows, 2 * FF, 2 * RANK),
            (6, pair_rows, 0, FF),
            (7, ff_rows, 0, width),
            (7, ff_rows, width, RANK),
            (8, rank_rows, 0, width),
        ],
    )
    return (
        output.astype(BF16),
        hidden_grad.astype(BF16),
        merged_sum[model_rows, :model_rows],
        *grads[:7],
        gate_up_sum[model_rows, :model_rows],
        *grads[7:],
    )


def solution(mesh):
    rows, vector = P(AXES, None), P(AXES)
    return jax.shard_map(
        per_device,
        mesh=mesh,
        in_specs=(rows, rows, vector, P(), P("fsdp"), vector)
        + (rows,) * 7
        + (vector,)
        + (rows,) * 6,
        out_specs=(rows, rows, vector) + (rows,) * 7 + (vector,) + (rows,) * 6,
        check_vma=False,
    )
```

```python
from functools import partial

import jax
import jax.numpy as jnp
from jax import lax
from jax.experimental import pallas as pl
from jax.experimental.pallas import tpu as pltpu
from jax.sharding import PartitionSpec as P

HEADS = 4
HEAD_DIM = 256
FF = 2048
RANK = 256
DATASETS = 16
EPSILON = 1e-06
MESH = pl.DeviceIdType.MESH
VMEM_LIMIT = 60 * 1024 * 1024
AXES = ("fsdp", "seq")
BF16 = jnp.bfloat16
F32 = jnp.float32


def rms_scale(values, gain_vector):
    inverse = lax.rsqrt(jnp.mean(values * values, axis=-1, keepdims=True) + EPSILON)
    return values * inverse * gain_vector


def rotary_tables(positions):
    half_width = HEAD_DIM // 2
    inverse = 10000.0 ** (-2.0 * jnp.arange(half_width, dtype=F32) / HEAD_DIM)
    angles = positions.astype(F32)[:, None] * inverse[None, :]
    return (jnp.cos(angles), jnp.sin(angles))


def rotate(values, cosine_table, sine_table):
    half_width = values.shape[-1] // 2
    first = values[..., :half_width]
    second = values[..., half_width:]
    return jnp.concatenate(
        [first * cosine_table - second * sine_table, second * cosine_table + first * sine_table],
        axis=-1,
    )


def matmul(left_side, right_side):
    return jnp.dot(left_side, right_side, preferred_element_type=F32)


def times_transposed(left_side, right_side):
    return lax.dot_general(
        left_side, right_side, (((1,), (1,)), ((), ())), preferred_element_type=F32
    )


def transposed_times(left_side, right_side, out=F32):
    return lax.dot_general(
        left_side, right_side, (((0,), (0,)), ((), ())), preferred_element_type=F32
    ).astype(out)


def padded_rows(rows):
    return -(-rows // 8) * 8


def padded_model_rows(rows):
    return -(-(rows + 1) // 8) * 8


def selection(rows, wide, count):
    source = lax.broadcasted_iota(jnp.int32, (count * rows, count * wide), 0)
    target = lax.broadcasted_iota(jnp.int32, (count * rows, count * wide), 1)
    inside = target % wide
    return ((source == target // wide * rows + inside) & (inside < rows)).astype(BF16)


def spread(values, rows, wide):
    if wide == rows:
        return values
    return matmul(values, selection(rows, wide, values.shape[1] // rows)).astype(BF16)


def collect(values, rows, wide):
    if wide == rows:
        return values
    chosen = selection(rows, wide, values.shape[1] // wide)
    first = values.astype(BF16)
    rest = values - first.astype(F32)
    second = rest.astype(BF16)
    third = (rest - second.astype(F32)).astype(BF16)
    return (
        times_transposed(first, chosen)
        + times_transposed(second, chosen)
        + times_transposed(third, chosen)
    )


def place(groups):
    f = lax.axis_index("fsdp")
    s = lax.axis_index("seq")
    c = lax.rem(s, 2)
    y = lax.rem(s // 2, 2)
    z = s // 4
    return f, z, y, c


def device(f, z, y, c):
    return (f, (z * 2 + y) * 2 + c)


def greet(groups, both):
    f, z, y, c = place(groups)
    barrier = pltpu.get_barrier_semaphore()
    peers = [device(f, z, y, 1 - c), device(f, z, 1 - y, c)]
    if both:
        peers.append(device(1 - f, z, y, c))
    for d in range(1, groups):
        peers.append(device(f, lax.rem(z + d, groups), y, c))
    for peer in peers:
        pl.semaphore_signal(barrier, inc=1, device_id=peer, device_id_type=MESH)
    pl.semaphore_wait(barrier, len(peers))


def pieces(rows, columns, target):
    count = max(1, min(columns // 128, round(rows * columns * 2 / target)))
    edges = [round(columns // 128 * i / count) * 128 for i in range(count)] + [columns]
    return [(lo, hi - lo) for lo, hi in zip(edges[:-1], edges[1:])]


def balanced(entries, first, second):
    orders = []
    x = y = 0
    for is_rows, size in entries:
        if is_rows:
            orders.append("y")
            y += 4 * size
        elif max(x + first * size, y + second * size) <= max(x + second * size, y + first * size):
            orders.append("xy")
            x, y = x + first * size, y + second * size
        else:
            orders.append("yx")
            x, y = x + second * size, y + first * size
    return orders


def mixed(row_chunks, chunks):
    step = MIX * len(chunks) / max(1, len(row_chunks))
    keyed = [(i * step, 0, (True,) + chunk) for i, chunk in enumerate(row_chunks)]
    keyed += [(float(i), 1, (False,) + chunk) for i, chunk in enumerate(chunks)]
    return [chunk for _, _, chunk in sorted(keyed, key=lambda entry: entry[:2])]


def run_jobs(jobs, spacing, hooks=()):
    depth = max(len(stages) for stages in jobs)
    for tick in range(len(jobs) + spacing * (depth - 1)):
        for stage in reversed(range(depth)):
            j = tick - spacing * stage
            if 0 <= j < len(jobs) and stage < len(jobs[j]):
                jobs[j][stage]()
        for at, work in hooks:
            if at == tick:
                work()


class Mover:
    def __init__(self, groups, send, recv, local):
        self.groups = groups
        self.send, self.recv, self.local = send, recv, local
        self.f, self.z, self.y, self.c = place(groups)
        f, z, y, c = self.f, self.z, self.y, self.c
        self.core = device(f, z, y, 1 - c)
        self.across = {"y": device(f, z, 1 - y, c), "x": device(1 - f, z, y, c)}
        self.started = []

    def along_z(self, d):
        return device(self.f, lax.rem(self.z + d, self.groups), self.y, self.c)

    def remote(self, src, dst, job, slot, peer):
        return pltpu.make_async_remote_copy(
            src_ref=src,
            dst_ref=dst,
            send_sem=self.send.at[job, slot],
            recv_sem=self.recv.at[job, slot],
            device_id=peer,
            device_id_type=MESH,
        )

    def start(self, src, dst, job, slot, peer):
        copy = self.remote(src, dst, job, slot, peer)
        copy.start()
        self.started.append(copy)

    def arrived(self, ref, job, slot):
        self.remote(ref, ref, job, slot, self.core).wait_recv()

    def drain(self):
        for copy in self.started:
            copy.wait_send()


def gather_job(m, job, order, source, whole, lo, width):
    groups, f, z, y, c = m.groups, m.f, m.z, m.y, m.c
    columns = slice(lo, lo + width)
    own = source.at[:, columns]

    def at(*index):
        return whole.at[index + (slice(None), columns)]

    every = slice(None)

    def begin():
        pltpu.make_async_copy(own, at(f, z, y, c), m.local.at[job]).start()
        for d in range(1, groups):
            m.start(own, at(f, z, y, c), job, d, m.along_z(d))

    def first():
        pltpu.make_async_copy(own, at(f, z, y, c), m.local.at[job]).wait()
        for d in range(1, groups):
            m.arrived(at(f, lax.rem(z + groups - d, groups), y, c), job, d)
        mine = at(f, every, y, c)
        m.start(mine, mine, job, 0, m.across[order[0]])
        m.start(mine, mine, job, groups, m.core)

    def second():
        if order == "yx":
            got, mine = at(f, every, 1 - y, c), at(f, every, every, c)
        else:
            got, mine = at(1 - f, every, y, c), at(every, every, y, c)
        m.arrived(got, job, 0)
        m.start(mine, mine, job, groups + 1, m.across[order[1]])
        m.start(got, got, job, groups + 2, m.core)

    def third():
        got = at(1 - f, every, every, c) if order == "yx" else at(every, every, 1 - y, c)
        m.arrived(got, job, groups + 1)
        m.start(got, got, job, groups + 3, m.core)

    def last():
        other = 1 - c
        m.arrived(at(f, every, y, other), job, groups)
        if order == "yx":
            m.arrived(at(f, every, 1 - y, other), job, groups + 2)
            m.arrived(at(1 - f, every, every, other), job, groups + 3)
        else:
            m.arrived(at(1 - f, every, y, other), job, groups + 2)
            m.arrived(at(every, every, 1 - y, other), job, groups + 3)

    return [begin, first, second, third, last]


def gather_rows_job(m, job, source, whole, lo, width):
    groups, z, y, c = m.groups, m.z, m.y, m.c
    columns = slice(lo, lo + width)
    own = source.at[:, columns]
    every = slice(None)

    def at(*index):
        return whole.at[index + (slice(None), columns)]

    def begin():
        pltpu.make_async_copy(own, at(z, y, c), m.local.at[job]).start()
        for d in range(1, groups):
            m.start(own, at(z, y, c), job, d, m.along_z(d))

    def first():
        pltpu.make_async_copy(own, at(z, y, c), m.local.at[job]).wait()
        for d in range(1, groups):
            m.arrived(at(lax.rem(z + groups - d, groups), y, c), job, d)
        mine = at(every, y, c)
        m.start(mine, mine, job, 0, m.across["y"])
        m.start(mine, mine, job, groups, m.core)

    def second():
        got = at(every, 1 - y, c)
        m.arrived(got, job, 0)
        m.start(got, got, job, groups + 1, m.core)

    def last():
        m.arrived(at(every, y, 1 - c), job, groups)
        m.arrived(at(every, 1 - y, 1 - c), job, groups + 1)

    return [begin, first, second, last]


MIX = 0.6
ATTENTION_PARTS = 4
GATHER_BYTES = 20 * 1024
ROWS_BYTES = 32 * 1024
GATHER_SPACING = 4
SCATTER_BYTES = 20 * 1024
SCATTER_SPACING = 4


def plan_of(row_blocks, blocks, target, first, second):
    row_cuts = [
        (a, lo, width)
        for a, (rows, columns) in enumerate(row_blocks)
        for lo, width in pieces(rows, columns, ROWS_BYTES)
    ]
    cuts = [
        (a, lo, width)
        for a, (rows, columns) in enumerate(blocks)
        for lo, width in pieces(rows, columns, target)
    ]
    chunks = mixed(row_cuts, cuts)
    entries = [
        (is_rows, (row_blocks if is_rows else blocks)[a][0] * width) for is_rows, a, _, width in chunks
    ]
    orders = balanced(entries, first, second)
    return tuple(chunk + (order,) for chunk, order in zip(chunks, orders))


def gather_kernel(groups, plan, rows_count, count, attends, *refs):
    extra = 4 if attends else 0
    ins, refs = refs[:count], refs[count:]
    queries, refs = refs[:extra], refs[extra:]
    outs, refs = refs[:count], refs[count:]
    results, refs = refs[:extra], refs[extra:]
    send, recv, local = refs[:3]
    greet(groups, True)
    m = Mover(groups, send, recv, local)
    jobs = []
    for is_rows, a, lo, width, order in plan:
        if is_rows:
            jobs.append(gather_rows_job(m, len(jobs), ins[a], outs[a], lo, width))
        else:
            b = rows_count + a
            jobs.append(gather_job(m, len(jobs), order, ins[b], outs[b], lo, width))
    hooks = []
    if attends:
        ready = max(i for i, entry in enumerate(plan) if entry[0]) + 3 * GATHER_SPACING
        parts = attention_parts(m, queries, outs[0], outs[1], results, refs[3:])
        step = max(1, (len(plan) + 2 * GATHER_SPACING - ready) // (len(parts) - 1))
        hooks = [(1, parts[0])] + [(ready + i * step, part) for i, part in enumerate(parts[1:])]
    run_jobs(jobs, GATHER_SPACING, hooks)
    m.drain()


def gather(token_rows, shards, identity, queries=None):
    n_f, n_s = lax.axis_size("fsdp"), lax.axis_size("seq")
    groups = n_s // 4
    operands = list(token_rows) + list(shards)
    plan = plan_of(
        [block.shape for block in token_rows], [shard.shape for shard in shards], GATHER_BYTES, 4, 8
    )
    attends = queries is not None
    out_shape = [
        jax.ShapeDtypeStruct((groups, 2, 2) + block.shape, block.dtype) for block in token_rows
    ] + [
        jax.ShapeDtypeStruct((n_f, groups, 2, 2) + shard.shape, shard.dtype) for shard in shards
    ]
    in_specs = [pl.BlockSpec(memory_space=pltpu.VMEM)] * len(operands)
    out_specs = [pl.BlockSpec(memory_space=pltpu.VMEM)] * len(token_rows) + [
        pl.BlockSpec(memory_space=pltpu.HBM)
    ] * len(shards)
    scratch = [
        pltpu.SemaphoreType.DMA((len(plan), groups + 4)),
        pltpu.SemaphoreType.DMA((len(plan), groups + 4)),
        pltpu.SemaphoreType.DMA((len(plan),)),
    ]
    if attends:
        tokens, columns = queries[1].shape
        rows = tokens * HEADS
        in_specs += [pl.BlockSpec(memory_space=pltpu.SMEM)]
        in_specs += [pl.BlockSpec(memory_space=pltpu.VMEM)] * 3
        out_shape += [
            jax.ShapeDtypeStruct((rows, HEAD_DIM), F32),
            jax.ShapeDtypeStruct((tokens, columns), BF16),
            jax.ShapeDtypeStruct((1, rows), F32),
            jax.ShapeDtypeStruct((rows, HEAD_DIM), BF16),
        ]
        out_specs += [pl.BlockSpec(memory_space=pltpu.VMEM)] * 4
        scratch += [pltpu.VMEM((rows, 1), F32), pltpu.VMEM((rows, 1), F32)]
    results = pl.pallas_call(
        partial(gather_kernel, groups, plan, len(token_rows), len(operands), attends),
        out_shape=out_shape,
        in_specs=in_specs,
        out_specs=out_specs,
        scratch_shapes=scratch,
        compiler_params=pltpu.CompilerParams(
            collective_id=identity, has_side_effects=True, vmem_limit_bytes=VMEM_LIMIT
        ),
        name=f"gather_{identity}",
    )(*operands, *(queries if attends else ()))
    whole = [
        result.reshape(-1, block.shape[1]) for result, block in zip(results, operands)
    ]
    return whole + list(results[len(operands) :])


def scatter_job(m, job, order, source, out, lo, width, buffers):
    groups, f, z, y, c = m.groups, m.f, m.z, m.y, m.c
    columns = slice(lo, lo + width)
    every = slice(None)
    held, from_core, from_first, from_second, from_z = buffers

    def half(core):
        return source.at[:, :, :, core, :, columns]

    def add(into, other):
        into[...] = into[...] + other[...]

    def each(step):
        def part(g, carry):
            step(g)
            return carry

        lax.fori_loop(0, groups, part, 0)

    def begin():
        m.start(half(1 - c), from_core, job, 0, m.core)
        pltpu.make_async_copy(half(c), held, m.local.at[job]).start()

    def first():
        pltpu.make_async_copy(half(c), held, m.local.at[job]).wait()
        m.arrived(from_core, job, 0)
        if order == "xy":
            def pair(side):
                def step(g):
                    for k in range(2):
                        add(held.at[side, g, k], from_core.at[side, g, k])
                return step

            each(pair(1 - f))
            m.start(held.at[1 - f], from_first, job, 1, m.across["x"])
            each(pair(f))
        else:
            def pair(side):
                def step(g):
                    for k in range(2):
                        add(held.at[k, g, side], from_core.at[k, g, side])
                return step

            each(pair(1 - y))
            m.start(held.at[:, :, 1 - y], from_first, job, 1, m.across["y"])
            each(pair(y))

    def second():
        m.arrived(from_first, job, 1)
        if order == "xy":
            def side(k):
                return lambda g: add(held.at[f, g, k], from_first.at[g, k])

            each(side(1 - y))
            m.start(held.at[f, :, 1 - y], from_second, job, 2, m.across["y"])
            each(side(y))
        else:
            def side(k):
                return lambda g: add(held.at[k, g, y], from_first.at[k, g])

            each(side(1 - f))
            m.start(held.at[1 - f, :, y], from_second, job, 2, m.across["x"])
            each(side(f))

    def third():
        m.arrived(from_second, job, 2)
        each(lambda g: add(held.at[f, g, y], from_second.at[g]))
        for d in range(1, groups):
            there = lax.rem(z + d, groups)
            m.start(held.at[f, there, y], from_z.at[d - 1], job, 2 + d, m.along_z(d))

    def last():
        total = held[f, z, y].astype(F32)
        for d in range(1, groups):
            m.arrived(from_z.at[d - 1], job, 2 + d)
            total = total + from_z[d - 1].astype(F32)
        out[:, columns] = total

    return [begin, first, second, third, last]


def scatter_rows_job(m, job, source, out, lo, width, buffers):
    groups, z, y, c = m.groups, m.z, m.y, m.c
    columns = slice(lo, lo + width)
    held, from_core, from_y, from_z = buffers

    def half(core):
        return source.at[:, :, core, :, columns]

    def add(into, other):
        into[...] = into[...] + other[...]

    def each(step):
        def part(g, carry):
            step(g)
            return carry

        lax.fori_loop(0, groups, part, 0)

    def begin():
        m.start(half(1 - c), from_core, job, 0, m.core)
        pltpu.make_async_copy(half(c), held, m.local.at[job]).start()

    def first():
        pltpu.make_async_copy(half(c), held, m.local.at[job]).wait()
        m.arrived(from_core, job, 0)
        each(lambda g: add(held.at[g, 1 - y], from_core.at[g, 1 - y]))
        m.start(held.at[:, 1 - y], from_y, job, 1, m.across["y"])
        each(lambda g: add(held.at[g, y], from_core.at[g, y]))

    def second():
        m.arrived(from_y, job, 1)
        each(lambda g: add(held.at[g, y], from_y.at[g]))
        for d in range(1, groups):
            there = lax.rem(z + d, groups)
            m.start(held.at[there, y], from_z.at[d - 1], job, 2 + d, m.along_z(d))

    def last():
        total = held[z, y].astype(F32)
        for d in range(1, groups):
            m.arrived(from_z.at[d - 1], job, 2 + d)
            total = total + from_z[d - 1].astype(F32)
        out[:, columns] = total

    return [begin, first, second, last]


def scatter_kernel(groups, plan, rows_count, count, *refs):
    ins, outs = refs[:count], refs[count : 2 * count]
    send, recv, local = refs[2 * count : 2 * count + 3]
    scratch = list(refs[2 * count + 3 :])
    greet(groups, True)
    m = Mover(groups, send, recv, local)
    jobs = []
    for is_rows, a, lo, width, order in plan:
        if is_rows:
            buffers, scratch = scratch[:4], scratch[4:]
            jobs.append(scatter_rows_job(m, len(jobs), ins[a], outs[a], lo, width, buffers))
        else:
            buffers, scratch = scratch[:5], scratch[5:]
            b = rows_count + a
            jobs.append(scatter_job(m, len(jobs), order, ins[b], outs[b], lo, width, buffers))
    run_jobs(jobs, SCATTER_SPACING)
    m.drain()


def scatter(token_rows, partials, identity):
    n_f, n_s = lax.axis_size("fsdp"), lax.axis_size("seq")
    groups = n_s // 4
    row_blocks = [(p.shape[0] // n_s, p.shape[1]) for p in token_rows]
    blocks = [(p.shape[0] // (n_f * n_s), p.shape[1]) for p in partials]
    plan = plan_of(row_blocks, blocks, SCATTER_BYTES, 8, 4)
    scratch = []
    for is_rows, a, _, width, order in plan:
        if is_rows:
            block = (row_blocks[a][0], width)
            scratch += [
                pltpu.VMEM((groups, 2) + block, BF16),
                pltpu.VMEM((groups, 2) + block, BF16),
                pltpu.VMEM((groups,) + block, BF16),
                pltpu.VMEM((groups - 1,) + block, BF16),
            ]
        else:
            block = (blocks[a][0], width)
            scratch += [
                pltpu.VMEM((n_f, groups, 2) + block, BF16),
                pltpu.VMEM((n_f, groups, 2) + block, BF16),
                pltpu.VMEM(((groups, 2) if order == "xy" else (n_f, groups)) + block, BF16),
                pltpu.VMEM((groups,) + block, BF16),
                pltpu.VMEM((groups - 1,) + block, BF16),
            ]
    count = len(row_blocks) + len(blocks)
    return pl.pallas_call(
        partial(scatter_kernel, groups, plan, len(row_blocks), count),
        out_shape=[jax.ShapeDtypeStruct(b, F32) for b in row_blocks + blocks],
        in_specs=[pl.BlockSpec(memory_space=pltpu.HBM)] * count,
        out_specs=[pl.BlockSpec(memory_space=pltpu.VMEM)] * count,
        scratch_shapes=[
            pltpu.SemaphoreType.DMA((len(plan), groups + 2)),
            pltpu.SemaphoreType.DMA((len(plan), groups + 2)),
            pltpu.SemaphoreType.DMA((len(plan),)),
        ]
        + scratch,
        compiler_params=pltpu.CompilerParams(
            collective_id=identity, has_side_effects=True, vmem_limit_bytes=VMEM_LIMIT
        ),
        name=f"scatter_{identity}",
    )(
        *[p.reshape((groups, 2, 2) + b) for p, b in zip(token_rows, row_blocks)],
        *[p.reshape((n_f, groups, 2, 2) + b) for p, b in zip(partials, blocks)],
    )


def finish_kernel(cuts, count, *refs):
    total = len(cuts)
    ins, outs = refs[:count], refs[count : count + total]
    staged, sems = refs[count + total : count + 2 * total], refs[count + 2 * total]
    for i, (a, rows, lo, width) in enumerate(cuts):
        staged[i][...] = ins[a][0:rows, lo : lo + width]
    for i in range(total):
        pltpu.make_async_copy(staged[i], outs[i], sems.at[i]).start()
    for i in range(total):
        pltpu.make_async_copy(staged[i], outs[i], sems.at[i]).wait()


def finish(sums, cuts):
    shapes = [(rows, width) for _, rows, _, width in cuts]
    return pl.pallas_call(
        partial(finish_kernel, tuple(cuts), len(sums)),
        out_shape=[jax.ShapeDtypeStruct(shape, F32) for shape in shapes],
        in_specs=[pl.BlockSpec(memory_space=pltpu.VMEM)] * len(sums),
        out_specs=[pl.BlockSpec(memory_space=pltpu.HBM)] * len(cuts),
        scratch_shapes=[pltpu.VMEM(shape, F32) for shape in shapes]
        + [pltpu.SemaphoreType.DMA((len(cuts),))],
        compiler_params=pltpu.CompilerParams(vmem_limit_bytes=VMEM_LIMIT),
        name="finish",
    )(*sums)


def as_row(column):
    return jnp.transpose(jnp.broadcast_to(column, (column.shape[0], 128)))[0:1, :]


def attention_parts(m, queries, keys, values, results, scratch):
    valid_ref, query_ref, cosine, sine = queries
    out_ref, low_ref, norm_ref, stacked = results
    peak, total = scratch
    tokens = query_ref.shape[0]
    half = HEAD_DIM // 2
    span = 4 * tokens
    scale = HEAD_DIM ** (-0.5)
    start = lax.axis_index("seq") * tokens

    def begin():
        for h in range(HEADS):
            first = query_ref[:, h * HEAD_DIM : h * HEAD_DIM + half]
            second = query_ref[:, h * HEAD_DIM + half : (h + 1) * HEAD_DIM]
            at = slice(h * tokens, (h + 1) * tokens)
            stacked[at, :half] = (first * cosine[...] - second * sine[...]).astype(BF16)
            stacked[at, half:] = (second * cosine[...] + first * sine[...]).astype(BF16)
        peak[...] = jnp.full(peak.shape, -jnp.inf, F32)
        total[...] = jnp.zeros(total.shape, F32)
        out_ref[...] = jnp.zeros(out_ref.shape, F32)

    def block(i, carry):
        j, h = i // HEADS, lax.rem(i, HEADS)
        own = pl.ds(pl.multiple_of(h * tokens, tokens), tokens)
        raw = times_transposed(stacked[own, :], keys[j].reshape(span, HEAD_DIM)) * scale
        key_pos = j * span + lax.broadcasted_iota(jnp.int32, (tokens, span), 1)
        row_pos = start + lax.broadcasted_iota(jnp.int32, (tokens, span), 0)
        raw = jnp.where(key_pos <= jnp.minimum(row_pos, valid_ref[0] - 1), raw, -jnp.inf)
        old = peak[own, :]
        new = jnp.maximum(old, jnp.max(raw, axis=1, keepdims=True))
        shrink = jnp.exp(old - new)
        weights = jnp.exp(raw - new)
        total[own, :] = total[own, :] * shrink + jnp.sum(weights, axis=1, keepdims=True)
        out_ref[own, :] = out_ref[own, :] * shrink + matmul(
            weights.astype(BF16), values[j].reshape(span, HEAD_DIM)
        )
        peak[own, :] = new
        return carry

    count = (m.z + 1) * HEADS

    def some(part):
        def work():
            lax.fori_loop(
                count * part // ATTENTION_PARTS, count * (part + 1) // ATTENTION_PARTS, block, 0
            )

        return work

    def end():
        for h in range(HEADS):
            at = slice(h * tokens, (h + 1) * tokens)
            result = out_ref[at, :] / total[at, :]
            out_ref[at, :] = result
            low_ref[:, h * HEAD_DIM : (h + 1) * HEAD_DIM] = result.astype(BF16)
            norm_ref[0:1, at] = as_row(peak[at, :] + jnp.log(total[at, :]))

    return [begin] + [some(part) for part in range(ATTENTION_PARTS)] + [end]


def backward_kernel(
    span,
    bounds,
    stacked,
    grad_ref,
    attended,
    cosine,
    sine,
    key_ref,
    value_ref,
    norm_ref,
    gq_ref,
    gkv_ref,
    grads,
    gathered,
    delta,
    sums,
):
    tokens = grad_ref.shape[0]
    half = HEAD_DIM // 2
    scale = HEAD_DIM ** (-0.5)
    start, valid = bounds[0], bounds[1]
    for h in range(HEADS):
        at = slice(h * tokens, (h + 1) * tokens)
        part = grad_ref[:, h * HEAD_DIM : (h + 1) * HEAD_DIM]
        grads[at, :] = part
        delta[0:1, at] = as_row(
            jnp.sum(part.astype(F32) * attended[at, :], axis=1, keepdims=True)
        )
    gathered[...] = jnp.zeros(gathered.shape, F32)

    def block(j, masked):
        at = pl.multiple_of(j * span, span)
        here = pl.ds(at, span)
        sums[...] = jnp.zeros(sums.shape, F32)

        def head(h, carry):
            low = pl.multiple_of(h * tokens, tokens)
            own = pl.ds(low, tokens)
            raw = times_transposed(key_ref[here, :], stacked[own, :]) * scale
            soft = jnp.exp(raw - norm_ref[:, own])
            if masked:
                key_pos = at + lax.broadcasted_iota(jnp.int32, (span, tokens), 0)
                row_pos = start + lax.broadcasted_iota(jnp.int32, (span, tokens), 1)
                soft = jnp.where(key_pos <= jnp.minimum(row_pos, valid - 1), soft, 0.0)
            toward = times_transposed(value_ref[here, :], grads[own, :])
            pulled = (soft * (toward - delta[:, own])).astype(BF16)
            sums[:, HEAD_DIM:] += matmul(soft.astype(BF16), grads[own, :])
            sums[:, :HEAD_DIM] += matmul(pulled, stacked[own, :])
            gathered[own, :] += transposed_times(pulled, key_ref[here, :])
            return carry

        lax.fori_loop(0, HEADS, head, 0)
        gkv_ref[here, HEAD_DIM:] = sums[:, HEAD_DIM:].astype(BF16)
        gkv_ref[here, :HEAD_DIM] = (sums[:, :HEAD_DIM] * scale).astype(BF16)

    plain = jnp.minimum(start, valid) // span
    last = jnp.minimum(start + tokens, valid)
    every = jnp.where(start < valid, (last + span - 1) // span, 0)
    plain = jnp.minimum(plain, every)

    def free(j, carry):
        block(j, False)
        return carry

    def edge(j, carry):
        block(j, True)
        return carry

    def empty(j, carry):
        at = pl.multiple_of(j * span, span)
        gkv_ref[pl.ds(at, span), :] = jnp.zeros((span, 2 * HEAD_DIM), BF16)
        return carry

    lax.fori_loop(0, plain, free, 0)
    lax.fori_loop(plain, every, edge, 0)
    lax.fori_loop(every, key_ref.shape[0] // span, empty, 0)
    for h in range(HEADS):
        at = slice(h * tokens, (h + 1) * tokens)
        first = gathered[at, :half] * scale
        second = gathered[at, half:] * scale
        lo = h * HEAD_DIM
        gq_ref[:, lo : lo + half] = (first * cosine[...] + second * sine[...]).astype(BF16)
        gq_ref[:, lo + half : lo + HEAD_DIM] = (second * cosine[...] - first * sine[...]).astype(BF16)


def attention_backward(bounds, stacked, grad, attended, cosine, sine, keys, values, norm, span):
    tokens = grad.shape[0]
    rows = tokens * HEADS
    return pl.pallas_call(
        partial(backward_kernel, span),
        out_shape=[
            jax.ShapeDtypeStruct((tokens, HEADS * HEAD_DIM), BF16),
            jax.ShapeDtypeStruct((keys.shape[0], 2 * HEAD_DIM), BF16),
        ],
        in_specs=[pl.BlockSpec(memory_space=pltpu.SMEM)]
        + [pl.BlockSpec(memory_space=pltpu.VMEM)] * 8,
        out_specs=[pl.BlockSpec(memory_space=pltpu.VMEM)] * 2,
        scratch_shapes=[
            pltpu.VMEM((rows, HEAD_DIM), BF16),
            pltpu.VMEM((rows, HEAD_DIM), F32),
            pltpu.VMEM((1, rows), F32),
            pltpu.VMEM((span, 2 * HEAD_DIM), F32),
        ],
        compiler_params=pltpu.CompilerParams(vmem_limit_bytes=VMEM_LIMIT),
        name="attention_backward",
    )(bounds, stacked, grad, attended, cosine, sine, keys, values, norm)


def pack_kernel(cuts, gains, count, *refs):
    ins, gain_refs = refs[:count], refs[count : count + len(gains)]
    outs = refs[count + len(gains) :]
    for out in outs:
        out[...] = jnp.zeros(out.shape, BF16)
    for source, (target, lo) in zip(ins, cuts):
        outs[target][0 : source.shape[0], lo : lo + source.shape[1]] = source[...]
    for gain, target in zip(gain_refs, gains):
        rows = gain.shape[1]
        outs[target][rows : rows + 1, 0:rows] = gain[...]


def pack(groups_of_weights, gains, gain_targets):
    weights, cuts, shapes = [], [], []
    for target, (wide, members) in enumerate(groups_of_weights):
        lo = 0
        for member in members:
            weights.append(member)
            cuts.append((target, lo))
            lo += member.shape[1]
        shapes.append((wide, lo))
    return pl.pallas_call(
        partial(pack_kernel, tuple(cuts), tuple(gain_targets), len(weights)),
        out_shape=[jax.ShapeDtypeStruct(shape, BF16) for shape in shapes],
        in_specs=[pl.BlockSpec(memory_space=pltpu.VMEM)] * (len(weights) + len(gains)),
        out_specs=[pl.BlockSpec(memory_space=pltpu.VMEM)] * len(shapes),
        compiler_params=pltpu.CompilerParams(vmem_limit_bytes=VMEM_LIMIT),
        name="pack",
    )(*weights, *[gain[None] for gain in gains])


def gain_whole(gathered, rows):
    wide = padded_model_rows(rows)
    return gathered.reshape(-1, wide, gathered.shape[1])[:, rows, :rows].reshape(-1).astype(F32)


def with_gain(partial_sums, gain_grad, rows):
    wide = padded_model_rows(rows)
    blocks = partial_sums.reshape(-1, wide, partial_sums.shape[1])
    return blocks.at[:, rows, :rows].set(gain_grad.reshape(-1, rows).astype(BF16)).reshape(partial_sums.shape)


def per_device(
    hidden_in,
    cotangent,
    dataset_ids,
    mixing,
    pad_lengths,
    attention_gain,
    merged_projection,
    merged_adapter_in,
    query_adapter_out,
    keyval_adapter_out,
    output_projection,
    output_adapter_in,
    output_adapter_out,
    feedforward_gain,
    gate_up_weight,
    gate_up_adapter_in,
    gate_up_adapter_out,
    down_weight,
    down_adapter_in,
    down_adapter_out,
):
    tokens, width = hidden_in.shape
    query_width = HEADS * HEAD_DIM
    merged_width = query_width + 2 * HEAD_DIM
    model_rows = merged_projection.shape[0]
    rank_rows = query_adapter_out.shape[0]
    pair_rows = keyval_adapter_out.shape[0]
    out_rows = output_projection.shape[0]
    ff_rows = down_weight.shape[0]
    model_wide, rank_wide = padded_model_rows(model_rows), padded_rows(rank_rows)
    pair_wide, ff_wide = padded_rows(pair_rows), padded_rows(ff_rows)

    packed = pack(
        [
            (model_wide, [merged_projection, merged_adapter_in]),
            (model_wide, [gate_up_weight, gate_up_adapter_in]),
            (rank_wide, [query_adapter_out]),
            (pair_wide, [keyval_adapter_out]),
            (padded_rows(out_rows), [output_projection, output_adapter_in]),
            (rank_wide, [output_adapter_out]),
            (pair_wide, [gate_up_adapter_out]),
            (ff_wide, [down_weight, down_adapter_in]),
            (rank_wide, [down_adapter_out]),
        ],
        [attention_gain, feedforward_gain],
        [0, 1],
    )
    merged, lift_query, lift_keyval = gather([], [packed[0], packed[2], packed[3]], 0)
    gain_one = gain_whole(merged, model_rows)

    hidden = hidden_in.astype(F32)
    normed_one, norm_one_back = jax.vjp(rms_scale, hidden, gain_one)
    first_in = spread(normed_one.astype(BF16), model_rows, model_wide)
    projected = matmul(first_in, merged)
    lifted = projected[:, merged_width:].astype(BF16)
    lifted_query = spread(lifted[:, :RANK], rank_rows, rank_wide)
    lifted_pair = spread(lifted[:, RANK:], pair_rows, pair_wide)
    half_pair = lifted_pair.shape[1] // 2
    query_rows = projected[:, :query_width] + matmul(lifted_query, lift_query)
    key_rows = projected[:, query_width : query_width + HEAD_DIM] + matmul(
        lifted_pair[:, :half_pair], lift_keyval[:half_pair]
    )
    value_rows = projected[:, query_width + HEAD_DIM : merged_width] + matmul(
        lifted_pair[:, half_pair:], lift_keyval[half_pair:]
    )
    start_pos = lax.axis_index("seq") * tokens
    positions = start_pos + jnp.arange(tokens, dtype=jnp.int32)
    cosine_table, sine_table = rotary_tables(positions)
    keys_rot = rotate(key_rows, cosine_table, sine_table).astype(BF16)
    length = lax.axis_size("seq") * tokens
    valid_count = length - pad_lengths[0]
    span = min(1024, length)
    bounds = jnp.stack([start_pos, valid_count])
    (
        keys_all,
        values_all,
        out_full,
        lift_out,
        gate_up,
        lift_gate_up,
        down,
        lift_down,
        attended,
        attended_low,
        log_norm,
        query_rot,
    ) = gather(
        [keys_rot, value_rows.astype(BF16)],
        [packed[4], packed[5], packed[1], packed[6], packed[7], packed[8]],
        1,
        (valid_count.reshape(1), query_rows, cosine_table, sine_table),
    )
    gain_two = gain_whole(gate_up, model_rows)
    out_both = matmul(attended_low, out_full)
    lifted_out = spread(out_both[:, width:].astype(BF16), rank_rows, rank_wide)
    middle = hidden + (out_both[:, :width] + matmul(lifted_out, lift_out))

    normed_two, norm_two_back = jax.vjp(rms_scale, middle, gain_two)
    second_in = spread(normed_two.astype(BF16), model_rows, model_wide)
    pre_gate = matmul(second_in, gate_up)
    lifted_gate_up = spread(pre_gate[:, 2 * FF :].astype(BF16), pair_rows, pair_wide)
    half_gate = lifted_gate_up.shape[1] // 2
    gate_part = pre_gate[:, :FF] + matmul(lifted_gate_up[:, :half_gate], lift_gate_up[:half_gate])
    upper_part = pre_gate[:, FF : 2 * FF] + matmul(
        lifted_gate_up[:, half_gate:], lift_gate_up[half_gate:]
    )
    activated, gelu_back = jax.vjp(partial(jax.nn.gelu, approximate=True), gate_part)
    inner = spread((activated * upper_part).astype(BF16), ff_rows, ff_wide)
    down_both = matmul(inner, down)
    lifted_down = spread(down_both[:, width:].astype(BF16), rank_rows, rank_wide)
    output = middle + (down_both[:, :width] + matmul(lifted_down, lift_down))

    matches = dataset_ids[:, None] == jnp.arange(DATASETS, dtype=jnp.int32)[None, :]
    picked = jnp.sum(jnp.where(matches, mixing[None, :], 0.0), axis=1)
    row_weight = jnp.where(positions < valid_count, picked, 0.0)
    scaled = cotangent.astype(F32) * row_weight[:, None]

    grad_branch = scaled.astype(BF16)
    grad_lifted_down = collect(times_transposed(grad_branch, lift_down), rank_rows, rank_wide)
    grad_down = jnp.concatenate([grad_branch, grad_lifted_down.astype(BF16)], axis=1)
    grad_inner = collect(times_transposed(grad_down, down), ff_rows, ff_wide)
    grad_gate = gelu_back(grad_inner * upper_part)[0].astype(BF16)
    grad_upper = (grad_inner * activated).astype(BF16)
    grad_gate_up = jnp.concatenate(
        [
            grad_gate,
            grad_upper,
            collect(
                times_transposed(grad_gate, lift_gate_up[:half_gate]), pair_rows, pair_wide
            ).astype(BF16),
            collect(
                times_transposed(grad_upper, lift_gate_up[half_gate:]), pair_rows, pair_wide
            ).astype(BF16),
        ],
        axis=1,
    )
    grad_normed_two = collect(times_transposed(grad_gate_up, gate_up), model_rows, model_wide)
    grad_middle_norm, gain_two_grad = norm_two_back(grad_normed_two)
    grad_middle = scaled + grad_middle_norm

    grad_attn = grad_middle.astype(BF16)
    grad_lifted_out = collect(times_transposed(grad_attn, lift_out), rank_rows, rank_wide)
    grad_out = jnp.concatenate([grad_attn, grad_lifted_out.astype(BF16)], axis=1)
    grad_attention = times_transposed(grad_out, out_full).astype(BF16)
    grad_query_low, kv_terms = attention_backward(
        bounds,
        query_rot,
        grad_attention,
        attended,
        cosine_table,
        sine_table,
        keys_all,
        values_all,
        log_norm,
        span,
    )
    gate_up_out_term = jnp.concatenate(
        [
            transposed_times(lifted_gate_up[:, :half_gate], grad_gate, BF16),
            transposed_times(lifted_gate_up[:, half_gate:], grad_upper, BF16),
        ],
        axis=0,
    )
    kv_summed, gate_up_sum, down_sum, out_sum, gate_up_out_sum, out_out_sum, down_out_sum = scatter(
        [kv_terms],
        [
            with_gain(transposed_times(second_in, grad_gate_up, BF16), gain_two_grad, model_rows),
            transposed_times(inner, grad_down, BF16),
            transposed_times(attended_low, grad_out, BF16),
            gate_up_out_term,
            transposed_times(lifted_out, grad_attn, BF16),
            transposed_times(lifted_down, grad_branch, BF16),
        ],
        2,
    )
    grad_keys = rotate(kv_summed[:, :HEAD_DIM], cosine_table, -sine_table)
    grad_keys_low = grad_keys.astype(BF16)
    grad_values_low = kv_summed[:, HEAD_DIM:].astype(BF16)
    grad_merged = jnp.concatenate(
        [
            grad_query_low,
            grad_keys_low,
            grad_values_low,
            collect(times_transposed(grad_query_low, lift_query), rank_rows, rank_wide).astype(BF16),
            collect(
                times_transposed(grad_keys_low, lift_keyval[:half_pair]), pair_rows, pair_wide
            ).astype(BF16),
            collect(
                times_transposed(grad_values_low, lift_keyval[half_pair:]), pair_rows, pair_wide
            ).astype(BF16),
        ],
        axis=1,
    )
    grad_normed_one = collect(times_transposed(grad_merged, merged), model_rows, model_wide)
    grad_hidden_norm, gain_one_grad = norm_one_back(grad_normed_one)
    hidden_grad = grad_middle + grad_hidden_norm

    keyval_term = jnp.concatenate(
        [
            transposed_times(lifted_pair[:, :half_pair], grad_keys_low, BF16),
            transposed_times(lifted_pair[:, half_pair:], grad_values_low, BF16),
        ],
        axis=0,
    )
    merged_sum, query_out_sum, keyval_sum = scatter(
        [],
        [
            with_gain(transposed_times(first_in, grad_merged, BF16), gain_one_grad, model_rows),
            transposed_times(lifted_query, grad_query_low, BF16),
            keyval_term,
        ],
        3,
    )
    grads = finish(
        [
            merged_sum,
            query_out_sum,
            keyval_sum,
            out_sum,
            out_out_sum,
            gate_up_sum,
            gate_up_out_sum,
            down_sum,
            down_out_sum,
        ],
        [
            (0, model_rows, 0, merged_width),
            (0, model_rows, merged_width, 3 * RANK),
            (1, rank_rows, 0, query_width),
            (2, pair_rows, 0, HEAD_DIM),
            (3, out_rows, 0, width),
            (3, out_rows, width, RANK),
            (4, rank_rows, 0, width),
            (5, model_rows, 0, 2 * FF),
            (5, model_rows, 2 * FF, 2 * RANK),
            (6, pair_rows, 0, FF),
            (7, ff_rows, 0, width),
            (7, ff_rows, width, RANK),
            (8, rank_rows, 0, width),
        ],
    )
    return (
        output.astype(BF16),
        hidden_grad.astype(BF16),
        merged_sum[model_rows, :model_rows],
        *grads[:7],
        gate_up_sum[model_rows, :model_rows],
        *grads[7:],
    )


def solution(mesh):
    rows, vector = P(AXES, None), P(AXES)
    return jax.shard_map(
        per_device,
        mesh=mesh,
        in_specs=(rows, rows, vector, P(), P("fsdp"), vector)
        + (rows,) * 7
        + (vector,)
        + (rows,) * 6,
        out_specs=(rows, rows, vector) + (rows,) * 7 + (vector,) + (rows,) * 6,
        check_vma=False,
    )
```

```python
from functools import partial

import jax
import jax.numpy as jnp
from jax import lax
from jax.experimental import pallas as pl
from jax.experimental.pallas import tpu as pltpu
from jax.sharding import PartitionSpec as P

HEADS = 4
HEAD_DIM = 256
FF = 2048
RANK = 256
DATASETS = 16
EPSILON = 1e-06
MESH = pl.DeviceIdType.MESH
VMEM_LIMIT = 60 * 1024 * 1024
AXES = ("fsdp", "seq")
BF16 = jnp.bfloat16
F32 = jnp.float32


def rms_scale(values, gain_vector):
    inverse = lax.rsqrt(jnp.mean(values * values, axis=-1, keepdims=True) + EPSILON)
    return values * inverse * gain_vector


def rotary_tables(positions):
    half_width = HEAD_DIM // 2
    inverse = 10000.0 ** (-2.0 * jnp.arange(half_width, dtype=F32) / HEAD_DIM)
    angles = positions.astype(F32)[:, None] * inverse[None, :]
    return (jnp.cos(angles), jnp.sin(angles))


def rotate(values, cosine_table, sine_table):
    half_width = values.shape[-1] // 2
    first = values[..., :half_width]
    second = values[..., half_width:]
    return jnp.concatenate(
        [first * cosine_table - second * sine_table, second * cosine_table + first * sine_table],
        axis=-1,
    )


def matmul(left_side, right_side):
    return jnp.dot(left_side, right_side, preferred_element_type=F32)


def times_transposed(left_side, right_side):
    return lax.dot_general(
        left_side, right_side, (((1,), (1,)), ((), ())), preferred_element_type=F32
    )


def transposed_times(left_side, right_side, out=F32):
    return lax.dot_general(
        left_side, right_side, (((0,), (0,)), ((), ())), preferred_element_type=F32
    ).astype(out)


def padded_rows(rows):
    return -(-rows // 8) * 8


def padded_model_rows(rows):
    return -(-(rows + 1) // 8) * 8


def selection(rows, wide, count):
    source = lax.broadcasted_iota(jnp.int32, (count * rows, count * wide), 0)
    target = lax.broadcasted_iota(jnp.int32, (count * rows, count * wide), 1)
    inside = target % wide
    return ((source == target // wide * rows + inside) & (inside < rows)).astype(BF16)


def spread(values, rows, wide):
    if wide == rows:
        return values
    return matmul(values, selection(rows, wide, values.shape[1] // rows)).astype(BF16)


def collect(values, rows, wide):
    if wide == rows:
        return values
    chosen = selection(rows, wide, values.shape[1] // wide)
    first = values.astype(BF16)
    rest = values - first.astype(F32)
    second = rest.astype(BF16)
    third = (rest - second.astype(F32)).astype(BF16)
    return (
        times_transposed(first, chosen)
        + times_transposed(second, chosen)
        + times_transposed(third, chosen)
    )


def place(groups):
    f = lax.axis_index("fsdp")
    s = lax.axis_index("seq")
    c = lax.rem(s, 2)
    y = lax.rem(s // 2, 2)
    z = s // 4
    return f, z, y, c


def device(f, z, y, c):
    return (f, (z * 2 + y) * 2 + c)


def greet(groups, both):
    f, z, y, c = place(groups)
    barrier = pltpu.get_barrier_semaphore()
    peers = [device(f, z, y, 1 - c), device(f, z, 1 - y, c)]
    if both:
        peers.append(device(1 - f, z, y, c))
    for d in range(1, groups):
        peers.append(device(f, lax.rem(z + d, groups), y, c))
    for peer in peers:
        pl.semaphore_signal(barrier, inc=1, device_id=peer, device_id_type=MESH)
    pl.semaphore_wait(barrier, len(peers))


def pieces(rows, columns, target):
    count = max(1, min(columns // 128, round(rows * columns * 2 / target)))
    edges = [round(columns // 128 * i / count) * 128 for i in range(count)] + [columns]
    return [(lo, hi - lo) for lo, hi in zip(edges[:-1], edges[1:])]


def balanced(entries, first, second):
    orders = []
    x = y = 0
    for is_rows, size in entries:
        if is_rows:
            orders.append("y")
            y += 4 * size
        elif max(x + first * size, y + second * size) <= max(x + second * size, y + first * size):
            orders.append("xy")
            x, y = x + first * size, y + second * size
        else:
            orders.append("yx")
            x, y = x + second * size, y + first * size
    return orders


def mixed(row_chunks, chunks, begin, end):
    step = (end - begin) * len(chunks) / max(1, len(row_chunks))
    keyed = [
        (begin * len(chunks) + i * step, 0, (True,) + chunk) for i, chunk in enumerate(row_chunks)
    ]
    keyed += [(float(i), 1, (False,) + chunk) for i, chunk in enumerate(chunks)]
    return [chunk for _, _, chunk in sorted(keyed, key=lambda entry: entry[:2])]


def run_jobs(jobs, spacing, hooks=()):
    depth = max(len(stages) for stages in jobs)
    for tick in range(len(jobs) + spacing * (depth - 1)):
        for stage in reversed(range(depth)):
            j = tick - spacing * stage
            if 0 <= j < len(jobs) and stage < len(jobs[j]):
                jobs[j][stage]()
        for at, work in hooks:
            if at == tick:
                work()


class Mover:
    def __init__(self, groups, send, recv, local):
        self.groups = groups
        self.send, self.recv, self.local = send, recv, local
        self.f, self.z, self.y, self.c = place(groups)
        f, z, y, c = self.f, self.z, self.y, self.c
        self.core = device(f, z, y, 1 - c)
        self.across = {"y": device(f, z, 1 - y, c), "x": device(1 - f, z, y, c)}
        self.started = []

    def along_z(self, d):
        return device(self.f, lax.rem(self.z + d, self.groups), self.y, self.c)

    def remote(self, src, dst, job, slot, peer):
        return pltpu.make_async_remote_copy(
            src_ref=src,
            dst_ref=dst,
            send_sem=self.send.at[job, slot],
            recv_sem=self.recv.at[job, slot],
            device_id=peer,
            device_id_type=MESH,
        )

    def start(self, src, dst, job, slot, peer):
        copy = self.remote(src, dst, job, slot, peer)
        copy.start()
        self.started.append(copy)

    def arrived(self, ref, job, slot):
        self.remote(ref, ref, job, slot, self.core).wait_recv()

    def drain(self):
        for copy in self.started:
            copy.wait_send()


def gather_job(m, job, order, source, whole, lo, width):
    groups, f, z, y, c = m.groups, m.f, m.z, m.y, m.c
    columns = slice(lo, lo + width)
    own = source.at[:, columns]

    def at(*index):
        return whole.at[index + (slice(None), columns)]

    every = slice(None)

    def begin():
        pltpu.make_async_copy(own, at(f, z, y, c), m.local.at[job]).start()
        for d in range(1, groups):
            m.start(own, at(f, z, y, c), job, d, m.along_z(d))

    def first():
        pltpu.make_async_copy(own, at(f, z, y, c), m.local.at[job]).wait()
        for d in range(1, groups):
            m.arrived(at(f, lax.rem(z + groups - d, groups), y, c), job, d)
        mine = at(f, every, y, c)
        m.start(mine, mine, job, 0, m.across[order[0]])
        m.start(mine, mine, job, groups, m.core)

    def second():
        if order == "yx":
            got, mine = at(f, every, 1 - y, c), at(f, every, every, c)
        else:
            got, mine = at(1 - f, every, y, c), at(every, every, y, c)
        m.arrived(got, job, 0)
        m.start(mine, mine, job, groups + 1, m.across[order[1]])
        m.start(got, got, job, groups + 2, m.core)

    def third():
        got = at(1 - f, every, every, c) if order == "yx" else at(every, every, 1 - y, c)
        m.arrived(got, job, groups + 1)
        m.start(got, got, job, groups + 3, m.core)

    def last():
        other = 1 - c
        m.arrived(at(f, every, y, other), job, groups)
        if order == "yx":
            m.arrived(at(f, every, 1 - y, other), job, groups + 2)
            m.arrived(at(1 - f, every, every, other), job, groups + 3)
        else:
            m.arrived(at(1 - f, every, y, other), job, groups + 2)
            m.arrived(at(every, every, 1 - y, other), job, groups + 3)

    return [begin, first, second, third, last]


def gather_rows_job(m, job, source, whole, lo, width):
    groups, z, y, c = m.groups, m.z, m.y, m.c
    columns = slice(lo, lo + width)
    own = source.at[:, columns]
    every = slice(None)

    def at(*index):
        return whole.at[index + (slice(None), columns)]

    def begin():
        pltpu.make_async_copy(own, at(z, y, c), m.local.at[job]).start()
        for d in range(1, groups):
            m.start(own, at(z, y, c), job, d, m.along_z(d))

    def first():
        pltpu.make_async_copy(own, at(z, y, c), m.local.at[job]).wait()
        for d in range(1, groups):
            m.arrived(at(lax.rem(z + groups - d, groups), y, c), job, d)
        mine = at(every, y, c)
        m.start(mine, mine, job, 0, m.across["y"])
        m.start(mine, mine, job, groups, m.core)

    def second():
        got = at(every, 1 - y, c)
        m.arrived(got, job, 0)
        m.start(got, got, job, groups + 1, m.core)

    def last():
        m.arrived(at(every, y, 1 - c), job, groups)
        m.arrived(at(every, 1 - y, 1 - c), job, groups + 1)

    return [begin, first, second, last]


MIX = 0.6
FUSED_BYTES = 24 * 1024 * 1024
ATTENTION_PARTS = 4
GATHER_BYTES = 20 * 1024
ROWS_BYTES = 32 * 1024
GATHER_SPACING = 4
SCATTER_BYTES = 20 * 1024
SCATTER_SPACING = 4


def plan_of(row_blocks, blocks, target, first, second, begin, end):
    row_cuts = [
        (a, lo, width)
        for a, (rows, columns) in enumerate(row_blocks)
        for lo, width in pieces(rows, columns, ROWS_BYTES)
    ]
    cuts = [
        (a, lo, width)
        for a, (rows, columns) in enumerate(blocks)
        for lo, width in pieces(rows, columns, target)
    ]
    chunks = mixed(row_cuts, cuts, begin, end)
    entries = [
        (is_rows, (row_blocks if is_rows else blocks)[a][0] * width) for is_rows, a, _, width in chunks
    ]
    orders = balanced(entries, first, second)
    return tuple(chunk + (order,) for chunk, order in zip(chunks, orders))


def gather_kernel(groups, plan, rows_count, count, attends, *refs):
    extra = 4 if attends else 0
    ins, refs = refs[:count], refs[count:]
    queries, refs = refs[:extra], refs[extra:]
    outs, refs = refs[:count], refs[count:]
    results, refs = refs[:extra], refs[extra:]
    send, recv, local = refs[:3]
    greet(groups, True)
    m = Mover(groups, send, recv, local)
    jobs = []
    for is_rows, a, lo, width, order in plan:
        if is_rows:
            jobs.append(gather_rows_job(m, len(jobs), ins[a], outs[a], lo, width))
        else:
            b = rows_count + a
            jobs.append(gather_job(m, len(jobs), order, ins[b], outs[b], lo, width))
    hooks = []
    if attends:
        ready = max(i for i, entry in enumerate(plan) if entry[0]) + 3 * GATHER_SPACING
        parts = attention_parts(m, queries, outs[0], outs[1], results, refs[3:])
        step = max(1, (len(plan) + 2 * GATHER_SPACING - ready) // (len(parts) - 1))
        hooks = [(1, parts[0])] + [(ready + i * step, part) for i, part in enumerate(parts[1:])]
    run_jobs(jobs, GATHER_SPACING, hooks)
    m.drain()


def gather(token_rows, shards, identity, queries=None):
    n_f, n_s = lax.axis_size("fsdp"), lax.axis_size("seq")
    groups = n_s // 4
    operands = list(token_rows) + list(shards)
    plan = plan_of(
        [block.shape for block in token_rows],
        [shard.shape for shard in shards],
        GATHER_BYTES,
        4,
        8,
        0.0,
        MIX,
    )
    attends = queries is not None
    out_shape = [
        jax.ShapeDtypeStruct((groups, 2, 2) + block.shape, block.dtype) for block in token_rows
    ] + [
        jax.ShapeDtypeStruct((n_f, groups, 2, 2) + shard.shape, shard.dtype) for shard in shards
    ]
    in_specs = [pl.BlockSpec(memory_space=pltpu.VMEM)] * len(operands)
    out_specs = [pl.BlockSpec(memory_space=pltpu.VMEM)] * len(token_rows) + [
        pl.BlockSpec(memory_space=pltpu.HBM)
    ] * len(shards)
    scratch = [
        pltpu.SemaphoreType.DMA((len(plan), groups + 4)),
        pltpu.SemaphoreType.DMA((len(plan), groups + 4)),
        pltpu.SemaphoreType.DMA((len(plan),)),
    ]
    if attends:
        tokens, columns = queries[1].shape
        rows = tokens * HEADS
        in_specs += [pl.BlockSpec(memory_space=pltpu.SMEM)]
        in_specs += [pl.BlockSpec(memory_space=pltpu.VMEM)] * 3
        out_shape += [
            jax.ShapeDtypeStruct((rows, HEAD_DIM), F32),
            jax.ShapeDtypeStruct((tokens, columns), BF16),
            jax.ShapeDtypeStruct((1, rows), F32),
            jax.ShapeDtypeStruct((rows, HEAD_DIM), BF16),
        ]
        out_specs += [pl.BlockSpec(memory_space=pltpu.VMEM)] * 4
        scratch += [pltpu.VMEM((rows, 1), F32), pltpu.VMEM((rows, 1), F32)]
    results = pl.pallas_call(
        partial(gather_kernel, groups, plan, len(token_rows), len(operands), attends),
        out_shape=out_shape,
        in_specs=in_specs,
        out_specs=out_specs,
        scratch_shapes=scratch,
        compiler_params=pltpu.CompilerParams(
            collective_id=identity, has_side_effects=True, vmem_limit_bytes=VMEM_LIMIT
        ),
        name=f"gather_{identity}",
    )(*operands, *(queries if attends else ()))
    whole = [
        result.reshape(-1, block.shape[1]) for result, block in zip(results, operands)
    ]
    return whole + list(results[len(operands) :])


def scatter_job(m, job, order, source, out, lo, width, buffers):
    groups, f, z, y, c = m.groups, m.f, m.z, m.y, m.c
    columns = slice(lo, lo + width)
    every = slice(None)
    held, from_core, from_first, from_second, from_z = buffers

    def half(core):
        return source.at[:, :, :, core, :, columns]

    def add(into, other):
        into[...] = into[...] + other[...]

    def each(step):
        def part(g, carry):
            step(g)
            return carry

        lax.fori_loop(0, groups, part, 0)

    def begin():
        m.start(half(1 - c), from_core, job, 0, m.core)
        pltpu.make_async_copy(half(c), held, m.local.at[job]).start()

    def first():
        pltpu.make_async_copy(half(c), held, m.local.at[job]).wait()
        m.arrived(from_core, job, 0)
        if order == "xy":
            def pair(side):
                def step(g):
                    for k in range(2):
                        add(held.at[side, g, k], from_core.at[side, g, k])
                return step

            each(pair(1 - f))
            m.start(held.at[1 - f], from_first, job, 1, m.across["x"])
            each(pair(f))
        else:
            def pair(side):
                def step(g):
                    for k in range(2):
                        add(held.at[k, g, side], from_core.at[k, g, side])
                return step

            each(pair(1 - y))
            m.start(held.at[:, :, 1 - y], from_first, job, 1, m.across["y"])
            each(pair(y))

    def second():
        m.arrived(from_first, job, 1)
        if order == "xy":
            def side(k):
                return lambda g: add(held.at[f, g, k], from_first.at[g, k])

            each(side(1 - y))
            m.start(held.at[f, :, 1 - y], from_second, job, 2, m.across["y"])
            each(side(y))
        else:
            def side(k):
                return lambda g: add(held.at[k, g, y], from_first.at[k, g])

            each(side(1 - f))
            m.start(held.at[1 - f, :, y], from_second, job, 2, m.across["x"])
            each(side(f))

    def third():
        m.arrived(from_second, job, 2)
        each(lambda g: add(held.at[f, g, y], from_second.at[g]))
        for d in range(1, groups):
            there = lax.rem(z + d, groups)
            m.start(held.at[f, there, y], from_z.at[d - 1], job, 2 + d, m.along_z(d))

    def last():
        total = held[f, z, y].astype(F32)
        for d in range(1, groups):
            m.arrived(from_z.at[d - 1], job, 2 + d)
            total = total + from_z[d - 1].astype(F32)
        out[:, columns] = total

    return [begin, first, second, third, last]


def scatter_rows_job(m, job, source, out, lo, width, buffers):
    groups, z, y, c = m.groups, m.z, m.y, m.c
    columns = slice(lo, lo + width)
    held, from_core, from_y, from_z = buffers

    def half(core):
        return source.at[:, :, core, :, columns]

    def add(into, other):
        into[...] = into[...] + other[...]

    def each(step):
        def part(g, carry):
            step(g)
            return carry

        lax.fori_loop(0, groups, part, 0)

    def begin():
        m.start(half(1 - c), from_core, job, 0, m.core)
        pltpu.make_async_copy(half(c), held, m.local.at[job]).start()

    def first():
        pltpu.make_async_copy(half(c), held, m.local.at[job]).wait()
        m.arrived(from_core, job, 0)
        each(lambda g: add(held.at[g, 1 - y], from_core.at[g, 1 - y]))
        m.start(held.at[:, 1 - y], from_y, job, 1, m.across["y"])
        each(lambda g: add(held.at[g, y], from_core.at[g, y]))

    def second():
        m.arrived(from_y, job, 1)
        each(lambda g: add(held.at[g, y], from_y.at[g]))
        for d in range(1, groups):
            there = lax.rem(z + d, groups)
            m.start(held.at[there, y], from_z.at[d - 1], job, 2 + d, m.along_z(d))

    def last():
        total = held[z, y].astype(F32)
        for d in range(1, groups):
            m.arrived(from_z.at[d - 1], job, 2 + d)
            total = total + from_z[d - 1].astype(F32)
        out[:, columns] = total

    return [begin, first, second, last]


def scatter_kernel(groups, plan, rows_count, count, fused, *refs):
    ins, refs = refs[:count], refs[count:]
    operands, refs = (refs[:9], refs[9:]) if fused else ((), refs)
    total = count + rows_count if fused else count
    outs, refs = refs[:total], refs[total:]
    query_grad, refs = (refs[0], refs[1:]) if fused else (None, refs)
    (send, recv, local), scratch = refs[:3], list(refs[3:])
    greet(groups, True)
    m = Mover(groups, send, recv, local)
    hooks = []
    if fused:
        row_sources, scratch = [scratch[0]], scratch[1:]
        parts = backward_parts(m, operands, row_sources[0], query_grad, scratch[:4])
        scratch = scratch[4:]
        early = min(i for i, entry in enumerate(plan) if entry[0])
        step = max(1, (early - 2) // len(parts))
        hooks = [(1 + i * step, part) for i, part in enumerate(parts)]
        sources = row_sources + list(ins)
    else:
        sources = ins
    jobs = []
    for is_rows, a, lo, width, order in plan:
        if is_rows:
            buffers, scratch = scratch[:4], scratch[4:]
            jobs.append(scatter_rows_job(m, len(jobs), sources[a], outs[a], lo, width, buffers))
        else:
            buffers, scratch = scratch[:5], scratch[5:]
            b = rows_count + a
            jobs.append(scatter_job(m, len(jobs), order, sources[b], outs[b], lo, width, buffers))
    run_jobs(jobs, SCATTER_SPACING, hooks)
    m.drain()


def scatter(token_rows, partials, identity, backward=None):
    n_f, n_s = lax.axis_size("fsdp"), lax.axis_size("seq")
    groups = n_s // 4
    fused = backward is not None
    if fused:
        tokens = backward[2].shape[0]
        row_blocks = [(tokens, 2 * HEAD_DIM)]
    else:
        row_blocks = [(p.shape[0] // n_s, p.shape[1]) for p in token_rows]
    blocks = [(p.shape[0] // (n_f * n_s), p.shape[1]) for p in partials]
    begin, end = (0.45, 0.85) if fused else (0.0, MIX)
    plan = plan_of(row_blocks, blocks, SCATTER_BYTES, 8, 4, begin, end)
    scratch = []
    if fused:
        rows = tokens * HEADS
        scratch += [
            pltpu.VMEM((groups, 2, 2, tokens, 2 * HEAD_DIM), BF16),
            pltpu.VMEM((rows, HEAD_DIM), BF16),
            pltpu.VMEM((rows, HEAD_DIM), F32),
            pltpu.VMEM((1, rows), F32),
            pltpu.VMEM((4 * tokens, 2 * HEAD_DIM), F32),
        ]
    for is_rows, a, _, width, order in plan:
        if is_rows:
            block = (row_blocks[a][0], width)
            scratch += [
                pltpu.VMEM((groups, 2) + block, BF16),
                pltpu.VMEM((groups, 2) + block, BF16),
                pltpu.VMEM((groups,) + block, BF16),
                pltpu.VMEM((groups - 1,) + block, BF16),
            ]
        else:
            block = (blocks[a][0], width)
            scratch += [
                pltpu.VMEM((n_f, groups, 2) + block, BF16),
                pltpu.VMEM((n_f, groups, 2) + block, BF16),
                pltpu.VMEM(((groups, 2) if order == "xy" else (n_f, groups)) + block, BF16),
                pltpu.VMEM((groups,) + block, BF16),
                pltpu.VMEM((groups - 1,) + block, BF16),
            ]
    operands = [p.reshape((groups, 2, 2) + b) for p, b in zip(token_rows, row_blocks)]
    operands += [p.reshape((n_f, groups, 2, 2) + b) for p, b in zip(partials, blocks)]
    in_specs = [pl.BlockSpec(memory_space=pltpu.HBM)] * len(operands)
    out_shape = [jax.ShapeDtypeStruct(b, F32) for b in row_blocks + blocks]
    count = len(operands)
    if fused:
        operands += list(backward)
        in_specs += [pl.BlockSpec(memory_space=pltpu.SMEM)]
        in_specs += [pl.BlockSpec(memory_space=pltpu.VMEM)] * (len(backward) - 1)
        out_shape += [jax.ShapeDtypeStruct((tokens, HEADS * HEAD_DIM), BF16)]
    return pl.pallas_call(
        partial(scatter_kernel, groups, plan, len(row_blocks), count, fused),
        out_shape=out_shape,
        in_specs=in_specs,
        out_specs=[pl.BlockSpec(memory_space=pltpu.VMEM)] * len(out_shape),
        scratch_shapes=[
            pltpu.SemaphoreType.DMA((len(plan), groups + 2)),
            pltpu.SemaphoreType.DMA((len(plan), groups + 2)),
            pltpu.SemaphoreType.DMA((len(plan),)),
        ]
        + scratch,
        compiler_params=pltpu.CompilerParams(
            collective_id=identity, has_side_effects=True, vmem_limit_bytes=VMEM_LIMIT
        ),
        name=f"scatter_{identity}",
    )(*operands)


def finish_kernel(cuts, count, *refs):
    total = len(cuts)
    ins, outs = refs[:count], refs[count : count + total]
    staged, sems = refs[count + total : count + 2 * total], refs[count + 2 * total]
    for i, (a, rows, lo, width) in enumerate(cuts):
        staged[i][...] = ins[a][0:rows, lo : lo + width]
    for i in range(total):
        pltpu.make_async_copy(staged[i], outs[i], sems.at[i]).start()
    for i in range(total):
        pltpu.make_async_copy(staged[i], outs[i], sems.at[i]).wait()


def finish(sums, cuts):
    shapes = [(rows, width) for _, rows, _, width in cuts]
    return pl.pallas_call(
        partial(finish_kernel, tuple(cuts), len(sums)),
        out_shape=[jax.ShapeDtypeStruct(shape, F32) for shape in shapes],
        in_specs=[pl.BlockSpec(memory_space=pltpu.VMEM)] * len(sums),
        out_specs=[pl.BlockSpec(memory_space=pltpu.HBM)] * len(cuts),
        scratch_shapes=[pltpu.VMEM(shape, F32) for shape in shapes]
        + [pltpu.SemaphoreType.DMA((len(cuts),))],
        compiler_params=pltpu.CompilerParams(vmem_limit_bytes=VMEM_LIMIT),
        name="finish",
    )(*sums)


def as_row(column):
    return jnp.transpose(jnp.broadcast_to(column, (column.shape[0], 128)))[0:1, :]


def attention_parts(m, queries, keys, values, results, scratch):
    valid_ref, query_ref, cosine, sine = queries
    out_ref, low_ref, norm_ref, stacked = results
    peak, total = scratch
    tokens = query_ref.shape[0]
    half = HEAD_DIM // 2
    span = 4 * tokens
    scale = HEAD_DIM ** (-0.5)
    start = lax.axis_index("seq") * tokens

    def begin():
        for h in range(HEADS):
            first = query_ref[:, h * HEAD_DIM : h * HEAD_DIM + half]
            second = query_ref[:, h * HEAD_DIM + half : (h + 1) * HEAD_DIM]
            at = slice(h * tokens, (h + 1) * tokens)
            stacked[at, :half] = (first * cosine[...] - second * sine[...]).astype(BF16)
            stacked[at, half:] = (second * cosine[...] + first * sine[...]).astype(BF16)
        peak[...] = jnp.full(peak.shape, -jnp.inf, F32)
        total[...] = jnp.zeros(total.shape, F32)
        out_ref[...] = jnp.zeros(out_ref.shape, F32)

    def block(i, carry):
        j, h = i // HEADS, lax.rem(i, HEADS)
        own = pl.ds(pl.multiple_of(h * tokens, tokens), tokens)
        raw = times_transposed(stacked[own, :], keys[j].reshape(span, HEAD_DIM)) * scale
        key_pos = j * span + lax.broadcasted_iota(jnp.int32, (tokens, span), 1)
        row_pos = start + lax.broadcasted_iota(jnp.int32, (tokens, span), 0)
        raw = jnp.where(key_pos <= jnp.minimum(row_pos, valid_ref[0] - 1), raw, -jnp.inf)
        old = peak[own, :]
        new = jnp.maximum(old, jnp.max(raw, axis=1, keepdims=True))
        shrink = jnp.exp(old - new)
        weights = jnp.exp(raw - new)
        total[own, :] = total[own, :] * shrink + jnp.sum(weights, axis=1, keepdims=True)
        out_ref[own, :] = out_ref[own, :] * shrink + matmul(
            weights.astype(BF16), values[j].reshape(span, HEAD_DIM)
        )
        peak[own, :] = new
        return carry

    count = (m.z + 1) * HEADS

    def some(part):
        def work():
            lax.fori_loop(
                count * part // ATTENTION_PARTS, count * (part + 1) // ATTENTION_PARTS, block, 0
            )

        return work

    def end():
        for h in range(HEADS):
            at = slice(h * tokens, (h + 1) * tokens)
            result = out_ref[at, :] / total[at, :]
            out_ref[at, :] = result
            low_ref[:, h * HEAD_DIM : (h + 1) * HEAD_DIM] = result.astype(BF16)
            norm_ref[0:1, at] = as_row(peak[at, :] + jnp.log(total[at, :]))

    return [begin] + [some(part) for part in range(ATTENTION_PARTS)] + [end]


def backward_parts(m, operands, kv_terms, gq_ref, scratch):
    valid_ref, stacked, grad_ref, attended, cosine, sine, key_ref, value_ref, norm_ref = operands
    grads, gathered, delta, sums = scratch
    tokens = grad_ref.shape[0]
    half = HEAD_DIM // 2
    span = 4 * tokens
    scale = HEAD_DIM ** (-0.5)
    start = lax.axis_index("seq") * tokens

    def begin():
        for h in range(HEADS):
            at = slice(h * tokens, (h + 1) * tokens)
            part = grad_ref[:, h * HEAD_DIM : (h + 1) * HEAD_DIM]
            grads[at, :] = part
            delta[0:1, at] = as_row(
                jnp.sum(part.astype(F32) * attended[at, :], axis=1, keepdims=True)
            )
        gathered[...] = jnp.zeros(gathered.shape, F32)

    def block(j, carry):
        sums[...] = jnp.zeros(sums.shape, F32)

        def head(h, carry):
            own = pl.ds(pl.multiple_of(h * tokens, tokens), tokens)
            raw = times_transposed(key_ref[j], stacked[own, :]) * scale
            soft = jnp.exp(raw - norm_ref[:, own])
            key_pos = j * span + lax.broadcasted_iota(jnp.int32, (span, tokens), 0)
            row_pos = start + lax.broadcasted_iota(jnp.int32, (span, tokens), 1)
            soft = jnp.where(key_pos <= jnp.minimum(row_pos, valid_ref[0] - 1), soft, 0.0)
            toward = times_transposed(value_ref[j], grads[own, :])
            pulled = (soft * (toward - delta[:, own])).astype(BF16)
            sums[:, HEAD_DIM:] += matmul(soft.astype(BF16), grads[own, :])
            sums[:, :HEAD_DIM] += matmul(pulled, stacked[own, :])
            gathered[own, :] += transposed_times(pulled, key_ref[j])
            return carry

        @pl.when(j <= m.z)
        def _():
            lax.fori_loop(0, HEADS, head, 0)

        kv_terms[j, :, :, :, HEAD_DIM:] = (
            sums[:, HEAD_DIM:].astype(BF16).reshape(2, 2, tokens, HEAD_DIM)
        )
        kv_terms[j, :, :, :, :HEAD_DIM] = (
            (sums[:, :HEAD_DIM] * scale).astype(BF16).reshape(2, 2, tokens, HEAD_DIM)
        )
        return carry

    def some(part):
        def work():
            if part == 0:
                begin()
            lax.fori_loop(
                m.groups * part // ATTENTION_PARTS, m.groups * (part + 1) // ATTENTION_PARTS, block, 0
            )
            if part == ATTENTION_PARTS - 1:
                end()

        return work

    def end():
        for h in range(HEADS):
            at = slice(h * tokens, (h + 1) * tokens)
            first = gathered[at, :half] * scale
            second = gathered[at, half:] * scale
            lo = h * HEAD_DIM
            gq_ref[:, lo : lo + half] = (first * cosine[...] + second * sine[...]).astype(BF16)
            gq_ref[:, lo + half : lo + HEAD_DIM] = (second * cosine[...] - first * sine[...]).astype(
                BF16
            )

    return [some(part) for part in range(ATTENTION_PARTS)]


def backward_kernel(
    span,
    bounds,
    stacked,
    grad_ref,
    attended,
    cosine,
    sine,
    key_ref,
    value_ref,
    norm_ref,
    gq_ref,
    gkv_ref,
    grads,
    gathered,
    delta,
    sums,
):
    tokens = grad_ref.shape[0]
    half = HEAD_DIM // 2
    scale = HEAD_DIM ** (-0.5)
    start, valid = bounds[0], bounds[1]
    for h in range(HEADS):
        at = slice(h * tokens, (h + 1) * tokens)
        part = grad_ref[:, h * HEAD_DIM : (h + 1) * HEAD_DIM]
        grads[at, :] = part
        delta[0:1, at] = as_row(
            jnp.sum(part.astype(F32) * attended[at, :], axis=1, keepdims=True)
        )
    gathered[...] = jnp.zeros(gathered.shape, F32)

    def block(j, masked):
        at = pl.multiple_of(j * span, span)
        here = pl.ds(at, span)
        sums[...] = jnp.zeros(sums.shape, F32)

        def head(h, carry):
            low = pl.multiple_of(h * tokens, tokens)
            own = pl.ds(low, tokens)
            raw = times_transposed(key_ref[here, :], stacked[own, :]) * scale
            soft = jnp.exp(raw - norm_ref[:, own])
            if masked:
                key_pos = at + lax.broadcasted_iota(jnp.int32, (span, tokens), 0)
                row_pos = start + lax.broadcasted_iota(jnp.int32, (span, tokens), 1)
                soft = jnp.where(key_pos <= jnp.minimum(row_pos, valid - 1), soft, 0.0)
            toward = times_transposed(value_ref[here, :], grads[own, :])
            pulled = (soft * (toward - delta[:, own])).astype(BF16)
            sums[:, HEAD_DIM:] += matmul(soft.astype(BF16), grads[own, :])
            sums[:, :HEAD_DIM] += matmul(pulled, stacked[own, :])
            gathered[own, :] += transposed_times(pulled, key_ref[here, :])
            return carry

        lax.fori_loop(0, HEADS, head, 0)
        gkv_ref[here, HEAD_DIM:] = sums[:, HEAD_DIM:].astype(BF16)
        gkv_ref[here, :HEAD_DIM] = (sums[:, :HEAD_DIM] * scale).astype(BF16)

    plain = jnp.minimum(start, valid) // span
    last = jnp.minimum(start + tokens, valid)
    every = jnp.where(start < valid, (last + span - 1) // span, 0)
    plain = jnp.minimum(plain, every)

    def free(j, carry):
        block(j, False)
        return carry

    def edge(j, carry):
        block(j, True)
        return carry

    def empty(j, carry):
        at = pl.multiple_of(j * span, span)
        gkv_ref[pl.ds(at, span), :] = jnp.zeros((span, 2 * HEAD_DIM), BF16)
        return carry

    lax.fori_loop(0, plain, free, 0)
    lax.fori_loop(plain, every, edge, 0)
    lax.fori_loop(every, key_ref.shape[0] // span, empty, 0)
    for h in range(HEADS):
        at = slice(h * tokens, (h + 1) * tokens)
        first = gathered[at, :half] * scale
        second = gathered[at, half:] * scale
        lo = h * HEAD_DIM
        gq_ref[:, lo : lo + half] = (first * cosine[...] + second * sine[...]).astype(BF16)
        gq_ref[:, lo + half : lo + HEAD_DIM] = (second * cosine[...] - first * sine[...]).astype(BF16)


def attention_backward(bounds, stacked, grad, attended, cosine, sine, keys, values, norm, span):
    tokens = grad.shape[0]
    rows = tokens * HEADS
    return pl.pallas_call(
        partial(backward_kernel, span),
        out_shape=[
            jax.ShapeDtypeStruct((tokens, HEADS * HEAD_DIM), BF16),
            jax.ShapeDtypeStruct((keys.shape[0], 2 * HEAD_DIM), BF16),
        ],
        in_specs=[pl.BlockSpec(memory_space=pltpu.SMEM)]
        + [pl.BlockSpec(memory_space=pltpu.VMEM)] * 8,
        out_specs=[pl.BlockSpec(memory_space=pltpu.VMEM)] * 2,
        scratch_shapes=[
            pltpu.VMEM((rows, HEAD_DIM), BF16),
            pltpu.VMEM((rows, HEAD_DIM), F32),
            pltpu.VMEM((1, rows), F32),
            pltpu.VMEM((span, 2 * HEAD_DIM), F32),
        ],
        compiler_params=pltpu.CompilerParams(vmem_limit_bytes=VMEM_LIMIT),
        name="attention_backward",
    )(bounds, stacked, grad, attended, cosine, sine, keys, values, norm)


def pack_kernel(cuts, gains, count, *refs):
    ins, gain_refs = refs[:count], refs[count : count + len(gains)]
    outs = refs[count + len(gains) :]
    for out in outs:
        out[...] = jnp.zeros(out.shape, BF16)
    for source, (target, lo) in zip(ins, cuts):
        outs[target][0 : source.shape[0], lo : lo + source.shape[1]] = source[...]
    for gain, target in zip(gain_refs, gains):
        rows = gain.shape[1]
        outs[target][rows : rows + 1, 0:rows] = gain[...]


def pack(groups_of_weights, gains, gain_targets):
    weights, cuts, shapes = [], [], []
    for target, (wide, members) in enumerate(groups_of_weights):
        lo = 0
        for member in members:
            weights.append(member)
            cuts.append((target, lo))
            lo += member.shape[1]
        shapes.append((wide, lo))
    return pl.pallas_call(
        partial(pack_kernel, tuple(cuts), tuple(gain_targets), len(weights)),
        out_shape=[jax.ShapeDtypeStruct(shape, BF16) for shape in shapes],
        in_specs=[pl.BlockSpec(memory_space=pltpu.VMEM)] * (len(weights) + len(gains)),
        out_specs=[pl.BlockSpec(memory_space=pltpu.VMEM)] * len(shapes),
        compiler_params=pltpu.CompilerParams(vmem_limit_bytes=VMEM_LIMIT),
        name="pack",
    )(*weights, *[gain[None] for gain in gains])


def gain_whole(gathered, rows):
    wide = padded_model_rows(rows)
    return gathered.reshape(-1, wide, gathered.shape[1])[:, rows, :rows].reshape(-1).astype(F32)


def with_gain(partial_sums, gain_grad, rows):
    wide = padded_model_rows(rows)
    blocks = partial_sums.reshape(-1, wide, partial_sums.shape[1])
    return blocks.at[:, rows, :rows].set(gain_grad.reshape(-1, rows).astype(BF16)).reshape(partial_sums.shape)


def per_device(
    hidden_in,
    cotangent,
    dataset_ids,
    mixing,
    pad_lengths,
    attention_gain,
    merged_projection,
    merged_adapter_in,
    query_adapter_out,
    keyval_adapter_out,
    output_projection,
    output_adapter_in,
    output_adapter_out,
    feedforward_gain,
    gate_up_weight,
    gate_up_adapter_in,
    gate_up_adapter_out,
    down_weight,
    down_adapter_in,
    down_adapter_out,
):
    tokens, width = hidden_in.shape
    query_width = HEADS * HEAD_DIM
    merged_width = query_width + 2 * HEAD_DIM
    model_rows = merged_projection.shape[0]
    rank_rows = query_adapter_out.shape[0]
    pair_rows = keyval_adapter_out.shape[0]
    out_rows = output_projection.shape[0]
    ff_rows = down_weight.shape[0]
    model_wide, rank_wide = padded_model_rows(model_rows), padded_rows(rank_rows)
    pair_wide, ff_wide = padded_rows(pair_rows), padded_rows(ff_rows)

    packed = pack(
        [
            (model_wide, [merged_projection, merged_adapter_in]),
            (model_wide, [gate_up_weight, gate_up_adapter_in]),
            (rank_wide, [query_adapter_out]),
            (pair_wide, [keyval_adapter_out]),
            (padded_rows(out_rows), [output_projection, output_adapter_in]),
            (rank_wide, [output_adapter_out]),
            (pair_wide, [gate_up_adapter_out]),
            (ff_wide, [down_weight, down_adapter_in]),
            (rank_wide, [down_adapter_out]),
        ],
        [attention_gain, feedforward_gain],
        [0, 1],
    )
    merged, lift_query, lift_keyval = gather([], [packed[0], packed[2], packed[3]], 0)
    gain_one = gain_whole(merged, model_rows)

    hidden = hidden_in.astype(F32)
    normed_one, norm_one_back = jax.vjp(rms_scale, hidden, gain_one)
    first_in = spread(normed_one.astype(BF16), model_rows, model_wide)
    projected = matmul(first_in, merged)
    lifted = projected[:, merged_width:].astype(BF16)
    lifted_query = spread(lifted[:, :RANK], rank_rows, rank_wide)
    lifted_pair = spread(lifted[:, RANK:], pair_rows, pair_wide)
    half_pair = lifted_pair.shape[1] // 2
    query_rows = projected[:, :query_width] + matmul(lifted_query, lift_query)
    key_rows = projected[:, query_width : query_width + HEAD_DIM] + matmul(
        lifted_pair[:, :half_pair], lift_keyval[:half_pair]
    )
    value_rows = projected[:, query_width + HEAD_DIM : merged_width] + matmul(
        lifted_pair[:, half_pair:], lift_keyval[half_pair:]
    )
    start_pos = lax.axis_index("seq") * tokens
    positions = start_pos + jnp.arange(tokens, dtype=jnp.int32)
    cosine_table, sine_table = rotary_tables(positions)
    keys_rot = rotate(key_rows, cosine_table, sine_table).astype(BF16)
    length = lax.axis_size("seq") * tokens
    valid_count = length - pad_lengths[0]
    span = min(1024, length)
    bounds = jnp.stack([start_pos, valid_count])
    (
        keys_all,
        values_all,
        out_full,
        lift_out,
        gate_up,
        lift_gate_up,
        down,
        lift_down,
        attended,
        attended_low,
        log_norm,
        query_rot,
    ) = gather(
        [keys_rot, value_rows.astype(BF16)],
        [packed[4], packed[5], packed[1], packed[6], packed[7], packed[8]],
        1,
        (valid_count.reshape(1), query_rows, cosine_table, sine_table),
    )
    gain_two = gain_whole(gate_up, model_rows)
    out_both = matmul(attended_low, out_full)
    lifted_out = spread(out_both[:, width:].astype(BF16), rank_rows, rank_wide)
    middle = hidden + (out_both[:, :width] + matmul(lifted_out, lift_out))

    normed_two, norm_two_back = jax.vjp(rms_scale, middle, gain_two)
    second_in = spread(normed_two.astype(BF16), model_rows, model_wide)
    pre_gate = matmul(second_in, gate_up)
    lifted_gate_up = spread(pre_gate[:, 2 * FF :].astype(BF16), pair_rows, pair_wide)
    half_gate = lifted_gate_up.shape[1] // 2
    gate_part = pre_gate[:, :FF] + matmul(lifted_gate_up[:, :half_gate], lift_gate_up[:half_gate])
    upper_part = pre_gate[:, FF : 2 * FF] + matmul(
        lifted_gate_up[:, half_gate:], lift_gate_up[half_gate:]
    )
    activated, gelu_back = jax.vjp(partial(jax.nn.gelu, approximate=True), gate_part)
    inner = spread((activated * upper_part).astype(BF16), ff_rows, ff_wide)
    down_both = matmul(inner, down)
    lifted_down = spread(down_both[:, width:].astype(BF16), rank_rows, rank_wide)
    output = middle + (down_both[:, :width] + matmul(lifted_down, lift_down))

    matches = dataset_ids[:, None] == jnp.arange(DATASETS, dtype=jnp.int32)[None, :]
    picked = jnp.sum(jnp.where(matches, mixing[None, :], 0.0), axis=1)
    row_weight = jnp.where(positions < valid_count, picked, 0.0)
    scaled = cotangent.astype(F32) * row_weight[:, None]

    grad_branch = scaled.astype(BF16)
    grad_lifted_down = collect(times_transposed(grad_branch, lift_down), rank_rows, rank_wide)
    grad_down = jnp.concatenate([grad_branch, grad_lifted_down.astype(BF16)], axis=1)
    grad_inner = collect(times_transposed(grad_down, down), ff_rows, ff_wide)
    grad_gate = gelu_back(grad_inner * upper_part)[0].astype(BF16)
    grad_upper = (grad_inner * activated).astype(BF16)
    grad_gate_up = jnp.concatenate(
        [
            grad_gate,
            grad_upper,
            collect(
                times_transposed(grad_gate, lift_gate_up[:half_gate]), pair_rows, pair_wide
            ).astype(BF16),
            collect(
                times_transposed(grad_upper, lift_gate_up[half_gate:]), pair_rows, pair_wide
            ).astype(BF16),
        ],
        axis=1,
    )
    grad_normed_two = collect(times_transposed(grad_gate_up, gate_up), model_rows, model_wide)
    grad_middle_norm, gain_two_grad = norm_two_back(grad_normed_two)
    grad_middle = scaled + grad_middle_norm

    grad_attn = grad_middle.astype(BF16)
    grad_lifted_out = collect(times_transposed(grad_attn, lift_out), rank_rows, rank_wide)
    grad_out = jnp.concatenate([grad_attn, grad_lifted_out.astype(BF16)], axis=1)
    grad_attention = times_transposed(grad_out, out_full).astype(BF16)
    gate_up_out_term = jnp.concatenate(
        [
            transposed_times(lifted_gate_up[:, :half_gate], grad_gate, BF16),
            transposed_times(lifted_gate_up[:, half_gate:], grad_upper, BF16),
        ],
        axis=0,
    )
    partials = [
        with_gain(transposed_times(second_in, grad_gate_up, BF16), gain_two_grad, model_rows),
        transposed_times(inner, grad_down, BF16),
        transposed_times(attended_low, grad_out, BF16),
        gate_up_out_term,
        transposed_times(lifted_out, grad_attn, BF16),
        transposed_times(lifted_down, grad_branch, BF16),
    ]
    if length * 2 * HEAD_DIM * 7 <= FUSED_BYTES:
        *sums, grad_query_low = scatter(
            [],
            partials,
            2,
            (
                valid_count.reshape(1),
                query_rot,
                grad_attention,
                attended,
                cosine_table,
                sine_table,
                keys_all.reshape(-1, 4 * tokens, HEAD_DIM),
                values_all.reshape(-1, 4 * tokens, HEAD_DIM),
                log_norm,
            ),
        )
    else:
        grad_query_low, kv_terms = attention_backward(
            bounds,
            query_rot,
            grad_attention,
            attended,
            cosine_table,
            sine_table,
            keys_all,
            values_all,
            log_norm,
            span,
        )
        sums = scatter([kv_terms], partials, 2)
    kv_summed, gate_up_sum, down_sum, out_sum, gate_up_out_sum, out_out_sum, down_out_sum = sums
    grad_keys = rotate(kv_summed[:, :HEAD_DIM], cosine_table, -sine_table)
    grad_keys_low = grad_keys.astype(BF16)
    grad_values_low = kv_summed[:, HEAD_DIM:].astype(BF16)
    grad_merged = jnp.concatenate(
        [
            grad_query_low,
            grad_keys_low,
            grad_values_low,
            collect(times_transposed(grad_query_low, lift_query), rank_rows, rank_wide).astype(BF16),
            collect(
                times_transposed(grad_keys_low, lift_keyval[:half_pair]), pair_rows, pair_wide
            ).astype(BF16),
            collect(
                times_transposed(grad_values_low, lift_keyval[half_pair:]), pair_rows, pair_wide
            ).astype(BF16),
        ],
        axis=1,
    )
    grad_normed_one = collect(times_transposed(grad_merged, merged), model_rows, model_wide)
    grad_hidden_norm, gain_one_grad = norm_one_back(grad_normed_one)
    hidden_grad = grad_middle + grad_hidden_norm

    keyval_term = jnp.concatenate(
        [
            transposed_times(lifted_pair[:, :half_pair], grad_keys_low, BF16),
            transposed_times(lifted_pair[:, half_pair:], grad_values_low, BF16),
        ],
        axis=0,
    )
    merged_sum, query_out_sum, keyval_sum = scatter(
        [],
        [
            with_gain(transposed_times(first_in, grad_merged, BF16), gain_one_grad, model_rows),
            transposed_times(lifted_query, grad_query_low, BF16),
            keyval_term,
        ],
        3,
    )
    grads = finish(
        [
            merged_sum,
            query_out_sum,
            keyval_sum,
            out_sum,
            out_out_sum,
            gate_up_sum,
            gate_up_out_sum,
            down_sum,
            down_out_sum,
        ],
        [
            (0, model_rows, 0, merged_width),
            (0, model_rows, merged_width, 3 * RANK),
            (1, rank_rows, 0, query_width),
            (2, pair_rows, 0, HEAD_DIM),
            (3, out_rows, 0, width),
            (3, out_rows, width, RANK),
            (4, rank_rows, 0, width),
            (5, model_rows, 0, 2 * FF),
            (5, model_rows, 2 * FF, 2 * RANK),
            (6, pair_rows, 0, FF),
            (7, ff_rows, 0, width),
            (7, ff_rows, width, RANK),
            (8, rank_rows, 0, width),
        ],
    )
    return (
        output.astype(BF16),
        hidden_grad.astype(BF16),
        merged_sum[model_rows, :model_rows],
        *grads[:7],
        gate_up_sum[model_rows, :model_rows],
        *grads[7:],
    )


def solution(mesh):
    rows, vector = P(AXES, None), P(AXES)
    return jax.shard_map(
        per_device,
        mesh=mesh,
        in_specs=(rows, rows, vector, P(), P("fsdp"), vector)
        + (rows,) * 7
        + (vector,)
        + (rows,) * 6,
        out_specs=(rows, rows, vector) + (rows,) * 7 + (vector,) + (rows,) * 6,
        check_vma=False,
    )
```

```python
from functools import partial

import jax
import jax.numpy as jnp
from jax import lax
from jax.experimental import pallas as pl
from jax.experimental.pallas import tpu as pltpu
from jax.sharding import PartitionSpec as P

HEADS = 4
HEAD_DIM = 256
FF = 2048
RANK = 256
DATASETS = 16
EPSILON = 1e-06
MESH = pl.DeviceIdType.MESH
VMEM_LIMIT = 60 * 1024 * 1024
AXES = ("fsdp", "seq")
BF16 = jnp.bfloat16
F32 = jnp.float32


def rms_scale(values, gain_vector):
    inverse = lax.rsqrt(jnp.mean(values * values, axis=-1, keepdims=True) + EPSILON)
    return values * inverse * gain_vector


def rotary_tables(positions):
    half_width = HEAD_DIM // 2
    inverse = 10000.0 ** (-2.0 * jnp.arange(half_width, dtype=F32) / HEAD_DIM)
    angles = positions.astype(F32)[:, None] * inverse[None, :]
    return (jnp.cos(angles), jnp.sin(angles))


def rotate(values, cosine_table, sine_table):
    half_width = values.shape[-1] // 2
    first = values[..., :half_width]
    second = values[..., half_width:]
    return jnp.concatenate(
        [first * cosine_table - second * sine_table, second * cosine_table + first * sine_table],
        axis=-1,
    )


def matmul(left_side, right_side):
    return jnp.dot(left_side, right_side, preferred_element_type=F32)


def times_transposed(left_side, right_side):
    return lax.dot_general(
        left_side, right_side, (((1,), (1,)), ((), ())), preferred_element_type=F32
    )


def transposed_times(left_side, right_side, out=F32):
    return lax.dot_general(
        left_side, right_side, (((0,), (0,)), ((), ())), preferred_element_type=F32
    ).astype(out)


def padded_rows(rows):
    return -(-rows // 8) * 8


def padded_model_rows(rows):
    return -(-(rows + 1) // 8) * 8


def selection(rows, wide, count):
    source = lax.broadcasted_iota(jnp.int32, (count * rows, count * wide), 0)
    target = lax.broadcasted_iota(jnp.int32, (count * rows, count * wide), 1)
    inside = target % wide
    return ((source == target // wide * rows + inside) & (inside < rows)).astype(BF16)


def spread(values, rows, wide):
    if wide == rows:
        return values
    return matmul(values, selection(rows, wide, values.shape[1] // rows)).astype(BF16)


def collect(values, rows, wide):
    if wide == rows:
        return values
    chosen = selection(rows, wide, values.shape[1] // wide)
    first = values.astype(BF16)
    rest = values - first.astype(F32)
    second = rest.astype(BF16)
    third = (rest - second.astype(F32)).astype(BF16)
    return (
        times_transposed(first, chosen)
        + times_transposed(second, chosen)
        + times_transposed(third, chosen)
    )


def place(groups):
    f = lax.axis_index("fsdp")
    s = lax.axis_index("seq")
    c = lax.rem(s, 2)
    y = lax.rem(s // 2, 2)
    z = s // 4
    return f, z, y, c


def device(f, z, y, c):
    return (f, (z * 2 + y) * 2 + c)


def greet(groups, both):
    f, z, y, c = place(groups)
    barrier = pltpu.get_barrier_semaphore()
    peers = [device(f, z, y, 1 - c), device(f, z, 1 - y, c)]
    if both:
        peers.append(device(1 - f, z, y, c))
    for d in range(1, groups):
        peers.append(device(f, lax.rem(z + d, groups), y, c))
    for peer in peers:
        pl.semaphore_signal(barrier, inc=1, device_id=peer, device_id_type=MESH)
    pl.semaphore_wait(barrier, len(peers))


def pieces(rows, columns, target):
    count = max(1, min(columns // 128, round(rows * columns * 2 / target)))
    edges = [round(columns // 128 * i / count) * 128 for i in range(count)] + [columns]
    return [(lo, hi - lo) for lo, hi in zip(edges[:-1], edges[1:])]


def balanced(entries, first, second):
    orders = []
    x = y = 0
    for is_rows, size in entries:
        if is_rows:
            orders.append("y")
            y += 4 * size
        elif max(x + first * size, y + second * size) <= max(x + second * size, y + first * size):
            orders.append("xy")
            x, y = x + first * size, y + second * size
        else:
            orders.append("yx")
            x, y = x + second * size, y + first * size
    return orders


def mixed(row_chunks, chunks, begin, end):
    step = (end - begin) * len(chunks) / max(1, len(row_chunks))
    keyed = [
        (begin * len(chunks) + i * step, 0, (True,) + chunk) for i, chunk in enumerate(row_chunks)
    ]
    keyed += [(float(i), 1, (False,) + chunk) for i, chunk in enumerate(chunks)]
    return [chunk for _, _, chunk in sorted(keyed, key=lambda entry: entry[:2])]


def run_jobs(jobs, spacing, hooks=()):
    depth = max(len(stages) for stages in jobs)
    for tick in range(len(jobs) + spacing * (depth - 1)):
        for stage in reversed(range(depth)):
            j = tick - spacing * stage
            if 0 <= j < len(jobs) and stage < len(jobs[j]):
                jobs[j][stage]()
        for at, work in hooks:
            if at == tick:
                work()


class Mover:
    def __init__(self, groups, send, recv, local):
        self.groups = groups
        self.send, self.recv, self.local = send, recv, local
        self.f, self.z, self.y, self.c = place(groups)
        f, z, y, c = self.f, self.z, self.y, self.c
        self.core = device(f, z, y, 1 - c)
        self.across = {"y": device(f, z, 1 - y, c), "x": device(1 - f, z, y, c)}
        self.started = []

    def along_z(self, d):
        return device(self.f, lax.rem(self.z + d, self.groups), self.y, self.c)

    def remote(self, src, dst, job, slot, peer):
        return pltpu.make_async_remote_copy(
            src_ref=src,
            dst_ref=dst,
            send_sem=self.send.at[job, slot],
            recv_sem=self.recv.at[job, slot],
            device_id=peer,
            device_id_type=MESH,
        )

    def start(self, src, dst, job, slot, peer):
        copy = self.remote(src, dst, job, slot, peer)
        copy.start()
        self.started.append(copy)

    def arrived(self, ref, job, slot):
        self.remote(ref, ref, job, slot, self.core).wait_recv()

    def drain(self):
        for copy in self.started:
            copy.wait_send()


def gather_job(m, job, order, source, whole, lo, width):
    groups, f, z, y, c = m.groups, m.f, m.z, m.y, m.c
    columns = slice(lo, lo + width)
    own = source.at[:, columns]

    def at(*index):
        return whole.at[index + (slice(None), columns)]

    every = slice(None)

    def begin():
        pltpu.make_async_copy(own, at(f, z, y, c), m.local.at[job]).start()
        for d in range(1, groups):
            m.start(own, at(f, z, y, c), job, d, m.along_z(d))

    def first():
        pltpu.make_async_copy(own, at(f, z, y, c), m.local.at[job]).wait()
        for d in range(1, groups):
            m.arrived(at(f, lax.rem(z + groups - d, groups), y, c), job, d)
        mine = at(f, every, y, c)
        m.start(mine, mine, job, 0, m.across[order[0]])
        m.start(mine, mine, job, groups, m.core)

    def second():
        if order == "yx":
            got, mine = at(f, every, 1 - y, c), at(f, every, every, c)
        else:
            got, mine = at(1 - f, every, y, c), at(every, every, y, c)
        m.arrived(got, job, 0)
        m.start(mine, mine, job, groups + 1, m.across[order[1]])
        m.start(got, got, job, groups + 2, m.core)

    def third():
        got = at(1 - f, every, every, c) if order == "yx" else at(every, every, 1 - y, c)
        m.arrived(got, job, groups + 1)
        m.start(got, got, job, groups + 3, m.core)

    def last():
        other = 1 - c
        m.arrived(at(f, every, y, other), job, groups)
        if order == "yx":
            m.arrived(at(f, every, 1 - y, other), job, groups + 2)
            m.arrived(at(1 - f, every, every, other), job, groups + 3)
        else:
            m.arrived(at(1 - f, every, y, other), job, groups + 2)
            m.arrived(at(every, every, 1 - y, other), job, groups + 3)

    return [begin, first, second, third, last]


def gather_rows_job(m, job, source, whole, lo, width):
    groups, z, y, c = m.groups, m.z, m.y, m.c
    columns = slice(lo, lo + width)
    own = source.at[:, columns]
    every = slice(None)

    def at(*index):
        return whole.at[index + (slice(None), columns)]

    def begin():
        pltpu.make_async_copy(own, at(z, y, c), m.local.at[job]).start()
        for d in range(1, groups):
            m.start(own, at(z, y, c), job, d, m.along_z(d))

    def first():
        pltpu.make_async_copy(own, at(z, y, c), m.local.at[job]).wait()
        for d in range(1, groups):
            m.arrived(at(lax.rem(z + groups - d, groups), y, c), job, d)
        mine = at(every, y, c)
        m.start(mine, mine, job, 0, m.across["y"])
        m.start(mine, mine, job, groups, m.core)

    def second():
        got = at(every, 1 - y, c)
        m.arrived(got, job, 0)
        m.start(got, got, job, groups + 1, m.core)

    def last():
        m.arrived(at(every, y, 1 - c), job, groups)
        m.arrived(at(every, 1 - y, 1 - c), job, groups + 1)

    return [begin, first, second, last]


MIX = 0.6
FUSED_BYTES = 24 * 1024 * 1024
ATTENTION_PARTS = 4
GATHER_PACE = (20 * 1024, 4)
GATHER_FEW_PACE = (12 * 1024, 5)
ROWS_BYTES = 32 * 1024
SCATTER_PACE = (20 * 1024, 4)
SCATTER_FEW_PACE = (10 * 1024, 4)


def plan_of(row_blocks, blocks, target, first, second, begin, end):
    row_cuts = [
        (a, lo, width)
        for a, (rows, columns) in enumerate(row_blocks)
        for lo, width in pieces(rows, columns, ROWS_BYTES)
    ]
    cuts = [
        (a, lo, width)
        for a, (rows, columns) in enumerate(blocks)
        for lo, width in pieces(rows, columns, target)
    ]
    chunks = mixed(row_cuts, cuts, begin, end)
    entries = [
        (is_rows, (row_blocks if is_rows else blocks)[a][0] * width) for is_rows, a, _, width in chunks
    ]
    orders = balanced(entries, first, second)
    return tuple(chunk + (order,) for chunk, order in zip(chunks, orders))


def gather_kernel(groups, plan, spacing, rows_count, count, attends, *refs):
    extra = 4 if attends else 0
    ins, refs = refs[:count], refs[count:]
    queries, refs = refs[:extra], refs[extra:]
    outs, refs = refs[:count], refs[count:]
    results, refs = refs[:extra], refs[extra:]
    send, recv, local = refs[:3]
    greet(groups, True)
    m = Mover(groups, send, recv, local)
    jobs = []
    for is_rows, a, lo, width, order in plan:
        if is_rows:
            jobs.append(gather_rows_job(m, len(jobs), ins[a], outs[a], lo, width))
        else:
            b = rows_count + a
            jobs.append(gather_job(m, len(jobs), order, ins[b], outs[b], lo, width))
    hooks = []
    if attends:
        ready = max(i for i, entry in enumerate(plan) if entry[0]) + 3 * spacing
        parts = attention_parts(m, queries, outs[0], outs[1], results, refs[3:])
        step = max(1, (len(plan) + 2 * spacing - ready) // (len(parts) - 1))
        hooks = [(1, parts[0])] + [(ready + i * step, part) for i, part in enumerate(parts[1:])]
    run_jobs(jobs, spacing, hooks)
    m.drain()


def gather(token_rows, shards, identity, queries=None):
    n_f, n_s = lax.axis_size("fsdp"), lax.axis_size("seq")
    groups = n_s // 4
    operands = list(token_rows) + list(shards)
    target, spacing = GATHER_PACE if token_rows else GATHER_FEW_PACE
    plan = plan_of(
        [block.shape for block in token_rows],
        [shard.shape for shard in shards],
        target,
        4,
        8,
        0.0,
        MIX,
    )
    attends = queries is not None
    out_shape = [
        jax.ShapeDtypeStruct((groups, 2, 2) + block.shape, block.dtype) for block in token_rows
    ] + [
        jax.ShapeDtypeStruct((n_f, groups, 2, 2) + shard.shape, shard.dtype) for shard in shards
    ]
    in_specs = [pl.BlockSpec(memory_space=pltpu.VMEM)] * len(operands)
    out_specs = [pl.BlockSpec(memory_space=pltpu.VMEM)] * len(token_rows) + [
        pl.BlockSpec(memory_space=pltpu.HBM)
    ] * len(shards)
    scratch = [
        pltpu.SemaphoreType.DMA((len(plan), groups + 4)),
        pltpu.SemaphoreType.DMA((len(plan), groups + 4)),
        pltpu.SemaphoreType.DMA((len(plan),)),
    ]
    if attends:
        tokens, columns = queries[1].shape
        rows = tokens * HEADS
        in_specs += [pl.BlockSpec(memory_space=pltpu.SMEM)]
        in_specs += [pl.BlockSpec(memory_space=pltpu.VMEM)] * 3
        out_shape += [
            jax.ShapeDtypeStruct((rows, HEAD_DIM), F32),
            jax.ShapeDtypeStruct((tokens, columns), BF16),
            jax.ShapeDtypeStruct((1, rows), F32),
            jax.ShapeDtypeStruct((rows, HEAD_DIM), BF16),
        ]
        out_specs += [pl.BlockSpec(memory_space=pltpu.VMEM)] * 4
        scratch += [pltpu.VMEM((rows, 1), F32), pltpu.VMEM((rows, 1), F32)]
    results = pl.pallas_call(
        partial(gather_kernel, groups, plan, spacing, len(token_rows), len(operands), attends),
        out_shape=out_shape,
        in_specs=in_specs,
        out_specs=out_specs,
        scratch_shapes=scratch,
        compiler_params=pltpu.CompilerParams(
            collective_id=identity, has_side_effects=True, vmem_limit_bytes=VMEM_LIMIT
        ),
        name=f"gather_{identity}",
    )(*operands, *(queries if attends else ()))
    whole = [
        result.reshape(-1, block.shape[1]) for result, block in zip(results, operands)
    ]
    return whole + list(results[len(operands) :])


def scatter_job(m, job, order, source, out, lo, width, buffers):
    groups, f, z, y, c = m.groups, m.f, m.z, m.y, m.c
    columns = slice(lo, lo + width)
    every = slice(None)
    held, from_core, from_first, from_second, from_z = buffers

    def half(core):
        return source.at[:, :, :, core, :, columns]

    def add(into, other):
        into[...] = into[...] + other[...]

    def each(step):
        def part(g, carry):
            step(g)
            return carry

        lax.fori_loop(0, groups, part, 0)

    def begin():
        m.start(half(1 - c), from_core, job, 0, m.core)
        pltpu.make_async_copy(half(c), held, m.local.at[job]).start()

    def first():
        pltpu.make_async_copy(half(c), held, m.local.at[job]).wait()
        m.arrived(from_core, job, 0)
        if order == "xy":
            def pair(side):
                def step(g):
                    for k in range(2):
                        add(held.at[side, g, k], from_core.at[side, g, k])
                return step

            each(pair(1 - f))
            m.start(held.at[1 - f], from_first, job, 1, m.across["x"])
            each(pair(f))
        else:
            def pair(side):
                def step(g):
                    for k in range(2):
                        add(held.at[k, g, side], from_core.at[k, g, side])
                return step

            each(pair(1 - y))
            m.start(held.at[:, :, 1 - y], from_first, job, 1, m.across["y"])
            each(pair(y))

    def second():
        m.arrived(from_first, job, 1)
        if order == "xy":
            def side(k):
                return lambda g: add(held.at[f, g, k], from_first.at[g, k])

            each(side(1 - y))
            m.start(held.at[f, :, 1 - y], from_second, job, 2, m.across["y"])
            each(side(y))
        else:
            def side(k):
                return lambda g: add(held.at[k, g, y], from_first.at[k, g])

            each(side(1 - f))
            m.start(held.at[1 - f, :, y], from_second, job, 2, m.across["x"])
            each(side(f))

    def third():
        m.arrived(from_second, job, 2)
        each(lambda g: add(held.at[f, g, y], from_second.at[g]))
        for d in range(1, groups):
            there = lax.rem(z + d, groups)
            m.start(held.at[f, there, y], from_z.at[d - 1], job, 2 + d, m.along_z(d))

    def last():
        total = held[f, z, y].astype(F32)
        for d in range(1, groups):
            m.arrived(from_z.at[d - 1], job, 2 + d)
            total = total + from_z[d - 1].astype(F32)
        out[:, columns] = total

    return [begin, first, second, third, last]


def scatter_rows_job(m, job, source, out, lo, width, buffers):
    groups, z, y, c = m.groups, m.z, m.y, m.c
    columns = slice(lo, lo + width)
    held, from_core, from_y, from_z = buffers

    def half(core):
        return source.at[:, :, core, :, columns]

    def add(into, other):
        into[...] = into[...] + other[...]

    def each(step):
        def part(g, carry):
            step(g)
            return carry

        lax.fori_loop(0, groups, part, 0)

    def begin():
        m.start(half(1 - c), from_core, job, 0, m.core)
        pltpu.make_async_copy(half(c), held, m.local.at[job]).start()

    def first():
        pltpu.make_async_copy(half(c), held, m.local.at[job]).wait()
        m.arrived(from_core, job, 0)
        each(lambda g: add(held.at[g, 1 - y], from_core.at[g, 1 - y]))
        m.start(held.at[:, 1 - y], from_y, job, 1, m.across["y"])
        each(lambda g: add(held.at[g, y], from_core.at[g, y]))

    def second():
        m.arrived(from_y, job, 1)
        each(lambda g: add(held.at[g, y], from_y.at[g]))
        for d in range(1, groups):
            there = lax.rem(z + d, groups)
            m.start(held.at[there, y], from_z.at[d - 1], job, 2 + d, m.along_z(d))

    def last():
        total = held[z, y].astype(F32)
        for d in range(1, groups):
            m.arrived(from_z.at[d - 1], job, 2 + d)
            total = total + from_z[d - 1].astype(F32)
        out[:, columns] = total

    return [begin, first, second, last]


def scatter_kernel(groups, plan, spacing, rows_count, count, fused, *refs):
    ins, refs = refs[:count], refs[count:]
    operands, refs = (refs[:9], refs[9:]) if fused else ((), refs)
    total = count + rows_count if fused else count
    outs, refs = refs[:total], refs[total:]
    query_grad, refs = (refs[0], refs[1:]) if fused else (None, refs)
    (send, recv, local), scratch = refs[:3], list(refs[3:])
    greet(groups, True)
    m = Mover(groups, send, recv, local)
    hooks = []
    if fused:
        row_sources, scratch = [scratch[0]], scratch[1:]
        parts = backward_parts(m, operands, row_sources[0], query_grad, scratch[:4])
        scratch = scratch[4:]
        early = min(i for i, entry in enumerate(plan) if entry[0])
        step = max(1, (early - 2) // len(parts))
        hooks = [(1 + i * step, part) for i, part in enumerate(parts)]
        sources = row_sources + list(ins)
    else:
        sources = ins
    jobs = []
    for is_rows, a, lo, width, order in plan:
        if is_rows:
            buffers, scratch = scratch[:4], scratch[4:]
            jobs.append(scatter_rows_job(m, len(jobs), sources[a], outs[a], lo, width, buffers))
        else:
            buffers, scratch = scratch[:5], scratch[5:]
            b = rows_count + a
            jobs.append(scatter_job(m, len(jobs), order, sources[b], outs[b], lo, width, buffers))
    run_jobs(jobs, spacing, hooks)
    m.drain()


def scatter(token_rows, partials, identity, backward=None):
    n_f, n_s = lax.axis_size("fsdp"), lax.axis_size("seq")
    groups = n_s // 4
    fused = backward is not None
    if fused:
        tokens = backward[2].shape[0]
        row_blocks = [(tokens, 2 * HEAD_DIM)]
    else:
        row_blocks = [(p.shape[0] // n_s, p.shape[1]) for p in token_rows]
    blocks = [(p.shape[0] // (n_f * n_s), p.shape[1]) for p in partials]
    begin, end = (0.45, 0.85) if fused else (0.0, MIX)
    target, spacing = SCATTER_PACE if row_blocks else SCATTER_FEW_PACE
    plan = plan_of(row_blocks, blocks, target, 8, 4, begin, end)
    scratch = []
    if fused:
        rows = tokens * HEADS
        scratch += [
            pltpu.VMEM((groups, 2, 2, tokens, 2 * HEAD_DIM), BF16),
            pltpu.VMEM((rows, HEAD_DIM), BF16),
            pltpu.VMEM((rows, HEAD_DIM), F32),
            pltpu.VMEM((1, rows), F32),
            pltpu.VMEM((4 * tokens, 2 * HEAD_DIM), F32),
        ]
    for is_rows, a, _, width, order in plan:
        if is_rows:
            block = (row_blocks[a][0], width)
            scratch += [
                pltpu.VMEM((groups, 2) + block, BF16),
                pltpu.VMEM((groups, 2) + block, BF16),
                pltpu.VMEM((groups,) + block, BF16),
                pltpu.VMEM((groups - 1,) + block, BF16),
            ]
        else:
            block = (blocks[a][0], width)
            scratch += [
                pltpu.VMEM((n_f, groups, 2) + block, BF16),
                pltpu.VMEM((n_f, groups, 2) + block, BF16),
                pltpu.VMEM(((groups, 2) if order == "xy" else (n_f, groups)) + block, BF16),
                pltpu.VMEM((groups,) + block, BF16),
                pltpu.VMEM((groups - 1,) + block, BF16),
            ]
    operands = [p.reshape((groups, 2, 2) + b) for p, b in zip(token_rows, row_blocks)]
    operands += [p.reshape((n_f, groups, 2, 2) + b) for p, b in zip(partials, blocks)]
    in_specs = [pl.BlockSpec(memory_space=pl.ANY)] * len(operands)
    out_shape = [jax.ShapeDtypeStruct(b, F32) for b in row_blocks + blocks]
    count = len(operands)
    if fused:
        operands += list(backward)
        in_specs += [pl.BlockSpec(memory_space=pltpu.SMEM)]
        in_specs += [pl.BlockSpec(memory_space=pltpu.VMEM)] * (len(backward) - 1)
        out_shape += [jax.ShapeDtypeStruct((tokens, HEADS * HEAD_DIM), BF16)]
    return pl.pallas_call(
        partial(scatter_kernel, groups, plan, spacing, len(row_blocks), count, fused),
        out_shape=out_shape,
        in_specs=in_specs,
        out_specs=[pl.BlockSpec(memory_space=pltpu.VMEM)] * len(out_shape),
        scratch_shapes=[
            pltpu.SemaphoreType.DMA((len(plan), groups + 2)),
            pltpu.SemaphoreType.DMA((len(plan), groups + 2)),
            pltpu.SemaphoreType.DMA((len(plan),)),
        ]
        + scratch,
        compiler_params=pltpu.CompilerParams(
            collective_id=identity,
            has_side_effects=True,
            vmem_limit_bytes=VMEM_LIMIT if row_blocks else VMEM_LIMIT // 3,
        ),
        name=f"scatter_{identity}",
    )(*operands)


def finish_kernel(cuts, count, *refs):
    total = len(cuts)
    ins, outs = refs[:count], refs[count : count + total]
    staged, sems = refs[count + total : count + 2 * total], refs[count + 2 * total]
    for i, (a, rows, lo, width) in enumerate(cuts):
        staged[i][...] = ins[a][0:rows, lo : lo + width]
    for i in range(total):
        pltpu.make_async_copy(staged[i], outs[i], sems.at[i]).start()
    for i in range(total):
        pltpu.make_async_copy(staged[i], outs[i], sems.at[i]).wait()


def finish(sums, cuts):
    shapes = [(rows, width) for _, rows, _, width in cuts]
    return pl.pallas_call(
        partial(finish_kernel, tuple(cuts), len(sums)),
        out_shape=[jax.ShapeDtypeStruct(shape, F32) for shape in shapes],
        in_specs=[pl.BlockSpec(memory_space=pltpu.VMEM)] * len(sums),
        out_specs=[pl.BlockSpec(memory_space=pltpu.HBM)] * len(cuts),
        scratch_shapes=[pltpu.VMEM(shape, F32) for shape in shapes]
        + [pltpu.SemaphoreType.DMA((len(cuts),))],
        compiler_params=pltpu.CompilerParams(vmem_limit_bytes=VMEM_LIMIT),
        name="finish",
    )(*sums)


def as_row(column):
    return jnp.transpose(jnp.broadcast_to(column, (column.shape[0], 128)))[0:1, :]


def attention_parts(m, queries, keys, values, results, scratch):
    valid_ref, query_ref, cosine, sine = queries
    out_ref, low_ref, norm_ref, stacked = results
    peak, total = scratch
    tokens = query_ref.shape[0]
    half = HEAD_DIM // 2
    span = 4 * tokens
    scale = HEAD_DIM ** (-0.5)
    start = lax.axis_index("seq") * tokens

    def begin():
        for h in range(HEADS):
            first = query_ref[:, h * HEAD_DIM : h * HEAD_DIM + half]
            second = query_ref[:, h * HEAD_DIM + half : (h + 1) * HEAD_DIM]
            at = slice(h * tokens, (h + 1) * tokens)
            stacked[at, :half] = (first * cosine[...] - second * sine[...]).astype(BF16)
            stacked[at, half:] = (second * cosine[...] + first * sine[...]).astype(BF16)
        peak[...] = jnp.full(peak.shape, -jnp.inf, F32)
        total[...] = jnp.zeros(total.shape, F32)
        out_ref[...] = jnp.zeros(out_ref.shape, F32)

    def block(i, carry):
        j, h = i // HEADS, lax.rem(i, HEADS)
        own = pl.ds(pl.multiple_of(h * tokens, tokens), tokens)
        raw = times_transposed(stacked[own, :], keys[j].reshape(span, HEAD_DIM)) * scale
        key_pos = j * span + lax.broadcasted_iota(jnp.int32, (tokens, span), 1)
        row_pos = start + lax.broadcasted_iota(jnp.int32, (tokens, span), 0)
        raw = jnp.where(key_pos <= jnp.minimum(row_pos, valid_ref[0] - 1), raw, -jnp.inf)
        old = peak[own, :]
        new = jnp.maximum(old, jnp.max(raw, axis=1, keepdims=True))
        shrink = jnp.exp(old - new)
        weights = jnp.exp(raw - new)
        total[own, :] = total[own, :] * shrink + jnp.sum(weights, axis=1, keepdims=True)
        out_ref[own, :] = out_ref[own, :] * shrink + matmul(
            weights.astype(BF16), values[j].reshape(span, HEAD_DIM)
        )
        peak[own, :] = new
        return carry

    count = (m.z + 1) * HEADS

    def some(part):
        def work():
            lax.fori_loop(
                count * part // ATTENTION_PARTS, count * (part + 1) // ATTENTION_PARTS, block, 0
            )

        return work

    def end():
        for h in range(HEADS):
            at = slice(h * tokens, (h + 1) * tokens)
            result = out_ref[at, :] / total[at, :]
            out_ref[at, :] = result
            low_ref[:, h * HEAD_DIM : (h + 1) * HEAD_DIM] = result.astype(BF16)
            norm_ref[0:1, at] = as_row(peak[at, :] + jnp.log(total[at, :]))

    return [begin] + [some(part) for part in range(ATTENTION_PARTS)] + [end]


def backward_parts(m, operands, kv_terms, gq_ref, scratch):
    valid_ref, stacked, grad_ref, attended, cosine, sine, key_ref, value_ref, norm_ref = operands
    grads, gathered, delta, sums = scratch
    tokens = grad_ref.shape[0]
    half = HEAD_DIM // 2
    span = 4 * tokens
    scale = HEAD_DIM ** (-0.5)
    start = lax.axis_index("seq") * tokens

    def begin():
        for h in range(HEADS):
            at = slice(h * tokens, (h + 1) * tokens)
            part = grad_ref[:, h * HEAD_DIM : (h + 1) * HEAD_DIM]
            grads[at, :] = part
            delta[0:1, at] = as_row(
                jnp.sum(part.astype(F32) * attended[at, :], axis=1, keepdims=True)
            )
        gathered[...] = jnp.zeros(gathered.shape, F32)

    def block(j, carry):
        sums[...] = jnp.zeros(sums.shape, F32)

        def head(h, carry):
            own = pl.ds(pl.multiple_of(h * tokens, tokens), tokens)
            raw = times_transposed(key_ref[j], stacked[own, :]) * scale
            soft = jnp.exp(raw - norm_ref[:, own])
            key_pos = j * span + lax.broadcasted_iota(jnp.int32, (span, tokens), 0)
            row_pos = start + lax.broadcasted_iota(jnp.int32, (span, tokens), 1)
            soft = jnp.where(key_pos <= jnp.minimum(row_pos, valid_ref[0] - 1), soft, 0.0)
            toward = times_transposed(value_ref[j], grads[own, :])
            pulled = (soft * (toward - delta[:, own])).astype(BF16)
            sums[:, HEAD_DIM:] += matmul(soft.astype(BF16), grads[own, :])
            sums[:, :HEAD_DIM] += matmul(pulled, stacked[own, :])
            gathered[own, :] += transposed_times(pulled, key_ref[j])
            return carry

        @pl.when(j <= m.z)
        def _():
            lax.fori_loop(0, HEADS, head, 0)

        kv_terms[j, :, :, :, HEAD_DIM:] = (
            sums[:, HEAD_DIM:].astype(BF16).reshape(2, 2, tokens, HEAD_DIM)
        )
        kv_terms[j, :, :, :, :HEAD_DIM] = (
            (sums[:, :HEAD_DIM] * scale).astype(BF16).reshape(2, 2, tokens, HEAD_DIM)
        )
        return carry

    def some(part):
        def work():
            if part == 0:
                begin()
            lax.fori_loop(
                m.groups * part // ATTENTION_PARTS, m.groups * (part + 1) // ATTENTION_PARTS, block, 0
            )
            if part == ATTENTION_PARTS - 1:
                end()

        return work

    def end():
        for h in range(HEADS):
            at = slice(h * tokens, (h + 1) * tokens)
            first = gathered[at, :half] * scale
            second = gathered[at, half:] * scale
            lo = h * HEAD_DIM
            gq_ref[:, lo : lo + half] = (first * cosine[...] + second * sine[...]).astype(BF16)
            gq_ref[:, lo + half : lo + HEAD_DIM] = (second * cosine[...] - first * sine[...]).astype(
                BF16
            )

    return [some(part) for part in range(ATTENTION_PARTS)]


def backward_kernel(
    span,
    bounds,
    stacked,
    grad_ref,
    attended,
    cosine,
    sine,
    key_ref,
    value_ref,
    norm_ref,
    gq_ref,
    gkv_ref,
    grads,
    gathered,
    delta,
    sums,
):
    tokens = grad_ref.shape[0]
    half = HEAD_DIM // 2
    scale = HEAD_DIM ** (-0.5)
    start, valid = bounds[0], bounds[1]
    for h in range(HEADS):
        at = slice(h * tokens, (h + 1) * tokens)
        part = grad_ref[:, h * HEAD_DIM : (h + 1) * HEAD_DIM]
        grads[at, :] = part
        delta[0:1, at] = as_row(
            jnp.sum(part.astype(F32) * attended[at, :], axis=1, keepdims=True)
        )
    gathered[...] = jnp.zeros(gathered.shape, F32)

    def block(j, masked):
        at = pl.multiple_of(j * span, span)
        here = pl.ds(at, span)
        sums[...] = jnp.zeros(sums.shape, F32)

        def head(h, carry):
            low = pl.multiple_of(h * tokens, tokens)
            own = pl.ds(low, tokens)
            raw = times_transposed(key_ref[here, :], stacked[own, :]) * scale
            soft = jnp.exp(raw - norm_ref[:, own])
            if masked:
                key_pos = at + lax.broadcasted_iota(jnp.int32, (span, tokens), 0)
                row_pos = start + lax.broadcasted_iota(jnp.int32, (span, tokens), 1)
                soft = jnp.where(key_pos <= jnp.minimum(row_pos, valid - 1), soft, 0.0)
            toward = times_transposed(value_ref[here, :], grads[own, :])
            pulled = (soft * (toward - delta[:, own])).astype(BF16)
            sums[:, HEAD_DIM:] += matmul(soft.astype(BF16), grads[own, :])
            sums[:, :HEAD_DIM] += matmul(pulled, stacked[own, :])
            gathered[own, :] += transposed_times(pulled, key_ref[here, :])
            return carry

        lax.fori_loop(0, HEADS, head, 0)
        gkv_ref[here, HEAD_DIM:] = sums[:, HEAD_DIM:].astype(BF16)
        gkv_ref[here, :HEAD_DIM] = (sums[:, :HEAD_DIM] * scale).astype(BF16)

    plain = jnp.minimum(start, valid) // span
    last = jnp.minimum(start + tokens, valid)
    every = jnp.where(start < valid, (last + span - 1) // span, 0)
    plain = jnp.minimum(plain, every)

    def free(j, carry):
        block(j, False)
        return carry

    def edge(j, carry):
        block(j, True)
        return carry

    def empty(j, carry):
        at = pl.multiple_of(j * span, span)
        gkv_ref[pl.ds(at, span), :] = jnp.zeros((span, 2 * HEAD_DIM), BF16)
        return carry

    lax.fori_loop(0, plain, free, 0)
    lax.fori_loop(plain, every, edge, 0)
    lax.fori_loop(every, key_ref.shape[0] // span, empty, 0)
    for h in range(HEADS):
        at = slice(h * tokens, (h + 1) * tokens)
        first = gathered[at, :half] * scale
        second = gathered[at, half:] * scale
        lo = h * HEAD_DIM
        gq_ref[:, lo : lo + half] = (first * cosine[...] + second * sine[...]).astype(BF16)
        gq_ref[:, lo + half : lo + HEAD_DIM] = (second * cosine[...] - first * sine[...]).astype(BF16)


def attention_backward(bounds, stacked, grad, attended, cosine, sine, keys, values, norm, span):
    tokens = grad.shape[0]
    rows = tokens * HEADS
    return pl.pallas_call(
        partial(backward_kernel, span),
        out_shape=[
            jax.ShapeDtypeStruct((tokens, HEADS * HEAD_DIM), BF16),
            jax.ShapeDtypeStruct((keys.shape[0], 2 * HEAD_DIM), BF16),
        ],
        in_specs=[pl.BlockSpec(memory_space=pltpu.SMEM)]
        + [pl.BlockSpec(memory_space=pltpu.VMEM)] * 8,
        out_specs=[pl.BlockSpec(memory_space=pltpu.VMEM)] * 2,
        scratch_shapes=[
            pltpu.VMEM((rows, HEAD_DIM), BF16),
            pltpu.VMEM((rows, HEAD_DIM), F32),
            pltpu.VMEM((1, rows), F32),
            pltpu.VMEM((span, 2 * HEAD_DIM), F32),
        ],
        compiler_params=pltpu.CompilerParams(vmem_limit_bytes=VMEM_LIMIT),
        name="attention_backward",
    )(bounds, stacked, grad, attended, cosine, sine, keys, values, norm)


def pack_kernel(cuts, gains, count, *refs):
    ins, gain_refs = refs[:count], refs[count : count + len(gains)]
    outs = refs[count + len(gains) :]
    for out in outs:
        out[...] = jnp.zeros(out.shape, BF16)
    for source, (target, lo) in zip(ins, cuts):
        outs[target][0 : source.shape[0], lo : lo + source.shape[1]] = source[...]
    for gain, target in zip(gain_refs, gains):
        rows = gain.shape[1]
        outs[target][rows : rows + 1, 0:rows] = gain[...]


def pack(groups_of_weights, gains, gain_targets):
    weights, cuts, shapes = [], [], []
    for target, (wide, members) in enumerate(groups_of_weights):
        lo = 0
        for member in members:
            weights.append(member)
            cuts.append((target, lo))
            lo += member.shape[1]
        shapes.append((wide, lo))
    return pl.pallas_call(
        partial(pack_kernel, tuple(cuts), tuple(gain_targets), len(weights)),
        out_shape=[jax.ShapeDtypeStruct(shape, BF16) for shape in shapes],
        in_specs=[pl.BlockSpec(memory_space=pltpu.VMEM)] * (len(weights) + len(gains)),
        out_specs=[pl.BlockSpec(memory_space=pltpu.VMEM)] * len(shapes),
        compiler_params=pltpu.CompilerParams(vmem_limit_bytes=VMEM_LIMIT),
        name="pack",
    )(*weights, *[gain[None] for gain in gains])


def gain_whole(gathered, rows):
    wide = padded_model_rows(rows)
    return gathered.reshape(-1, wide, gathered.shape[1])[:, rows, :rows].reshape(-1).astype(F32)


def with_gain(partial_sums, gain_grad, rows):
    wide = padded_model_rows(rows)
    blocks = partial_sums.reshape(-1, wide, partial_sums.shape[1])
    return blocks.at[:, rows, :rows].set(gain_grad.reshape(-1, rows).astype(BF16)).reshape(partial_sums.shape)


def per_device(
    hidden_in,
    cotangent,
    dataset_ids,
    mixing,
    pad_lengths,
    attention_gain,
    merged_projection,
    merged_adapter_in,
    query_adapter_out,
    keyval_adapter_out,
    output_projection,
    output_adapter_in,
    output_adapter_out,
    feedforward_gain,
    gate_up_weight,
    gate_up_adapter_in,
    gate_up_adapter_out,
    down_weight,
    down_adapter_in,
    down_adapter_out,
):
    tokens, width = hidden_in.shape
    query_width = HEADS * HEAD_DIM
    merged_width = query_width + 2 * HEAD_DIM
    model_rows = merged_projection.shape[0]
    rank_rows = query_adapter_out.shape[0]
    pair_rows = keyval_adapter_out.shape[0]
    out_rows = output_projection.shape[0]
    ff_rows = down_weight.shape[0]
    model_wide, rank_wide = padded_model_rows(model_rows), padded_rows(rank_rows)
    pair_wide, ff_wide = padded_rows(pair_rows), padded_rows(ff_rows)

    packed = pack(
        [
            (model_wide, [merged_projection, merged_adapter_in]),
            (model_wide, [gate_up_weight, gate_up_adapter_in]),
            (rank_wide, [query_adapter_out]),
            (pair_wide, [keyval_adapter_out]),
            (padded_rows(out_rows), [output_projection, output_adapter_in]),
            (rank_wide, [output_adapter_out]),
            (pair_wide, [gate_up_adapter_out]),
            (ff_wide, [down_weight, down_adapter_in]),
            (rank_wide, [down_adapter_out]),
        ],
        [attention_gain, feedforward_gain],
        [0, 1],
    )
    merged, lift_query, lift_keyval = gather([], [packed[0], packed[2], packed[3]], 0)
    gain_one = gain_whole(merged, model_rows)

    hidden = hidden_in.astype(F32)
    normed_one, norm_one_back = jax.vjp(rms_scale, hidden, gain_one)
    first_in = spread(normed_one.astype(BF16), model_rows, model_wide)
    projected = matmul(first_in, merged)
    lifted = projected[:, merged_width:].astype(BF16)
    lifted_query = spread(lifted[:, :RANK], rank_rows, rank_wide)
    lifted_pair = spread(lifted[:, RANK:], pair_rows, pair_wide)
    half_pair = lifted_pair.shape[1] // 2
    query_rows = projected[:, :query_width] + matmul(lifted_query, lift_query)
    key_rows = projected[:, query_width : query_width + HEAD_DIM] + matmul(
        lifted_pair[:, :half_pair], lift_keyval[:half_pair]
    )
    value_rows = projected[:, query_width + HEAD_DIM : merged_width] + matmul(
        lifted_pair[:, half_pair:], lift_keyval[half_pair:]
    )
    start_pos = lax.axis_index("seq") * tokens
    positions = start_pos + jnp.arange(tokens, dtype=jnp.int32)
    cosine_table, sine_table = rotary_tables(positions)
    keys_rot = rotate(key_rows, cosine_table, sine_table).astype(BF16)
    length = lax.axis_size("seq") * tokens
    valid_count = length - pad_lengths[0]
    span = min(1024, length)
    bounds = jnp.stack([start_pos, valid_count])
    (
        keys_all,
        values_all,
        out_full,
        lift_out,
        gate_up,
        lift_gate_up,
        down,
        lift_down,
        attended,
        attended_low,
        log_norm,
        query_rot,
    ) = gather(
        [keys_rot, value_rows.astype(BF16)],
        [packed[4], packed[5], packed[1], packed[6], packed[7], packed[8]],
        1,
        (valid_count.reshape(1), query_rows, cosine_table, sine_table),
    )
    gain_two = gain_whole(gate_up, model_rows)
    out_both = matmul(attended_low, out_full)
    lifted_out = spread(out_both[:, width:].astype(BF16), rank_rows, rank_wide)
    middle = hidden + (out_both[:, :width] + matmul(lifted_out, lift_out))

    normed_two, norm_two_back = jax.vjp(rms_scale, middle, gain_two)
    second_in = spread(normed_two.astype(BF16), model_rows, model_wide)
    pre_gate = matmul(second_in, gate_up)
    lifted_gate_up = spread(pre_gate[:, 2 * FF :].astype(BF16), pair_rows, pair_wide)
    half_gate = lifted_gate_up.shape[1] // 2
    gate_part = pre_gate[:, :FF] + matmul(lifted_gate_up[:, :half_gate], lift_gate_up[:half_gate])
    upper_part = pre_gate[:, FF : 2 * FF] + matmul(
        lifted_gate_up[:, half_gate:], lift_gate_up[half_gate:]
    )
    activated, gelu_back = jax.vjp(partial(jax.nn.gelu, approximate=True), gate_part)
    inner = spread((activated * upper_part).astype(BF16), ff_rows, ff_wide)
    down_both = matmul(inner, down)
    lifted_down = spread(down_both[:, width:].astype(BF16), rank_rows, rank_wide)
    output = middle + (down_both[:, :width] + matmul(lifted_down, lift_down))

    matches = dataset_ids[:, None] == jnp.arange(DATASETS, dtype=jnp.int32)[None, :]
    picked = jnp.sum(jnp.where(matches, mixing[None, :], 0.0), axis=1)
    row_weight = jnp.where(positions < valid_count, picked, 0.0)
    scaled = cotangent.astype(F32) * row_weight[:, None]

    grad_branch = scaled.astype(BF16)
    grad_lifted_down = collect(times_transposed(grad_branch, lift_down), rank_rows, rank_wide)
    grad_down = jnp.concatenate([grad_branch, grad_lifted_down.astype(BF16)], axis=1)
    grad_inner = collect(times_transposed(grad_down, down), ff_rows, ff_wide)
    grad_gate = gelu_back(grad_inner * upper_part)[0].astype(BF16)
    grad_upper = (grad_inner * activated).astype(BF16)
    grad_gate_up = jnp.concatenate(
        [
            grad_gate,
            grad_upper,
            collect(
                times_transposed(grad_gate, lift_gate_up[:half_gate]), pair_rows, pair_wide
            ).astype(BF16),
            collect(
                times_transposed(grad_upper, lift_gate_up[half_gate:]), pair_rows, pair_wide
            ).astype(BF16),
        ],
        axis=1,
    )
    grad_normed_two = collect(times_transposed(grad_gate_up, gate_up), model_rows, model_wide)
    grad_middle_norm, gain_two_grad = norm_two_back(grad_normed_two)
    grad_middle = scaled + grad_middle_norm

    grad_attn = grad_middle.astype(BF16)
    grad_lifted_out = collect(times_transposed(grad_attn, lift_out), rank_rows, rank_wide)
    grad_out = jnp.concatenate([grad_attn, grad_lifted_out.astype(BF16)], axis=1)
    grad_attention = times_transposed(grad_out, out_full).astype(BF16)
    gate_up_out_term = jnp.concatenate(
        [
            transposed_times(lifted_gate_up[:, :half_gate], grad_gate, BF16),
            transposed_times(lifted_gate_up[:, half_gate:], grad_upper, BF16),
        ],
        axis=0,
    )
    partials = [
        with_gain(transposed_times(second_in, grad_gate_up, BF16), gain_two_grad, model_rows),
        transposed_times(inner, grad_down, BF16),
        transposed_times(attended_low, grad_out, BF16),
        gate_up_out_term,
        transposed_times(lifted_out, grad_attn, BF16),
        transposed_times(lifted_down, grad_branch, BF16),
    ]
    if length * 2 * HEAD_DIM * 7 <= FUSED_BYTES:
        *sums, grad_query_low = scatter(
            [],
            partials,
            2,
            (
                valid_count.reshape(1),
                query_rot,
                grad_attention,
                attended,
                cosine_table,
                sine_table,
                keys_all.reshape(-1, 4 * tokens, HEAD_DIM),
                values_all.reshape(-1, 4 * tokens, HEAD_DIM),
                log_norm,
            ),
        )
    else:
        grad_query_low, kv_terms = attention_backward(
            bounds,
            query_rot,
            grad_attention,
            attended,
            cosine_table,
            sine_table,
            keys_all,
            values_all,
            log_norm,
            span,
        )
        sums = scatter([kv_terms], partials, 2)
    kv_summed, gate_up_sum, down_sum, out_sum, gate_up_out_sum, out_out_sum, down_out_sum = sums
    grad_keys = rotate(kv_summed[:, :HEAD_DIM], cosine_table, -sine_table)
    grad_keys_low = grad_keys.astype(BF16)
    grad_values_low = kv_summed[:, HEAD_DIM:].astype(BF16)
    grad_merged = jnp.concatenate(
        [
            grad_query_low,
            grad_keys_low,
            grad_values_low,
            collect(times_transposed(grad_query_low, lift_query), rank_rows, rank_wide).astype(BF16),
            collect(
                times_transposed(grad_keys_low, lift_keyval[:half_pair]), pair_rows, pair_wide
            ).astype(BF16),
            collect(
                times_transposed(grad_values_low, lift_keyval[half_pair:]), pair_rows, pair_wide
            ).astype(BF16),
        ],
        axis=1,
    )
    grad_normed_one = collect(times_transposed(grad_merged, merged), model_rows, model_wide)
    grad_hidden_norm, gain_one_grad = norm_one_back(grad_normed_one)
    hidden_grad = grad_middle + grad_hidden_norm

    keyval_term = jnp.concatenate(
        [
            transposed_times(lifted_pair[:, :half_pair], grad_keys_low, BF16),
            transposed_times(lifted_pair[:, half_pair:], grad_values_low, BF16),
        ],
        axis=0,
    )
    merged_sum, query_out_sum, keyval_sum = scatter(
        [],
        [
            with_gain(transposed_times(first_in, grad_merged, BF16), gain_one_grad, model_rows),
            transposed_times(lifted_query, grad_query_low, BF16),
            keyval_term,
        ],
        3,
    )
    grads = finish(
        [
            merged_sum,
            query_out_sum,
            keyval_sum,
            out_sum,
            out_out_sum,
            gate_up_sum,
            gate_up_out_sum,
            down_sum,
            down_out_sum,
        ],
        [
            (0, model_rows, 0, merged_width),
            (0, model_rows, merged_width, 3 * RANK),
            (1, rank_rows, 0, query_width),
            (2, pair_rows, 0, HEAD_DIM),
            (3, out_rows, 0, width),
            (3, out_rows, width, RANK),
            (4, rank_rows, 0, width),
            (5, model_rows, 0, 2 * FF),
            (5, model_rows, 2 * FF, 2 * RANK),
            (6, pair_rows, 0, FF),
            (7, ff_rows, 0, width),
            (7, ff_rows, width, RANK),
            (8, rank_rows, 0, width),
        ],
    )
    return (
        output.astype(BF16),
        hidden_grad.astype(BF16),
        merged_sum[model_rows, :model_rows],
        *grads[:7],
        gate_up_sum[model_rows, :model_rows],
        *grads[7:],
    )


def solution(mesh):
    rows, vector = P(AXES, None), P(AXES)
    return jax.shard_map(
        per_device,
        mesh=mesh,
        in_specs=(rows, rows, vector, P(), P("fsdp"), vector)
        + (rows,) * 7
        + (vector,)
        + (rows,) * 6,
        out_specs=(rows, rows, vector) + (rows,) * 7 + (vector,) + (rows,) * 6,
        check_vma=False,
    )
```

```python
from functools import partial

import jax
import jax.numpy as jnp
from jax import lax
from jax.experimental import pallas as pl
from jax.experimental.pallas import tpu as pltpu
from jax.sharding import PartitionSpec as P

HEADS = 4
HEAD_DIM = 256
FF = 2048
RANK = 256
DATASETS = 16
EPSILON = 1e-06
MESH = pl.DeviceIdType.MESH
VMEM_LIMIT = 60 * 1024 * 1024
AXES = ("fsdp", "seq")
BF16 = jnp.bfloat16
F32 = jnp.float32


def rms_scale(values, gain_vector):
    inverse = lax.rsqrt(jnp.mean(values * values, axis=-1, keepdims=True) + EPSILON)
    return values * inverse * gain_vector


def rotary_tables(positions):
    half_width = HEAD_DIM // 2
    inverse = 10000.0 ** (-2.0 * jnp.arange(half_width, dtype=F32) / HEAD_DIM)
    angles = positions.astype(F32)[:, None] * inverse[None, :]
    return (jnp.cos(angles), jnp.sin(angles))


def rotate(values, cosine_table, sine_table):
    half_width = values.shape[-1] // 2
    first = values[..., :half_width]
    second = values[..., half_width:]
    return jnp.concatenate(
        [first * cosine_table - second * sine_table, second * cosine_table + first * sine_table],
        axis=-1,
    )


def matmul(left_side, right_side):
    return jnp.dot(left_side, right_side, preferred_element_type=F32)


def times_transposed(left_side, right_side):
    return lax.dot_general(
        left_side, right_side, (((1,), (1,)), ((), ())), preferred_element_type=F32
    )


def transposed_times(left_side, right_side, out=F32):
    return lax.dot_general(
        left_side, right_side, (((0,), (0,)), ((), ())), preferred_element_type=F32
    ).astype(out)


def padded_rows(rows):
    return -(-rows // 8) * 8


def padded_model_rows(rows):
    return -(-(rows + 1) // 8) * 8


def selection(rows, wide, count):
    source = lax.broadcasted_iota(jnp.int32, (count * rows, count * wide), 0)
    target = lax.broadcasted_iota(jnp.int32, (count * rows, count * wide), 1)
    inside = target % wide
    return ((source == target // wide * rows + inside) & (inside < rows)).astype(BF16)


def spread(values, rows, wide):
    if wide == rows:
        return values
    return matmul(values, selection(rows, wide, values.shape[1] // rows)).astype(BF16)


def collect(values, rows, wide):
    if wide == rows:
        return values
    chosen = selection(rows, wide, values.shape[1] // wide)
    first = values.astype(BF16)
    rest = values - first.astype(F32)
    second = rest.astype(BF16)
    third = (rest - second.astype(F32)).astype(BF16)
    return (
        times_transposed(first, chosen)
        + times_transposed(second, chosen)
        + times_transposed(third, chosen)
    )


def place(groups):
    f = lax.axis_index("fsdp")
    s = lax.axis_index("seq")
    c = lax.rem(s, 2)
    y = lax.rem(s // 2, 2)
    z = s // 4
    return f, z, y, c


def device(f, z, y, c):
    return (f, (z * 2 + y) * 2 + c)


def greet(groups, both):
    f, z, y, c = place(groups)
    barrier = pltpu.get_barrier_semaphore()
    peers = [device(f, z, y, 1 - c), device(f, z, 1 - y, c)]
    if both:
        peers.append(device(1 - f, z, y, c))
    for d in range(1, groups):
        peers.append(device(f, lax.rem(z + d, groups), y, c))
    for peer in peers:
        pl.semaphore_signal(barrier, inc=1, device_id=peer, device_id_type=MESH)
    pl.semaphore_wait(barrier, len(peers))


def pieces(rows, columns, target):
    count = max(1, min(columns // 128, round(rows * columns * 2 / target)))
    edges = [round(columns // 128 * i / count) * 128 for i in range(count)] + [columns]
    return [(lo, hi - lo) for lo, hi in zip(edges[:-1], edges[1:])]


def balanced(entries, first, second):
    orders = []
    x = y = 0
    for is_rows, size in entries:
        if is_rows:
            orders.append("y")
            y += 4 * size
        elif max(x + first * size, y + second * size) <= max(x + second * size, y + first * size):
            orders.append("xy")
            x, y = x + first * size, y + second * size
        else:
            orders.append("yx")
            x, y = x + second * size, y + first * size
    return orders


def mixed(row_chunks, chunks, begin, end):
    step = (end - begin) * len(chunks) / max(1, len(row_chunks))
    keyed = [
        (begin * len(chunks) + i * step, 0, (True,) + chunk) for i, chunk in enumerate(row_chunks)
    ]
    keyed += [(float(i), 1, (False,) + chunk) for i, chunk in enumerate(chunks)]
    return [chunk for _, _, chunk in sorted(keyed, key=lambda entry: entry[:2])]


def run_jobs(jobs, spacing, hooks=()):
    depth = max(len(stages) for stages in jobs)
    for tick in range(len(jobs) + spacing * (depth - 1)):
        for stage in reversed(range(depth)):
            j = tick - spacing * stage
            if 0 <= j < len(jobs) and stage < len(jobs[j]):
                jobs[j][stage]()
        for at, work in hooks:
            if at == tick:
                work()


class Mover:
    def __init__(self, groups, send, recv, local):
        self.groups = groups
        self.send, self.recv, self.local = send, recv, local
        self.f, self.z, self.y, self.c = place(groups)
        f, z, y, c = self.f, self.z, self.y, self.c
        self.core = device(f, z, y, 1 - c)
        self.across = {"y": device(f, z, 1 - y, c), "x": device(1 - f, z, y, c)}
        self.started = []

    def along_z(self, d):
        return device(self.f, lax.rem(self.z + d, self.groups), self.y, self.c)

    def remote(self, src, dst, job, slot, peer):
        return pltpu.make_async_remote_copy(
            src_ref=src,
            dst_ref=dst,
            send_sem=self.send.at[job, slot],
            recv_sem=self.recv.at[job, slot],
            device_id=peer,
            device_id_type=MESH,
        )

    def start(self, src, dst, job, slot, peer):
        copy = self.remote(src, dst, job, slot, peer)
        copy.start()
        self.started.append(copy)

    def arrived(self, ref, job, slot):
        self.remote(ref, ref, job, slot, self.core).wait_recv()

    def drain(self):
        for copy in self.started:
            copy.wait_send()


def gather_job(m, job, order, source, whole, lo, width):
    groups, f, z, y, c = m.groups, m.f, m.z, m.y, m.c
    columns = slice(lo, lo + width)
    own = source.at[:, columns]

    def at(*index):
        return whole.at[index + (slice(None), columns)]

    every = slice(None)

    def begin():
        pltpu.make_async_copy(own, at(f, z, y, c), m.local.at[job]).start()
        for d in range(1, groups):
            m.start(own, at(f, z, y, c), job, d, m.along_z(d))

    def first():
        pltpu.make_async_copy(own, at(f, z, y, c), m.local.at[job]).wait()
        for d in range(1, groups):
            m.arrived(at(f, lax.rem(z + groups - d, groups), y, c), job, d)
        mine = at(f, every, y, c)
        m.start(mine, mine, job, 0, m.across[order[0]])
        m.start(mine, mine, job, groups, m.core)

    def second():
        if order == "yx":
            got, mine = at(f, every, 1 - y, c), at(f, every, every, c)
        else:
            got, mine = at(1 - f, every, y, c), at(every, every, y, c)
        m.arrived(got, job, 0)
        m.start(mine, mine, job, groups + 1, m.across[order[1]])
        m.start(got, got, job, groups + 2, m.core)

    def third():
        got = at(1 - f, every, every, c) if order == "yx" else at(every, every, 1 - y, c)
        m.arrived(got, job, groups + 1)
        m.start(got, got, job, groups + 3, m.core)

    def last():
        other = 1 - c
        m.arrived(at(f, every, y, other), job, groups)
        if order == "yx":
            m.arrived(at(f, every, 1 - y, other), job, groups + 2)
            m.arrived(at(1 - f, every, every, other), job, groups + 3)
        else:
            m.arrived(at(1 - f, every, y, other), job, groups + 2)
            m.arrived(at(every, every, 1 - y, other), job, groups + 3)

    return [begin, first, second, third, last]


def gather_rows_job(m, job, source, whole, lo, width):
    groups, z, y, c = m.groups, m.z, m.y, m.c
    columns = slice(lo, lo + width)
    own = source.at[:, columns]
    every = slice(None)

    def at(*index):
        return whole.at[index + (slice(None), columns)]

    def begin():
        pltpu.make_async_copy(own, at(z, y, c), m.local.at[job]).start()
        for d in range(1, groups):
            m.start(own, at(z, y, c), job, d, m.along_z(d))

    def first():
        pltpu.make_async_copy(own, at(z, y, c), m.local.at[job]).wait()
        for d in range(1, groups):
            m.arrived(at(lax.rem(z + groups - d, groups), y, c), job, d)
        mine = at(every, y, c)
        m.start(mine, mine, job, 0, m.across["y"])
        m.start(mine, mine, job, groups, m.core)

    def second():
        got = at(every, 1 - y, c)
        m.arrived(got, job, 0)
        m.start(got, got, job, groups + 1, m.core)

    def last():
        m.arrived(at(every, y, 1 - c), job, groups)
        m.arrived(at(every, 1 - y, 1 - c), job, groups + 1)

    return [begin, first, second, last]


MIX = 0.6
FUSED_BYTES = 24 * 1024 * 1024
ATTENTION_PARTS = 4
GATHER_PACE = (20 * 1024, 4)
GATHER_FEW_PACE = (12 * 1024, 5)
ROWS_BYTES = 32 * 1024
SCATTER_PACE = (20 * 1024, 4)
SCATTER_FEW_PACE = (10 * 1024, 4)


def plan_of(row_blocks, blocks, target, first, second, begin, end):
    row_cuts = [
        (a, lo, width)
        for a, (rows, columns) in enumerate(row_blocks)
        for lo, width in pieces(rows, columns, ROWS_BYTES)
    ]
    cuts = [
        (a, lo, width)
        for a, (rows, columns) in enumerate(blocks)
        for lo, width in pieces(rows, columns, target)
    ]
    chunks = mixed(row_cuts, cuts, begin, end)
    entries = [
        (is_rows, (row_blocks if is_rows else blocks)[a][0] * width) for is_rows, a, _, width in chunks
    ]
    orders = balanced(entries, first, second)
    return tuple(chunk + (order,) for chunk, order in zip(chunks, orders))


def gather_kernel(groups, plan, spacing, rows_count, count, attends, *refs):
    extra = 4 if attends else 0
    ins, refs = refs[:count], refs[count:]
    queries, refs = refs[:extra], refs[extra:]
    outs, refs = refs[:count], refs[count:]
    results, refs = refs[:extra], refs[extra:]
    send, recv, local = refs[:3]
    greet(groups, True)
    m = Mover(groups, send, recv, local)
    jobs = []
    for is_rows, a, lo, width, order in plan:
        if is_rows:
            jobs.append(gather_rows_job(m, len(jobs), ins[a], outs[a], lo, width))
        else:
            b = rows_count + a
            jobs.append(gather_job(m, len(jobs), order, ins[b], outs[b], lo, width))
    hooks = []
    if attends:
        ready = max(i for i, entry in enumerate(plan) if entry[0]) + 3 * spacing
        parts = attention_parts(m, queries, outs[0], outs[1], results, refs[3:])
        step = max(1, (len(plan) + 2 * spacing - ready) // (len(parts) - 1))
        hooks = [(1, parts[0])] + [(ready + i * step, part) for i, part in enumerate(parts[1:])]
    run_jobs(jobs, spacing, hooks)
    m.drain()


def gather(token_rows, shards, identity, queries=None):
    n_f, n_s = lax.axis_size("fsdp"), lax.axis_size("seq")
    groups = n_s // 4
    operands = list(token_rows) + list(shards)
    target, spacing = GATHER_PACE if token_rows else GATHER_FEW_PACE
    plan = plan_of(
        [block.shape for block in token_rows],
        [shard.shape for shard in shards],
        target,
        4,
        8,
        0.0,
        MIX,
    )
    attends = queries is not None
    out_shape = [
        jax.ShapeDtypeStruct((groups, 2, 2) + block.shape, block.dtype) for block in token_rows
    ] + [
        jax.ShapeDtypeStruct((n_f, groups, 2, 2) + shard.shape, shard.dtype) for shard in shards
    ]
    in_specs = [pl.BlockSpec(memory_space=pltpu.VMEM)] * len(operands)
    out_specs = [pl.BlockSpec(memory_space=pltpu.VMEM)] * len(token_rows) + [
        pl.BlockSpec(memory_space=pltpu.HBM)
    ] * len(shards)
    scratch = [
        pltpu.SemaphoreType.DMA((len(plan), groups + 4)),
        pltpu.SemaphoreType.DMA((len(plan), groups + 4)),
        pltpu.SemaphoreType.DMA((len(plan),)),
    ]
    if attends:
        tokens, columns = queries[1].shape
        rows = tokens * HEADS
        in_specs += [pl.BlockSpec(memory_space=pltpu.SMEM)]
        in_specs += [pl.BlockSpec(memory_space=pltpu.VMEM)] * 3
        out_shape += [
            jax.ShapeDtypeStruct((rows, HEAD_DIM), F32),
            jax.ShapeDtypeStruct((tokens, columns), BF16),
            jax.ShapeDtypeStruct((1, rows), F32),
            jax.ShapeDtypeStruct((rows, HEAD_DIM), BF16),
        ]
        out_specs += [pl.BlockSpec(memory_space=pltpu.VMEM)] * 4
        scratch += [pltpu.VMEM((rows, 1), F32), pltpu.VMEM((rows, 1), F32)]
    results = pl.pallas_call(
        partial(gather_kernel, groups, plan, spacing, len(token_rows), len(operands), attends),
        out_shape=out_shape,
        in_specs=in_specs,
        out_specs=out_specs,
        scratch_shapes=scratch,
        compiler_params=pltpu.CompilerParams(
            collective_id=identity, has_side_effects=True, vmem_limit_bytes=VMEM_LIMIT
        ),
        name=f"gather_{identity}",
    )(*operands, *(queries if attends else ()))
    whole = [
        result.reshape(-1, block.shape[1]) for result, block in zip(results, operands)
    ]
    return whole + list(results[len(operands) :])


def scatter_job(m, job, order, source, out, lo, width, buffers):
    groups, f, z, y, c = m.groups, m.f, m.z, m.y, m.c
    columns = slice(lo, lo + width)
    every = slice(None)
    held, from_core, from_first, from_second, from_z = buffers

    def half(core):
        return source.at[:, :, :, core, :, columns]

    def add(into, other):
        into[...] = into[...] + other[...]

    def each(step):
        def part(g, carry):
            step(g)
            return carry

        lax.fori_loop(0, groups, part, 0)

    def begin():
        m.start(half(1 - c), from_core, job, 0, m.core)
        pltpu.make_async_copy(half(c), held, m.local.at[job]).start()

    def first():
        pltpu.make_async_copy(half(c), held, m.local.at[job]).wait()
        m.arrived(from_core, job, 0)
        if order == "xy":
            def pair(side):
                def step(g):
                    for k in range(2):
                        add(held.at[side, g, k], from_core.at[side, g, k])
                return step

            each(pair(1 - f))
            m.start(held.at[1 - f], from_first, job, 1, m.across["x"])
            each(pair(f))
        else:
            def pair(side):
                def step(g):
                    for k in range(2):
                        add(held.at[k, g, side], from_core.at[k, g, side])
                return step

            each(pair(1 - y))
            m.start(held.at[:, :, 1 - y], from_first, job, 1, m.across["y"])
            each(pair(y))

    def second():
        m.arrived(from_first, job, 1)
        if order == "xy":
            def side(k):
                return lambda g: add(held.at[f, g, k], from_first.at[g, k])

            each(side(1 - y))
            m.start(held.at[f, :, 1 - y], from_second, job, 2, m.across["y"])
            each(side(y))
        else:
            def side(k):
                return lambda g: add(held.at[k, g, y], from_first.at[k, g])

            each(side(1 - f))
            m.start(held.at[1 - f, :, y], from_second, job, 2, m.across["x"])
            each(side(f))

    def third():
        m.arrived(from_second, job, 2)
        each(lambda g: add(held.at[f, g, y], from_second.at[g]))
        for d in range(1, groups):
            there = lax.rem(z + d, groups)
            m.start(held.at[f, there, y], from_z.at[d - 1], job, 2 + d, m.along_z(d))

    def last():
        total = held[f, z, y].astype(F32)
        for d in range(1, groups):
            m.arrived(from_z.at[d - 1], job, 2 + d)
            total = total + from_z[d - 1].astype(F32)
        out[:, columns] = total

    return [begin, first, second, third, last]


def scatter_rows_job(m, job, source, out, lo, width, buffers):
    groups, z, y, c = m.groups, m.z, m.y, m.c
    columns = slice(lo, lo + width)
    held, from_core, from_y, from_z = buffers

    def half(core):
        return source.at[:, :, core, :, columns]

    def add(into, other):
        into[...] = into[...] + other[...]

    def each(step):
        def part(g, carry):
            step(g)
            return carry

        lax.fori_loop(0, groups, part, 0)

    def begin():
        m.start(half(1 - c), from_core, job, 0, m.core)
        pltpu.make_async_copy(half(c), held, m.local.at[job]).start()

    def first():
        pltpu.make_async_copy(half(c), held, m.local.at[job]).wait()
        m.arrived(from_core, job, 0)
        each(lambda g: add(held.at[g, 1 - y], from_core.at[g, 1 - y]))
        m.start(held.at[:, 1 - y], from_y, job, 1, m.across["y"])
        each(lambda g: add(held.at[g, y], from_core.at[g, y]))

    def second():
        m.arrived(from_y, job, 1)
        each(lambda g: add(held.at[g, y], from_y.at[g]))
        for d in range(1, groups):
            there = lax.rem(z + d, groups)
            m.start(held.at[there, y], from_z.at[d - 1], job, 2 + d, m.along_z(d))

    def last():
        total = held[z, y].astype(F32)
        for d in range(1, groups):
            m.arrived(from_z.at[d - 1], job, 2 + d)
            total = total + from_z[d - 1].astype(F32)
        out[:, columns] = total

    return [begin, first, second, last]


def scatter_kernel(groups, plan, spacing, rows_count, count, fused, *refs):
    ins, refs = refs[:count], refs[count:]
    operands, refs = (refs[:9], refs[9:]) if fused else ((), refs)
    total = count + rows_count if fused else count
    outs, refs = refs[:total], refs[total:]
    query_grad, refs = (refs[0], refs[1:]) if fused else (None, refs)
    (send, recv, local), scratch = refs[:3], list(refs[3:])
    greet(groups, True)
    m = Mover(groups, send, recv, local)
    hooks = []
    if fused:
        row_sources, scratch = [scratch[0]], scratch[1:]
        parts = backward_parts(m, operands, row_sources[0], query_grad, scratch[:4])
        scratch = scratch[4:]
        hooks = [(1 + i * 2, part) for i, part in enumerate(parts)]
        sources = row_sources + list(ins)
    else:
        sources = ins
    jobs = []
    for is_rows, a, lo, width, order in plan:
        if is_rows:
            buffers, scratch = scratch[:4], scratch[4:]
            jobs.append(scatter_rows_job(m, len(jobs), sources[a], outs[a], lo, width, buffers))
        else:
            buffers, scratch = scratch[:5], scratch[5:]
            b = rows_count + a
            jobs.append(scatter_job(m, len(jobs), order, sources[b], outs[b], lo, width, buffers))
    run_jobs(jobs, spacing, hooks)
    m.drain()


def scatter(token_rows, partials, identity, backward=None):
    n_f, n_s = lax.axis_size("fsdp"), lax.axis_size("seq")
    groups = n_s // 4
    fused = backward is not None
    if fused:
        tokens = backward[2].shape[0]
        row_blocks = [(tokens, 2 * HEAD_DIM)]
    else:
        row_blocks = [(p.shape[0] // n_s, p.shape[1]) for p in token_rows]
    blocks = [(p.shape[0] // (n_f * n_s), p.shape[1]) for p in partials]
    begin, end = (0.3, 0.8) if fused else (0.0, MIX)
    target, spacing = SCATTER_PACE if row_blocks else SCATTER_FEW_PACE
    plan = plan_of(row_blocks, blocks, target, 8, 4, begin, end)
    scratch = []
    if fused:
        rows = tokens * HEADS
        scratch += [
            pltpu.VMEM((groups, 2, 2, tokens, 2 * HEAD_DIM), BF16),
            pltpu.VMEM((rows, HEAD_DIM), BF16),
            pltpu.VMEM((rows, HEAD_DIM), F32),
            pltpu.VMEM((1, rows), F32),
            pltpu.VMEM((4 * tokens, 2 * HEAD_DIM), F32),
        ]
    for is_rows, a, _, width, order in plan:
        if is_rows:
            block = (row_blocks[a][0], width)
            scratch += [
                pltpu.VMEM((groups, 2) + block, BF16),
                pltpu.VMEM((groups, 2) + block, BF16),
                pltpu.VMEM((groups,) + block, BF16),
                pltpu.VMEM((groups - 1,) + block, BF16),
            ]
        else:
            block = (blocks[a][0], width)
            scratch += [
                pltpu.VMEM((n_f, groups, 2) + block, BF16),
                pltpu.VMEM((n_f, groups, 2) + block, BF16),
                pltpu.VMEM(((groups, 2) if order == "xy" else (n_f, groups)) + block, BF16),
                pltpu.VMEM((groups,) + block, BF16),
                pltpu.VMEM((groups - 1,) + block, BF16),
            ]
    operands = [p.reshape((groups, 2, 2) + b) for p, b in zip(token_rows, row_blocks)]
    operands += [p.reshape((n_f, groups, 2, 2) + b) for p, b in zip(partials, blocks)]
    in_specs = [pl.BlockSpec(memory_space=pl.ANY)] * len(operands)
    out_shape = [jax.ShapeDtypeStruct(b, F32) for b in row_blocks + blocks]
    count = len(operands)
    if fused:
        operands += list(backward)
        in_specs += [pl.BlockSpec(memory_space=pltpu.SMEM)]
        in_specs += [pl.BlockSpec(memory_space=pltpu.VMEM)] * (len(backward) - 1)
        out_shape += [jax.ShapeDtypeStruct((tokens, HEADS * HEAD_DIM), BF16)]
    return pl.pallas_call(
        partial(scatter_kernel, groups, plan, spacing, len(row_blocks), count, fused),
        out_shape=out_shape,
        in_specs=in_specs,
        out_specs=[pl.BlockSpec(memory_space=pltpu.VMEM)] * len(out_shape),
        scratch_shapes=[
            pltpu.SemaphoreType.DMA((len(plan), groups + 2)),
            pltpu.SemaphoreType.DMA((len(plan), groups + 2)),
            pltpu.SemaphoreType.DMA((len(plan),)),
        ]
        + scratch,
        compiler_params=pltpu.CompilerParams(
            collective_id=identity,
            has_side_effects=True,
            vmem_limit_bytes=VMEM_LIMIT if row_blocks else VMEM_LIMIT // 3,
        ),
        name=f"scatter_{identity}",
    )(*operands)


def finish_kernel(cuts, count, *refs):
    total = len(cuts)
    ins, outs = refs[:count], refs[count : count + total]
    staged, sems = refs[count + total : count + 2 * total], refs[count + 2 * total]
    for i, (a, rows, lo, width) in enumerate(cuts):
        staged[i][...] = ins[a][0:rows, lo : lo + width]
    for i in range(total):
        pltpu.make_async_copy(staged[i], outs[i], sems.at[i]).start()
    for i in range(total):
        pltpu.make_async_copy(staged[i], outs[i], sems.at[i]).wait()


def finish(sums, cuts):
    shapes = [(rows, width) for _, rows, _, width in cuts]
    return pl.pallas_call(
        partial(finish_kernel, tuple(cuts), len(sums)),
        out_shape=[jax.ShapeDtypeStruct(shape, F32) for shape in shapes],
        in_specs=[pl.BlockSpec(memory_space=pltpu.VMEM)] * len(sums),
        out_specs=[pl.BlockSpec(memory_space=pltpu.HBM)] * len(cuts),
        scratch_shapes=[pltpu.VMEM(shape, F32) for shape in shapes]
        + [pltpu.SemaphoreType.DMA((len(cuts),))],
        compiler_params=pltpu.CompilerParams(vmem_limit_bytes=VMEM_LIMIT),
        name="finish",
    )(*sums)


def as_row(column):
    return jnp.transpose(jnp.broadcast_to(column, (column.shape[0], 128)))[0:1, :]


def attention_parts(m, queries, keys, values, results, scratch):
    valid_ref, query_ref, cosine, sine = queries
    out_ref, low_ref, norm_ref, stacked = results
    peak, total = scratch
    tokens = query_ref.shape[0]
    half = HEAD_DIM // 2
    span = 4 * tokens
    scale = HEAD_DIM ** (-0.5)
    start = lax.axis_index("seq") * tokens

    def begin():
        for h in range(HEADS):
            first = query_ref[:, h * HEAD_DIM : h * HEAD_DIM + half]
            second = query_ref[:, h * HEAD_DIM + half : (h + 1) * HEAD_DIM]
            at = slice(h * tokens, (h + 1) * tokens)
            stacked[at, :half] = (first * cosine[...] - second * sine[...]).astype(BF16)
            stacked[at, half:] = (second * cosine[...] + first * sine[...]).astype(BF16)
        peak[...] = jnp.full(peak.shape, -jnp.inf, F32)
        total[...] = jnp.zeros(total.shape, F32)
        out_ref[...] = jnp.zeros(out_ref.shape, F32)

    def block(i, carry):
        j, h = i // HEADS, lax.rem(i, HEADS)
        own = pl.ds(pl.multiple_of(h * tokens, tokens), tokens)
        raw = times_transposed(stacked[own, :], keys[j].reshape(span, HEAD_DIM)) * scale
        key_pos = j * span + lax.broadcasted_iota(jnp.int32, (tokens, span), 1)
        row_pos = start + lax.broadcasted_iota(jnp.int32, (tokens, span), 0)
        raw = jnp.where(key_pos <= jnp.minimum(row_pos, valid_ref[0] - 1), raw, -jnp.inf)
        old = peak[own, :]
        new = jnp.maximum(old, jnp.max(raw, axis=1, keepdims=True))
        shrink = jnp.exp(old - new)
        weights = jnp.exp(raw - new)
        total[own, :] = total[own, :] * shrink + jnp.sum(weights, axis=1, keepdims=True)
        out_ref[own, :] = out_ref[own, :] * shrink + matmul(
            weights.astype(BF16), values[j].reshape(span, HEAD_DIM)
        )
        peak[own, :] = new
        return carry

    count = (m.z + 1) * HEADS

    def some(part):
        def work():
            lax.fori_loop(
                count * part // ATTENTION_PARTS, count * (part + 1) // ATTENTION_PARTS, block, 0
            )

        return work

    def end():
        for h in range(HEADS):
            at = slice(h * tokens, (h + 1) * tokens)
            result = out_ref[at, :] / total[at, :]
            out_ref[at, :] = result
            low_ref[:, h * HEAD_DIM : (h + 1) * HEAD_DIM] = result.astype(BF16)
            norm_ref[0:1, at] = as_row(peak[at, :] + jnp.log(total[at, :]))

    return [begin] + [some(part) for part in range(ATTENTION_PARTS)] + [end]


def backward_parts(m, operands, kv_terms, gq_ref, scratch):
    valid_ref, stacked, grad_ref, attended, cosine, sine, key_ref, value_ref, norm_ref = operands
    grads, gathered, delta, sums = scratch
    tokens = grad_ref.shape[0]
    half = HEAD_DIM // 2
    span = 4 * tokens
    scale = HEAD_DIM ** (-0.5)
    start = lax.axis_index("seq") * tokens

    def begin():
        for h in range(HEADS):
            at = slice(h * tokens, (h + 1) * tokens)
            part = grad_ref[:, h * HEAD_DIM : (h + 1) * HEAD_DIM]
            grads[at, :] = part
            delta[0:1, at] = as_row(
                jnp.sum(part.astype(F32) * attended[at, :], axis=1, keepdims=True)
            )
        gathered[...] = jnp.zeros(gathered.shape, F32)

    def block(j, carry):
        sums[...] = jnp.zeros(sums.shape, F32)

        def head(h, carry):
            own = pl.ds(pl.multiple_of(h * tokens, tokens), tokens)
            raw = times_transposed(key_ref[j], stacked[own, :]) * scale
            soft = jnp.exp(raw - norm_ref[:, own])
            key_pos = j * span + lax.broadcasted_iota(jnp.int32, (span, tokens), 0)
            row_pos = start + lax.broadcasted_iota(jnp.int32, (span, tokens), 1)
            soft = jnp.where(key_pos <= jnp.minimum(row_pos, valid_ref[0] - 1), soft, 0.0)
            toward = times_transposed(value_ref[j], grads[own, :])
            pulled = (soft * (toward - delta[:, own])).astype(BF16)
            sums[:, HEAD_DIM:] += matmul(soft.astype(BF16), grads[own, :])
            sums[:, :HEAD_DIM] += matmul(pulled, stacked[own, :])
            gathered[own, :] += transposed_times(pulled, key_ref[j])
            return carry

        @pl.when(j <= m.z)
        def _():
            lax.fori_loop(0, HEADS, head, 0)

        kv_terms[j, :, :, :, HEAD_DIM:] = (
            sums[:, HEAD_DIM:].astype(BF16).reshape(2, 2, tokens, HEAD_DIM)
        )
        kv_terms[j, :, :, :, :HEAD_DIM] = (
            (sums[:, :HEAD_DIM] * scale).astype(BF16).reshape(2, 2, tokens, HEAD_DIM)
        )
        return carry

    def some(part):
        def work():
            if part == 0:
                begin()
            lax.fori_loop(
                m.groups * part // ATTENTION_PARTS, m.groups * (part + 1) // ATTENTION_PARTS, block, 0
            )
            if part == ATTENTION_PARTS - 1:
                end()

        return work

    def end():
        for h in range(HEADS):
            at = slice(h * tokens, (h + 1) * tokens)
            first = gathered[at, :half] * scale
            second = gathered[at, half:] * scale
            lo = h * HEAD_DIM
            gq_ref[:, lo : lo + half] = (first * cosine[...] + second * sine[...]).astype(BF16)
            gq_ref[:, lo + half : lo + HEAD_DIM] = (second * cosine[...] - first * sine[...]).astype(
                BF16
            )

    return [some(part) for part in range(ATTENTION_PARTS)]


def backward_kernel(
    span,
    bounds,
    stacked,
    grad_ref,
    attended,
    cosine,
    sine,
    key_ref,
    value_ref,
    norm_ref,
    gq_ref,
    gkv_ref,
    grads,
    gathered,
    delta,
    sums,
):
    tokens = grad_ref.shape[0]
    half = HEAD_DIM // 2
    scale = HEAD_DIM ** (-0.5)
    start, valid = bounds[0], bounds[1]
    for h in range(HEADS):
        at = slice(h * tokens, (h + 1) * tokens)
        part = grad_ref[:, h * HEAD_DIM : (h + 1) * HEAD_DIM]
        grads[at, :] = part
        delta[0:1, at] = as_row(
            jnp.sum(part.astype(F32) * attended[at, :], axis=1, keepdims=True)
        )
    gathered[...] = jnp.zeros(gathered.shape, F32)

    def block(j, masked):
        at = pl.multiple_of(j * span, span)
        here = pl.ds(at, span)
        sums[...] = jnp.zeros(sums.shape, F32)

        def head(h, carry):
            low = pl.multiple_of(h * tokens, tokens)
            own = pl.ds(low, tokens)
            raw = times_transposed(key_ref[here, :], stacked[own, :]) * scale
            soft = jnp.exp(raw - norm_ref[:, own])
            if masked:
                key_pos = at + lax.broadcasted_iota(jnp.int32, (span, tokens), 0)
                row_pos = start + lax.broadcasted_iota(jnp.int32, (span, tokens), 1)
                soft = jnp.where(key_pos <= jnp.minimum(row_pos, valid - 1), soft, 0.0)
            toward = times_transposed(value_ref[here, :], grads[own, :])
            pulled = (soft * (toward - delta[:, own])).astype(BF16)
            sums[:, HEAD_DIM:] += matmul(soft.astype(BF16), grads[own, :])
            sums[:, :HEAD_DIM] += matmul(pulled, stacked[own, :])
            gathered[own, :] += transposed_times(pulled, key_ref[here, :])
            return carry

        lax.fori_loop(0, HEADS, head, 0)
        gkv_ref[here, HEAD_DIM:] = sums[:, HEAD_DIM:].astype(BF16)
        gkv_ref[here, :HEAD_DIM] = (sums[:, :HEAD_DIM] * scale).astype(BF16)

    plain = jnp.minimum(start, valid) // span
    last = jnp.minimum(start + tokens, valid)
    every = jnp.where(start < valid, (last + span - 1) // span, 0)
    plain = jnp.minimum(plain, every)

    def free(j, carry):
        block(j, False)
        return carry

    def edge(j, carry):
        block(j, True)
        return carry

    def empty(j, carry):
        at = pl.multiple_of(j * span, span)
        gkv_ref[pl.ds(at, span), :] = jnp.zeros((span, 2 * HEAD_DIM), BF16)
        return carry

    lax.fori_loop(0, plain, free, 0)
    lax.fori_loop(plain, every, edge, 0)
    lax.fori_loop(every, key_ref.shape[0] // span, empty, 0)
    for h in range(HEADS):
        at = slice(h * tokens, (h + 1) * tokens)
        first = gathered[at, :half] * scale
        second = gathered[at, half:] * scale
        lo = h * HEAD_DIM
        gq_ref[:, lo : lo + half] = (first * cosine[...] + second * sine[...]).astype(BF16)
        gq_ref[:, lo + half : lo + HEAD_DIM] = (second * cosine[...] - first * sine[...]).astype(BF16)


def attention_backward(bounds, stacked, grad, attended, cosine, sine, keys, values, norm, span):
    tokens = grad.shape[0]
    rows = tokens * HEADS
    return pl.pallas_call(
        partial(backward_kernel, span),
        out_shape=[
            jax.ShapeDtypeStruct((tokens, HEADS * HEAD_DIM), BF16),
            jax.ShapeDtypeStruct((keys.shape[0], 2 * HEAD_DIM), BF16),
        ],
        in_specs=[pl.BlockSpec(memory_space=pltpu.SMEM)]
        + [pl.BlockSpec(memory_space=pltpu.VMEM)] * 8,
        out_specs=[pl.BlockSpec(memory_space=pltpu.VMEM)] * 2,
        scratch_shapes=[
            pltpu.VMEM((rows, HEAD_DIM), BF16),
            pltpu.VMEM((rows, HEAD_DIM), F32),
            pltpu.VMEM((1, rows), F32),
            pltpu.VMEM((span, 2 * HEAD_DIM), F32),
        ],
        compiler_params=pltpu.CompilerParams(vmem_limit_bytes=VMEM_LIMIT),
        name="attention_backward",
    )(bounds, stacked, grad, attended, cosine, sine, keys, values, norm)


def pack_kernel(cuts, gains, count, *refs):
    ins, gain_refs = refs[:count], refs[count : count + len(gains)]
    outs = refs[count + len(gains) :]
    for out in outs:
        out[...] = jnp.zeros(out.shape, BF16)
    for source, (target, lo) in zip(ins, cuts):
        outs[target][0 : source.shape[0], lo : lo + source.shape[1]] = source[...]
    for gain, target in zip(gain_refs, gains):
        rows = gain.shape[1]
        outs[target][rows : rows + 1, 0:rows] = gain[...]


def pack(groups_of_weights, gains, gain_targets):
    weights, cuts, shapes = [], [], []
    for target, (wide, members) in enumerate(groups_of_weights):
        lo = 0
        for member in members:
            weights.append(member)
            cuts.append((target, lo))
            lo += member.shape[1]
        shapes.append((wide, lo))
    return pl.pallas_call(
        partial(pack_kernel, tuple(cuts), tuple(gain_targets), len(weights)),
        out_shape=[jax.ShapeDtypeStruct(shape, BF16) for shape in shapes],
        in_specs=[pl.BlockSpec(memory_space=pltpu.VMEM)] * (len(weights) + len(gains)),
        out_specs=[pl.BlockSpec(memory_space=pltpu.VMEM)] * len(shapes),
        compiler_params=pltpu.CompilerParams(vmem_limit_bytes=VMEM_LIMIT),
        name="pack",
    )(*weights, *[gain[None] for gain in gains])


def gain_whole(gathered, rows):
    wide = padded_model_rows(rows)
    return gathered.reshape(-1, wide, gathered.shape[1])[:, rows, :rows].reshape(-1).astype(F32)


def with_gain(partial_sums, gain_grad, rows):
    wide = padded_model_rows(rows)
    blocks = partial_sums.reshape(-1, wide, partial_sums.shape[1])
    return blocks.at[:, rows, :rows].set(gain_grad.reshape(-1, rows).astype(BF16)).reshape(partial_sums.shape)


def per_device(
    hidden_in,
    cotangent,
    dataset_ids,
    mixing,
    pad_lengths,
    attention_gain,
    merged_projection,
    merged_adapter_in,
    query_adapter_out,
    keyval_adapter_out,
    output_projection,
    output_adapter_in,
    output_adapter_out,
    feedforward_gain,
    gate_up_weight,
    gate_up_adapter_in,
    gate_up_adapter_out,
    down_weight,
    down_adapter_in,
    down_adapter_out,
):
    tokens, width = hidden_in.shape
    query_width = HEADS * HEAD_DIM
    merged_width = query_width + 2 * HEAD_DIM
    model_rows = merged_projection.shape[0]
    rank_rows = query_adapter_out.shape[0]
    pair_rows = keyval_adapter_out.shape[0]
    out_rows = output_projection.shape[0]
    ff_rows = down_weight.shape[0]
    model_wide, rank_wide = padded_model_rows(model_rows), padded_rows(rank_rows)
    pair_wide, ff_wide = padded_rows(pair_rows), padded_rows(ff_rows)

    packed = pack(
        [
            (model_wide, [merged_projection, merged_adapter_in]),
            (model_wide, [gate_up_weight, gate_up_adapter_in]),
            (rank_wide, [query_adapter_out]),
            (pair_wide, [keyval_adapter_out]),
            (padded_rows(out_rows), [output_projection, output_adapter_in]),
            (rank_wide, [output_adapter_out]),
            (pair_wide, [gate_up_adapter_out]),
            (ff_wide, [down_weight, down_adapter_in]),
            (rank_wide, [down_adapter_out]),
        ],
        [attention_gain, feedforward_gain],
        [0, 1],
    )
    merged, lift_query, lift_keyval = gather([], [packed[0], packed[2], packed[3]], 0)
    gain_one = gain_whole(merged, model_rows)

    hidden = hidden_in.astype(F32)
    normed_one, norm_one_back = jax.vjp(rms_scale, hidden, gain_one)
    first_in = spread(normed_one.astype(BF16), model_rows, model_wide)
    projected = matmul(first_in, merged)
    lifted = projected[:, merged_width:].astype(BF16)
    lifted_query = spread(lifted[:, :RANK], rank_rows, rank_wide)
    lifted_pair = spread(lifted[:, RANK:], pair_rows, pair_wide)
    half_pair = lifted_pair.shape[1] // 2
    query_rows = projected[:, :query_width] + matmul(lifted_query, lift_query)
    key_rows = projected[:, query_width : query_width + HEAD_DIM] + matmul(
        lifted_pair[:, :half_pair], lift_keyval[:half_pair]
    )
    value_rows = projected[:, query_width + HEAD_DIM : merged_width] + matmul(
        lifted_pair[:, half_pair:], lift_keyval[half_pair:]
    )
    start_pos = lax.axis_index("seq") * tokens
    positions = start_pos + jnp.arange(tokens, dtype=jnp.int32)
    cosine_table, sine_table = rotary_tables(positions)
    keys_rot = rotate(key_rows, cosine_table, sine_table).astype(BF16)
    length = lax.axis_size("seq") * tokens
    valid_count = length - pad_lengths[0]
    span = min(1024, length)
    bounds = jnp.stack([start_pos, valid_count])
    (
        keys_all,
        values_all,
        out_full,
        lift_out,
        gate_up,
        lift_gate_up,
        down,
        lift_down,
        attended,
        attended_low,
        log_norm,
        query_rot,
    ) = gather(
        [keys_rot, value_rows.astype(BF16)],
        [packed[4], packed[5], packed[1], packed[6], packed[7], packed[8]],
        1,
        (valid_count.reshape(1), query_rows, cosine_table, sine_table),
    )
    gain_two = gain_whole(gate_up, model_rows)
    out_both = matmul(attended_low, out_full)
    lifted_out = spread(out_both[:, width:].astype(BF16), rank_rows, rank_wide)
    middle = hidden + (out_both[:, :width] + matmul(lifted_out, lift_out))

    normed_two, norm_two_back = jax.vjp(rms_scale, middle, gain_two)
    second_in = spread(normed_two.astype(BF16), model_rows, model_wide)
    pre_gate = matmul(second_in, gate_up)
    lifted_gate_up = spread(pre_gate[:, 2 * FF :].astype(BF16), pair_rows, pair_wide)
    half_gate = lifted_gate_up.shape[1] // 2
    gate_part = pre_gate[:, :FF] + matmul(lifted_gate_up[:, :half_gate], lift_gate_up[:half_gate])
    upper_part = pre_gate[:, FF : 2 * FF] + matmul(
        lifted_gate_up[:, half_gate:], lift_gate_up[half_gate:]
    )
    activated, gelu_back = jax.vjp(partial(jax.nn.gelu, approximate=True), gate_part)
    inner = spread((activated * upper_part).astype(BF16), ff_rows, ff_wide)
    down_both = matmul(inner, down)
    lifted_down = spread(down_both[:, width:].astype(BF16), rank_rows, rank_wide)
    output = middle + (down_both[:, :width] + matmul(lifted_down, lift_down))

    matches = dataset_ids[:, None] == jnp.arange(DATASETS, dtype=jnp.int32)[None, :]
    picked = jnp.sum(jnp.where(matches, mixing[None, :], 0.0), axis=1)
    row_weight = jnp.where(positions < valid_count, picked, 0.0)
    scaled = cotangent.astype(F32) * row_weight[:, None]

    grad_branch = scaled.astype(BF16)
    grad_lifted_down = collect(times_transposed(grad_branch, lift_down), rank_rows, rank_wide)
    grad_down = jnp.concatenate([grad_branch, grad_lifted_down.astype(BF16)], axis=1)
    grad_inner = collect(times_transposed(grad_down, down), ff_rows, ff_wide)
    grad_gate = gelu_back(grad_inner * upper_part)[0].astype(BF16)
    grad_upper = (grad_inner * activated).astype(BF16)
    grad_gate_up = jnp.concatenate(
        [
            grad_gate,
            grad_upper,
            collect(
                times_transposed(grad_gate, lift_gate_up[:half_gate]), pair_rows, pair_wide
            ).astype(BF16),
            collect(
                times_transposed(grad_upper, lift_gate_up[half_gate:]), pair_rows, pair_wide
            ).astype(BF16),
        ],
        axis=1,
    )
    grad_normed_two = collect(times_transposed(grad_gate_up, gate_up), model_rows, model_wide)
    grad_middle_norm, gain_two_grad = norm_two_back(grad_normed_two)
    grad_middle = scaled + grad_middle_norm

    grad_attn = grad_middle.astype(BF16)
    grad_lifted_out = collect(times_transposed(grad_attn, lift_out), rank_rows, rank_wide)
    grad_out = jnp.concatenate([grad_attn, grad_lifted_out.astype(BF16)], axis=1)
    grad_attention = times_transposed(grad_out, out_full).astype(BF16)
    gate_up_out_term = jnp.concatenate(
        [
            transposed_times(lifted_gate_up[:, :half_gate], grad_gate, BF16),
            transposed_times(lifted_gate_up[:, half_gate:], grad_upper, BF16),
        ],
        axis=0,
    )
    partials = [
        with_gain(transposed_times(second_in, grad_gate_up, BF16), gain_two_grad, model_rows),
        transposed_times(inner, grad_down, BF16),
        transposed_times(attended_low, grad_out, BF16),
        gate_up_out_term,
        transposed_times(lifted_out, grad_attn, BF16),
        transposed_times(lifted_down, grad_branch, BF16),
    ]
    if length * 2 * HEAD_DIM * 7 <= FUSED_BYTES:
        *sums, grad_query_low = scatter(
            [],
            partials,
            2,
            (
                valid_count.reshape(1),
                query_rot,
                grad_attention,
                attended,
                cosine_table,
                sine_table,
                keys_all.reshape(-1, 4 * tokens, HEAD_DIM),
                values_all.reshape(-1, 4 * tokens, HEAD_DIM),
                log_norm,
            ),
        )
    else:
        grad_query_low, kv_terms = attention_backward(
            bounds,
            query_rot,
            grad_attention,
            attended,
            cosine_table,
            sine_table,
            keys_all,
            values_all,
            log_norm,
            span,
        )
        sums = scatter([kv_terms], partials, 2)
    kv_summed, gate_up_sum, down_sum, out_sum, gate_up_out_sum, out_out_sum, down_out_sum = sums
    grad_keys = rotate(kv_summed[:, :HEAD_DIM], cosine_table, -sine_table)
    grad_keys_low = grad_keys.astype(BF16)
    grad_values_low = kv_summed[:, HEAD_DIM:].astype(BF16)
    grad_merged = jnp.concatenate(
        [
            grad_query_low,
            grad_keys_low,
            grad_values_low,
            collect(times_transposed(grad_query_low, lift_query), rank_rows, rank_wide).astype(BF16),
            collect(
                times_transposed(grad_keys_low, lift_keyval[:half_pair]), pair_rows, pair_wide
            ).astype(BF16),
            collect(
                times_transposed(grad_values_low, lift_keyval[half_pair:]), pair_rows, pair_wide
            ).astype(BF16),
        ],
        axis=1,
    )
    grad_normed_one = collect(times_transposed(grad_merged, merged), model_rows, model_wide)
    grad_hidden_norm, gain_one_grad = norm_one_back(grad_normed_one)
    hidden_grad = grad_middle + grad_hidden_norm

    keyval_term = jnp.concatenate(
        [
            transposed_times(lifted_pair[:, :half_pair], grad_keys_low, BF16),
            transposed_times(lifted_pair[:, half_pair:], grad_values_low, BF16),
        ],
        axis=0,
    )
    merged_sum, query_out_sum, keyval_sum = scatter(
        [],
        [
            with_gain(transposed_times(first_in, grad_merged, BF16), gain_one_grad, model_rows),
            transposed_times(lifted_query, grad_query_low, BF16),
            keyval_term,
        ],
        3,
    )
    grads = finish(
        [
            merged_sum,
            query_out_sum,
            keyval_sum,
            out_sum,
            out_out_sum,
            gate_up_sum,
            gate_up_out_sum,
            down_sum,
            down_out_sum,
        ],
        [
            (0, model_rows, 0, merged_width),
            (0, model_rows, merged_width, 3 * RANK),
            (1, rank_rows, 0, query_width),
            (2, pair_rows, 0, HEAD_DIM),
            (3, out_rows, 0, width),
            (3, out_rows, width, RANK),
            (4, rank_rows, 0, width),
            (5, model_rows, 0, 2 * FF),
            (5, model_rows, 2 * FF, 2 * RANK),
            (6, pair_rows, 0, FF),
            (7, ff_rows, 0, width),
            (7, ff_rows, width, RANK),
            (8, rank_rows, 0, width),
        ],
    )
    return (
        output.astype(BF16),
        hidden_grad.astype(BF16),
        merged_sum[model_rows, :model_rows],
        *grads[:7],
        gate_up_sum[model_rows, :model_rows],
        *grads[7:],
    )


def solution(mesh):
    rows, vector = P(AXES, None), P(AXES)
    return jax.shard_map(
        per_device,
        mesh=mesh,
        in_specs=(rows, rows, vector, P(), P("fsdp"), vector)
        + (rows,) * 7
        + (vector,)
        + (rows,) * 6,
        out_specs=(rows, rows, vector) + (rows,) * 7 + (vector,) + (rows,) * 6,
        check_vma=False,
    )
```
